32 devices in a mesh: dp: 2 (over y), seq: 16 (over z, x, core).
Axes of the slice: x: 2, y: 2, z: 4, core: 2. Of those that a mesh axis runs over, the one named last changes fastest.
Arguments:
- tokens: int32 [2, 2, 2, 1024], P(None, 'dp', None, 'seq'), may hold values from 0 to 50303
- targets: int32 [2, 2, 1024], P(None, 'dp', 'seq'), may hold values from 0 to 50303
- counted: int32 [2, 2, 1024], P(None, 'dp', 'seq'), may hold values from 0 to 1, as said below
- cont_label: int32 [2, 2, 2], replicated, may hold values from 0 to 1, each once within a row
- pair_map: int32 [2, 2, 2], replicated, may hold values from 0 to 1, each once within a row
- ref_logp: float32 [2, 2, 2], replicated, may hold values from -128 to 128
- vocab_slot: int32 [50304], replicated, may hold values from 0 to 50303, each once
- embed_table: float32 [50304, 1088], P(('dp', 'seq')), may hold values from -0.375 to 0.375
- embed_first: float32 [50304, 1088], P(('dp', 'seq')), may hold values from -7.6293945e-05 to 7.6293945e-05
- embed_second: float32 [50304, 1088], P(('dp', 'seq')), may hold values from 1.4e-11 to 5.8e-11
- layer_weights: float32 [1088, 13056], P(None, ('dp', 'seq'))
- layer_first: float32 [1088, 13056], P(None, ('dp', 'seq')), may hold values from -7.6293945e-05 to 7.6293945e-05
- layer_second: float32 [1088, 13056], P(None, ('dp', 'seq')), may hold values from 1.4e-11 to 5.8e-11
- norm_params: float32 [6528], P(('dp', 'seq')), may hold values from -0.3 to 1.4, as said below
- norm_first: float32 [6528], P(('dp', 'seq')), may hold values from -0.0004272461 to 0.0004272461
- norm_second: float32 [6528], P(('dp', 'seq')), may hold values from 3.6e-10 to 1.4e-09
Outputs:
- embed_new: float32 [50304, 1088], P(('dp', 'seq'))
- embed_first_new: float32 [50304, 1088], P(('dp', 'seq'))
- embed_second_new: float32 [50304, 1088], P(('dp', 'seq'))
- embed_low: bfloat16 [50304, 1088], P(('dp', 'seq'))
- layer_new: float32 [1088, 13056], P(None, ('dp', 'seq'))
- layer_first_new: float32 [1088, 13056], P(None, ('dp', 'seq'))
- layer_second_new: float32 [1088, 13056], P(None, ('dp', 'seq'))
- layer_low: bfloat16 [1088, 13056], P(None, ('dp', 'seq'))
- norm_new: float32 [6528], P(('dp', 'seq'))
- norm_first_new: float32 [6528], P(('dp', 'seq'))
- norm_second_new: float32 [6528], P(('dp', 'seq'))
- norm_low: bfloat16 [6528], P(('dp', 'seq'))
- grad_norm: float32 [], replicated
- loss: float32 [], replicated
The draws below stay inside these ranges and needn't reach their ends.
Inputs may be any that keep to these rules, and one draw needn't show every extreme that they name: `counted`: in each aligned block of 64 entries along the last dimension (the continuation rows of one device) exactly 32 entries are 1 and the others 0. `norm_params`: the first 3264 entries lie in 0.6 to 1.4.
All inputs are finite; a program needn't handle non-finite values.
Results may differ from the reference program's by a relative error of at most 0.02.
The reference program's roundings to bfloat16 on the way count: a program that leaves them out, or rounds other values in their place, can miss the bound.
Values may be sent and summed in bfloat16 or wider, within the bound.
A program may use at most 448 MiB of HBM per device.

```python
import math
import jax
import jax.numpy as jnp
import numpy as np
from jax import lax

D = 1088
HEADS = 17
HD = 64
FF = 4352
V = 50304
CDEV = 64
PICK = 32
CLEN = 512
MB = 2
STEP = 10
HALF = 1024
NCONT = 2
GROUPS = 2
N_SEQ = 16


def draw_counted(key, part):
    blocks = MB * GROUPS * HALF // CDEV
    subkeys = jax.random.split(key, blocks)
    orders = jax.vmap(lambda subkey: jax.random.permutation(subkey, CDEV))(subkeys)
    return (orders < PICK).astype(jnp.int32).reshape(MB, GROUPS, HALF)


def draw_layer_weights(key, part):
    columns = 4 * D + 2 * FF
    column = jnp.arange(columns)
    scales = jnp.where(column < 3 * D, D ** (-0.5), jnp.where(column < 4 * D, 2.0 * D ** (-0.5), jnp.where(column < 4 * D + FF, D ** (-0.5), 0.1 * FF ** (-0.5))))
    base = jnp.clip(jax.random.normal(key, (D, columns), jnp.float32), -6.0, 6.0)
    return (base * scales[None, :]).astype(jnp.float32)


def draw_norm_params(key, part):
    entries = 6 * D
    first_key = jax.random.fold_in(key, 11)
    second_key = jax.random.fold_in(key, 12)
    gains = 1.0 + 0.1 * jnp.clip(jax.random.normal(first_key, (entries,), jnp.float32), -3.0, 3.0)
    biases = 0.1 * jnp.clip(jax.random.normal(second_key, (entries,), jnp.float32), -3.0, 3.0)
    return jnp.where(jnp.arange(entries) < 3 * D, gains, biases).astype(jnp.float32)


def place_ends(array, key, least, high):
    extent = array.shape
    place = [jax.random.randint(jax.random.fold_in(key, axis), (), 0, extent[axis]) for axis in range(len(extent))]
    array = array.at[tuple(place)].set(least)
    longest = extent.index(max(extent))
    place[longest] = (place[longest] + 1) % extent[longest]
    return array.at[tuple(place)].set(high)


def block_scale(key, shape, pieces, low, largest):
    level = 1.0
    for axis_at, parts in pieces:
        heights = jax.random.uniform(jax.random.fold_in(jax.random.fold_in(key, 6), axis_at), (parts,), jnp.float32, low / len(pieces), largest / len(pieces))
        level = level * jnp.repeat(jnp.exp(heights), shape[axis_at] // parts).reshape((-1,) + (1,) * (len(shape) - 1 - axis_at))
    return level


def rank_bounds(count, skew):
    loads = [(1 << 20) // math.isqrt(rank ** skew) + 1 for rank in range(1, count + 1)]
    scale = 1 + sum(loads) // (1 << 30)
    return np.cumsum(np.array([max(1, weight // scale) for weight in loads]))


def ranked(stream_key, dims, count, skew):
    grid = rank_bounds(count, skew)
    lot = jax.random.randint(jax.random.fold_in(stream_key, 1), dims, 0, int(grid[count - 1]))
    rank = jnp.searchsorted(jnp.asarray(grid, jnp.int32), lot, side="right")
    return jax.random.permutation(jax.random.fold_in(stream_key, 2), count)[rank].astype(jnp.int32)


def bell_draw(stream_key, shape, spread, reach, cuts=(), kind=jnp.bfloat16):
    array = spread * jax.random.normal(stream_key, shape, jnp.float32)
    if cuts:
        array = array * block_scale(stream_key, shape, cuts, -0.22, 0.18)
    return jnp.clip(array, -reach, reach).astype(kind)


def setup_inputs(seed: int = 0) -> dict:
    arg_keys = jax.random.split(jax.random.key(seed), 17)
    return {
        "tokens": place_ends(ranked(arg_keys[0], (MB, GROUPS, 2, HALF), V, 2), jax.random.fold_in(arg_keys[0], 3), 0, V - 1).astype(jnp.int32),
        "targets": place_ends(ranked(arg_keys[1], (MB, GROUPS, HALF), V, 2), jax.random.fold_in(arg_keys[1], 3), 0, V - 1).astype(jnp.int32),
        "counted": draw_counted(jax.random.fold_in(arg_keys[16], 71), 0),
        "cont_label": jax.vmap(lambda own: jax.random.permutation(own, NCONT))(jax.random.split(arg_keys[3], MB * GROUPS)).reshape((MB, GROUPS, NCONT)).astype(jnp.int32),
        "pair_map": jax.vmap(lambda own: jax.random.permutation(own, NCONT))(jax.random.split(arg_keys[4], MB * GROUPS)).reshape((MB, GROUPS, NCONT)).astype(jnp.int32),
        "ref_logp": bell_draw(arg_keys[5], (MB, GROUPS, NCONT), 20.0, 128.0, (), jnp.float32),
        "vocab_slot": jax.random.permutation(arg_keys[6], V).astype(jnp.int32),
        "embed_table": bell_draw(arg_keys[7], (V, D), 0.06, 0.375, ((0, 32),), jnp.float32),
        "embed_first": bell_draw(arg_keys[8], (V, D), (1.3e-5), 7.62939453125e-05, ((0, 32),), jnp.float32),
        "embed_second": jnp.clip(jnp.exp(math.log(5.8000000635605176e-11) - 1.4213857 * jax.random.uniform(arg_keys[9], (V, D), jnp.float32) ** block_scale(arg_keys[9], (V, D), ((0, 32),), -0.2, 0.2)), 1.399999994405876e-11, 5.8000000635605176e-11),
        "layer_weights": draw_layer_weights(jax.random.fold_in(arg_keys[16], 71), 0),
        "layer_first": bell_draw(arg_keys[11], (D, 4 * D + 2 * FF), (1.3e-5), 7.62939453125e-05, ((1, 32),), jnp.float32),
        "layer_second": jnp.clip(jnp.exp(math.log(5.8000000635605176e-11) - 1.4213857 * jax.random.uniform(arg_keys[12], (D, 4 * D + 2 * FF), jnp.float32) ** block_scale(arg_keys[12], (D, 4 * D + 2 * FF), ((1, 32),), -0.2, 0.2)), 1.399999994405876e-11, 5.8000000635605176e-11),
        "norm_params": draw_norm_params(jax.random.fold_in(arg_keys[16], 71), 0),
        "norm_first": bell_draw(arg_keys[14], (6 * D,), (7e-5), 0.0004272461, ((0, 32),), jnp.float32),
        "norm_second": jnp.clip(jnp.exp(math.log(1.400000004814217e-09) - 1.3581235 * jax.random.uniform(arg_keys[15], (6 * D,), jnp.float32) ** block_scale(arg_keys[15], (6 * D,), ((0, 32),), -0.2, 0.2)), 3.6000000203095794e-10, 1.400000004814217e-09),
    }


EPS_NORM = 1e-05
DPO_BETA = 0.05
CLIP_NORM = 1.0
LEARN_RATE = 0.03
NORM_RATE = 0.4
WEIGHT_DECAY = 0.1
MOMENT_ONE = 0.9
MOMENT_TWO = 0.999
EPS_ADAM = 1e-08
HIGHEST = lax.Precision.HIGHEST

@jax.custom_vjp
def low(v):
    return lax.optimization_barrier(v.astype(jnp.bfloat16)).astype(jnp.float32)

@jax.custom_vjp
def low_back(v):
    return v

def low_keep(v):
    return (low(v), None)

def low_pass(kept, grad):
    return (grad,)

def back_keep(v):
    return (v, None)

def back_low(kept, grad):
    return (low(grad),)
low.defvjp(low_keep, low_pass)
low_back.defvjp(back_keep, back_low)

def matmul(left, right):
    return jnp.dot(left, right, precision=HIGHEST)

def layer_norm(values, gain, bias):
    centred = values - lax.optimization_barrier(jnp.mean(values, axis=-1, keepdims=True))
    return centred * lax.rsqrt(lax.optimization_barrier(jnp.mean(centred * centred, axis=-1, keepdims=True)) + EPS_NORM) * gain + bias

def attention(queries, keys, values):
    length = queries.shape[0]
    rows_block = min(512, length)
    scale = HD ** (-0.5)
    key_pos = jnp.arange(length).astype(jnp.int32)

    def one_block(inputs):
        query_part, query_pos = inputs
        scores = low_back(jnp.einsum('qhe,khe->hqk', query_part, keys, precision=HIGHEST) * scale)
        visible = (key_pos[None, :] <= query_pos[:, None]) & ((key_pos[None, :] < HALF) | (key_pos[None, :] // CLEN == query_pos[:, None] // CLEN))
        probs = jax.nn.softmax(jnp.where(visible[None], scores, -1e+30), axis=-1)
        return jnp.einsum('hqk,khe->qhe', low(probs), values, precision=HIGHEST)
    blocks = length // rows_block
    output = lax.map(jax.checkpoint(one_block), (queries.reshape(blocks, rows_block, HEADS, HD), key_pos.reshape(blocks, rows_block)))
    return output.reshape(length, HEADS * HD)

def head_logp(rows, table, target_slots):
    blocks = 8
    block_rows = table.shape[0] // blocks

    def one_block(inputs):
        table_part, start = inputs
        logits = low_back(matmul(rows, table_part.T))
        highest = lax.optimization_barrier(jnp.max(logits, axis=1))
        summed = lax.optimization_barrier(jnp.sum(jnp.exp(logits - highest[:, None]), axis=1))
        target_hit = target_slots[:, None] - start == jnp.arange(block_rows).astype(jnp.int32)[None, :]
        return (highest, summed, lax.optimization_barrier(jnp.sum(jnp.where(target_hit, logits, 0.0), axis=1)))
    starts = (jnp.arange(blocks) * block_rows).astype(jnp.int32)
    highs, sums, hits = lax.map(jax.checkpoint(one_block), (table.reshape(blocks, block_rows, table.shape[1]), starts))
    overall = lax.optimization_barrier(jnp.max(highs, axis=0))
    return lax.optimization_barrier(jnp.sum(hits, axis=0)) - overall - jnp.log(lax.optimization_barrier(jnp.sum(sums * jnp.exp(highs - overall[None, :]), axis=0)))

def group_loss(table, weights, norms, slots, target_slots, marks, labels, pairing, reference_lp):
    width = HEADS * HD
    gains = norms.reshape(6, width)
    stream = table[slots]
    hidden_one = low(layer_norm(stream, gains[0], gains[3]))
    qkv = low_back(low(matmul(hidden_one, weights[:, :3 * width])))
    split = qkv.reshape(-1, 3, HEADS, HD)
    attended = low_back(low(attention(split[:, 0], split[:, 1], split[:, 2])))
    stream_one = stream + low_back(matmul(attended, weights[:, 3 * width:4 * width].T))
    hidden_two = low(layer_norm(stream_one, gains[1], gains[4]))
    up_proj = low_back(matmul(hidden_two, weights[:, 4 * width:4 * width + FF]))
    activated = low(jax.nn.gelu(up_proj, approximate=False))
    stream_two = stream_one + low_back(matmul(activated, weights[:, 4 * width + FF:].T))
    final = low(layer_norm(stream_two, gains[2], gains[5]))
    picked = jnp.nonzero(marks, size=N_SEQ * PICK)[0].astype(jnp.int32)
    token_lp = head_logp(final[HALF + picked], table, target_slots[picked])
    run_of_row = picked // CLEN
    run_ids = jnp.arange(NCONT).astype(jnp.int32)
    run_lp = lax.optimization_barrier(jnp.sum(jnp.where(run_of_row[None, :] == run_ids[:, None], token_lp[None, :], 0.0), axis=1))
    label_lp = lax.optimization_barrier(jnp.sum(jnp.where(labels[:, None] == run_ids[None, :], run_lp[:, None], 0.0), axis=0))
    margin = label_lp - reference_lp
    delta = margin[pairing[0::2]] - margin[pairing[1::2]]
    return jnp.sum(jax.nn.softplus(-DPO_BETA * delta))

def adamw(weight, moment_a, moment_b, gradient, rate, decay):
    moment_a = MOMENT_ONE * moment_a + (1.0 - MOMENT_ONE) * gradient
    moment_b = MOMENT_TWO * moment_b + (1.0 - MOMENT_TWO) * gradient * gradient
    update = moment_a / (1.0 - MOMENT_ONE ** STEP) / (jnp.sqrt(moment_b / (1.0 - MOMENT_TWO ** STEP)) + EPS_ADAM)
    weight = weight - rate * (update + decay * weight)
    return (weight, moment_a, moment_b, weight.astype(jnp.bfloat16))

def reference(tokens, targets, counted, cont_label, pair_map, ref_logp, vocab_slot, embed_table, embed_first, embed_second, layer_weights, layer_first, layer_second, norm_params, norm_first, norm_second):
    groups_all = MB * GROUPS
    inputs = (vocab_slot[tokens].reshape(groups_all, 2 * HALF), vocab_slot[targets].reshape(groups_all, HALF), counted.reshape(groups_all, HALF), cont_label.reshape(groups_all, NCONT), pair_map.reshape(groups_all, NCONT), ref_logp.reshape(groups_all, NCONT))

    def full_loss(table, weights, norms):
        table_low, weights_low, norms_low = (low(table), low(weights), low(norms))

        def advance(total, item):
            return (total + group_loss(table_low, weights_low, norms_low, item[0], item[1], item[2], item[3], item[4], item[5]), None)
        total, _ = lax.scan(advance, jnp.zeros((), jnp.float32), inputs)
        return total
    loss, pull = jax.vjp(full_loss, embed_table, layer_weights, norm_params)
    table_grad, weight_grad, norm_grad = pull(jnp.ones((), jnp.float32))
    grad_norm = jnp.sqrt(jnp.sum(table_grad * table_grad) + jnp.sum(weight_grad * weight_grad) + jnp.sum(norm_grad * norm_grad))
    factor = jnp.minimum(1.0, CLIP_NORM / grad_norm)
    embed_out = adamw(embed_table, embed_first, embed_second, table_grad * factor, LEARN_RATE, WEIGHT_DECAY)
    layer_out = adamw(layer_weights, layer_first, layer_second, weight_grad * factor, LEARN_RATE, WEIGHT_DECAY)
    norm_out = adamw(norm_params, norm_first, norm_second, norm_grad * factor, NORM_RATE, 0.0)
    return (embed_out[0], embed_out[1], embed_out[2], embed_out[3], layer_out[0], layer_out[1], layer_out[2], layer_out[3], norm_out[0], norm_out[1], norm_out[2], norm_out[3], grad_norm, loss)
```

```python
import jax
import jax.numpy as jnp
from jax import lax
from jax.sharding import PartitionSpec as P

HEADS = 17
HD = 64
FF = 4352
PICK = 32
CLEN = 512
MB = 2
STEP = 10


EPS_NORM = 1e-05
DPO_BETA = 0.05
CLIP_NORM = 1.0
LEARN_RATE = 0.03
NORM_RATE = 0.4
WEIGHT_DECAY = 0.1
MOMENT_ONE = 0.9
MOMENT_TWO = 0.999
EPS_ADAM = 1e-08
MASKED = -1e30
BF = jnp.bfloat16
F32 = jnp.float32


def contract(left, right, left_dim, right_dim):
    return lax.dot_general(
        left, right, (((left_dim,), (right_dim,)), ((), ())), preferred_element_type=F32
    )


def norm_forward(values, gain, bias):
    centred = values - jnp.mean(values, axis=-1, keepdims=True)
    inverse = lax.rsqrt(jnp.mean(centred * centred, axis=-1, keepdims=True) + EPS_NORM)
    unit = centred * inverse
    return (unit * gain + bias, unit, inverse)


def norm_backward(upstream, unit, inverse, gain):
    scaled = upstream * gain
    inner = (
        scaled
        - jnp.mean(scaled, axis=-1, keepdims=True)
        - unit * jnp.mean(scaled * unit, axis=-1, keepdims=True)
    )
    return (inverse * inner, jnp.sum(upstream * unit, axis=0), jnp.sum(upstream, axis=0))


def probabilities(queries, keys, visible):
    scores = jnp.einsum("mqhe,mkhe->mhqk", queries, keys, preferred_element_type=F32) * HD ** (-0.5)
    scores = jnp.where(visible[None, None], scores, MASKED)
    shifted = jnp.exp(scores - jnp.max(scores, axis=-1, keepdims=True))
    return shifted / jnp.sum(shifted, axis=-1, keepdims=True)


def attend_forward(queries, keys, values, visible):
    probs = probabilities(queries, keys, visible)
    return jnp.einsum("mhqk,mkhe->mqhe", probs.astype(BF), values, preferred_element_type=F32)


def attend_backward(queries, keys, values, visible, grad_out):
    probs = probabilities(queries, keys, visible)
    grad_probs = jnp.einsum("mqhe,mkhe->mhqk", grad_out, values, preferred_element_type=F32)
    grad_scores = (
        probs * (grad_probs - jnp.sum(probs * grad_probs, axis=-1, keepdims=True))
    ).astype(BF)
    scale = HD ** (-0.5)
    grad_query = (
        jnp.einsum("mhqk,mkhe->mqhe", grad_scores, keys, preferred_element_type=F32) * scale
    )
    grad_keys = (
        jnp.einsum("mhqk,mqhe->mkhe", grad_scores, queries, preferred_element_type=F32) * scale
    )
    grad_values = jnp.einsum(
        "mhqk,mqhe->mkhe", probs.astype(BF), grad_out, preferred_element_type=F32
    )
    return (grad_query, grad_keys, grad_values)


def adamw(weight, moment_a, moment_b, gradient, rate, decay):
    moment_a = MOMENT_ONE * moment_a + (1.0 - MOMENT_ONE) * gradient
    moment_b = MOMENT_TWO * moment_b + (1.0 - MOMENT_TWO) * gradient * gradient
    update = (
        moment_a
        / (1.0 - MOMENT_ONE**STEP)
        / (jnp.sqrt(moment_b / (1.0 - MOMENT_TWO**STEP)) + EPS_ADAM)
    )
    weight = weight - rate * (update + decay * weight)
    return (weight, moment_a, moment_b, weight.astype(BF))


def on_device(
    tokens,
    targets,
    counted,
    cont_label,
    pair_map,
    ref_logp,
    vocab_slot,
    embed_table,
    embed_first,
    embed_second,
    layer_weights,
    layer_first,
    layer_second,
    norm_params,
    norm_first,
    norm_second,
):
    seq_count = lax.axis_size("seq")
    group_count = lax.axis_size("dp")
    all_count = seq_count * group_count
    seq_rank = lax.axis_index("seq")
    group_rank = lax.axis_index("dp")
    device_rank = group_rank * seq_count + seq_rank
    rows_dev = tokens.shape[3]
    half = rows_dev * seq_count
    vocab_dev, width = embed_table.shape
    run_count = half // CLEN
    run_devs = CLEN // rows_dev
    own_rows = MB * 2 * rows_dev
    norm_dev = norm_params.shape[0]

    table_t = embed_table.T
    slab_t = lax.all_gather(table_t.astype(BF)[None], "dp", axis=0, tiled=True)
    weights = lax.all_gather(
        layer_weights.T.astype(BF)[None], ("dp", "seq"), axis=0, tiled=True
    ).reshape(-1, width)
    w_q, w_k, w_v, w_o = (weights[i * width : (i + 1) * width] for i in range(4))
    w_qkv = weights[: 3 * width]
    w_kv = weights[width : 3 * width]
    w_up = weights[4 * width : 4 * width + FF]
    w_dn = weights[4 * width + FF :]

    marks = counted[:, 0]
    spots = jnp.arange(rows_dev, dtype=jnp.int32)
    ranks = (
        jnp.sum(jnp.where(spots[None, :, None] <= spots[None, None, :], marks[:, :, None], 0), axis=1)
        - 1
    )
    pick_ids = jnp.arange(PICK, dtype=jnp.int32)
    pick_hit = (ranks[:, None, :] == pick_ids[None, :, None]) & (marks[:, None, :] == 1)
    pick_targets = jnp.sum(jnp.where(pick_hit, targets[:, 0][:, None, :], 0), axis=2)
    pick_low = pick_hit.astype(BF)
    slots = vocab_slot[jnp.concatenate([tokens[:, 0].reshape(-1), pick_targets.reshape(-1)])]
    small = jnp.concatenate([slots.astype(F32), norm_params])
    small = jnp.pad(small, (0, -small.shape[0] % 128)).reshape(1, -1, 128)
    small_all = lax.all_gather(small, ("dp", "seq"), axis=0, tiled=True).reshape(all_count, -1)
    slots_all = lax.dynamic_slice_in_dim(small_all, group_rank * seq_count, seq_count, 0)[
        :, : own_rows + MB * PICK
    ].astype(jnp.int32)
    gains = small_all[:, own_rows + MB * PICK :][:, :norm_dev].astype(BF).astype(F32).reshape(6, width)
    row_slots = slots_all[:, :own_rows].reshape(-1)
    target_slots = slots_all[:, own_rows:].reshape(-1)
    vocab_ids = jnp.arange(vocab_dev, dtype=jnp.int32)

    def hits(slot_ids, part):
        first = (part * seq_count + seq_rank) * vocab_dev
        return (slot_ids - first)[:, None] == vocab_ids[None, :]

    partial = jnp.zeros((row_slots.shape[0], width), F32)
    for part in range(group_count):
        partial = partial + contract(hits(row_slots, part).astype(BF), slab_t[part], 1, 1)
    stream = lax.psum_scatter(
        partial.astype(BF).reshape(seq_count, own_rows, width), "seq", scatter_dimension=0, tiled=True
    )[0].astype(F32)

    normed, unit_one, inverse_one = norm_forward(stream, gains[0], gains[3])
    hidden_one = normed.astype(BF)
    hidden_all = lax.all_gather(
        hidden_one.reshape(1, MB, 2, rows_dev, width), "seq", axis=0, tiled=True
    )
    run_dev = seq_rank // run_devs * run_devs
    prompt_hidden = hidden_all[:, :, 0].transpose(1, 0, 2, 3).reshape(MB, half, width)
    run_hidden = (
        lax.dynamic_slice_in_dim(hidden_all[:, :, 1], run_dev, run_devs, 0)
        .transpose(1, 0, 2, 3)
        .reshape(MB, CLEN, width)
    )
    key_rows = half + CLEN
    hidden_sel = jnp.concatenate([prompt_hidden, run_hidden], axis=1).reshape(MB * key_rows, width)
    keys = contract(hidden_sel, w_k, 1, 1).astype(BF).reshape(MB, key_rows, HEADS, HD)
    values = contract(hidden_sel, w_v, 1, 1).astype(BF).reshape(MB, key_rows, HEADS, HD)
    queries = contract(hidden_one, w_q, 1, 1).astype(BF).reshape(MB, 2 * rows_dev, HEADS, HD)
    start = seq_rank * rows_dev
    query_pos = jnp.concatenate([start + spots, half + (start - run_dev * rows_dev) + spots])
    key_pos = jnp.arange(key_rows, dtype=jnp.int32)
    visible = key_pos[None, :] <= query_pos[:, None]
    attended = attend_forward(queries, keys, values, visible).reshape(own_rows, width).astype(BF)
    stream_one = stream + contract(attended, w_o, 1, 0)
    normed, unit_two, inverse_two = norm_forward(stream_one, gains[1], gains[4])
    hidden_two = normed.astype(BF)
    up_proj = contract(hidden_two, w_up, 1, 1)
    activated = jax.nn.gelu(up_proj, approximate=False).astype(BF)
    stream_two = stream_one + contract(activated, w_dn, 1, 0)
    normed, unit_final, inverse_final = norm_forward(stream_two, gains[2], gains[5])
    final = normed.astype(BF).reshape(MB, 2, rows_dev, width)[:, 1]
    picked = jnp.einsum("mpr,mrd->mpd", pick_low, final, preferred_element_type=F32).astype(BF)

    head_rows = lax.all_gather(
        picked.reshape(1, MB * PICK, width), "seq", axis=0, tiled=True
    ).reshape(seq_count * MB * PICK, width)
    logits = [contract(head_rows, slab_t[part], 1, 0) for part in range(group_count)]
    target_hits = [hits(target_slots, part) for part in range(group_count)]
    highest = jnp.max(logits[0], axis=1)
    for part in range(1, group_count):
        highest = jnp.maximum(highest, jnp.max(logits[part], axis=1))
    summed = jnp.zeros_like(highest)
    target_logit = jnp.zeros_like(highest)
    for part in range(group_count):
        summed = summed + jnp.sum(jnp.exp(logits[part] - highest[:, None]), axis=1)
        target_logit = target_logit + jnp.sum(jnp.where(target_hits[part], logits[part], 0.0), axis=1)
    stats = lax.all_gather(jnp.stack([highest, summed, target_logit])[None], "seq", axis=0, tiled=True)
    overall = jnp.max(stats[:, 0], axis=0)
    total = jnp.sum(stats[:, 1] * jnp.exp(stats[:, 0] - overall[None]), axis=0)
    log_total = overall + jnp.log(total)
    token_lp = jnp.sum(stats[:, 2], axis=0) - log_total

    run_ids = jnp.arange(run_count, dtype=jnp.int32)
    run_of_dev = jnp.arange(seq_count, dtype=jnp.int32) * rows_dev // CLEN
    run_match = run_of_dev[:, None] == run_ids[None, :]
    dev_lp = jnp.sum(token_lp.reshape(seq_count, MB, PICK), axis=2)
    run_lp = jnp.sum(jnp.where(run_match[:, None, :], dev_lp[:, :, None], 0.0), axis=0)
    labels = lax.dynamic_index_in_dim(cont_label, group_rank, 1, keepdims=False)
    pairing = lax.dynamic_index_in_dim(pair_map, group_rank, 1, keepdims=False)
    reference_lp = lax.dynamic_index_in_dim(ref_logp, group_rank, 1, keepdims=False)
    label_match = labels[:, :, None] == run_ids[None, None, :]
    label_lp = jnp.sum(jnp.where(label_match, run_lp[:, :, None], 0.0), axis=1)
    margin = label_lp - reference_lp
    chosen = pairing[:, 0::2, None] == run_ids[None, None, :]
    rejected = pairing[:, 1::2, None] == run_ids[None, None, :]
    delta = jnp.sum(jnp.where(chosen, margin[:, None, :], 0.0), axis=2) - jnp.sum(
        jnp.where(rejected, margin[:, None, :], 0.0), axis=2
    )
    loss = jnp.sum(jax.nn.softplus(-DPO_BETA * delta))
    pair_grad = -DPO_BETA * jax.nn.sigmoid(-DPO_BETA * delta)
    label_grad = jnp.sum(
        jnp.where(chosen, pair_grad[:, :, None], 0.0)
        - jnp.where(rejected, pair_grad[:, :, None], 0.0),
        axis=1,
    )
    run_grad = jnp.sum(jnp.where(label_match, label_grad[:, None, :], 0.0), axis=2)
    dev_grad = jnp.sum(jnp.where(run_match[:, None, :], run_grad[None], 0.0), axis=2)
    row_grad = jnp.broadcast_to(dev_grad[:, :, None], (seq_count, MB, PICK)).reshape(-1)

    head_back = jnp.zeros((head_rows.shape[0], width), F32)
    logit_grads = []
    for part in range(group_count):
        logit_grad = (
            row_grad[:, None]
            * (target_hits[part].astype(F32) - jnp.exp(logits[part] - log_total[:, None]))
        ).astype(BF)
        logit_grads.append(logit_grad)
        head_back = head_back + contract(logit_grad, slab_t[part], 1, 1)
    row_back = lax.psum_scatter(
        head_back.astype(BF).reshape(seq_count, MB * PICK, width),
        "seq",
        scatter_dimension=0,
        tiled=True,
    )[0].reshape(MB, PICK, width)
    cont_back = jnp.einsum("mpr,mpd->mrd", pick_low, row_back, preferred_element_type=F32)
    upstream = jnp.concatenate(
        [jnp.zeros((MB, 1, rows_dev, width), F32), cont_back[:, None]], axis=1
    ).reshape(own_rows, width)

    grad_two, gain_final, bias_final = norm_backward(upstream, unit_final, inverse_final, gains[2])
    grad_ffn = grad_two.astype(BF)
    down_grad = contract(activated, grad_ffn, 0, 0).astype(BF)
    grad_act = contract(grad_ffn, w_dn, 1, 1)
    _, gelu_pull = jax.vjp(lambda pre_act: jax.nn.gelu(pre_act, approximate=False), up_proj)
    grad_up = gelu_pull(grad_act)[0].astype(BF)
    up_grad = contract(grad_up, hidden_two, 0, 0).astype(BF)
    grad_hidden = contract(grad_up, w_up, 1, 0)
    grad_mid, gain_two, bias_two = norm_backward(grad_hidden, unit_two, inverse_two, gains[1])
    grad_one = grad_two + grad_mid
    grad_branch = grad_one.astype(BF)
    out_grad = contract(attended, grad_branch, 0, 0).astype(BF)
    grad_attended = (
        contract(grad_branch, w_o, 1, 1).astype(BF).reshape(MB, 2 * rows_dev, HEADS, HD)
    )
    grad_query, grad_keys, grad_values = attend_backward(
        queries, keys, values, visible, grad_attended
    )
    grad_query = grad_query.astype(BF).reshape(own_rows, width)
    grad_keys = grad_keys.astype(BF).reshape(MB * key_rows, width)
    grad_values = grad_values.astype(BF).reshape(MB * key_rows, width)
    low_sel = (
        contract(grad_keys, w_k, 1, 0) + contract(grad_values, w_v, 1, 0)
    ).astype(BF).reshape(MB, key_rows, width)
    prompt_low = low_sel[:, :half].reshape(MB, seq_count, rows_dev, width).transpose(1, 0, 2, 3)
    run_low = low_sel[:, half:].reshape(MB, run_devs, rows_dev, width).transpose(1, 0, 2, 3)
    blank = jnp.zeros((seq_count, MB, rows_dev, width), BF)
    low_all = jnp.stack(
        [prompt_low, lax.dynamic_update_slice_in_dim(blank, run_low, run_dev, 0)], axis=2
    ).reshape(seq_count, own_rows, width)
    low_own = lax.psum_scatter(low_all, "seq", scatter_dimension=0, tiled=True)[0]
    grad_low = low_own.astype(F32) + contract(grad_query, w_q, 1, 0)
    query_grad = contract(grad_query, hidden_one, 0, 0).astype(BF)
    key_grad = contract(grad_keys, hidden_sel, 0, 0).astype(BF)
    value_grad = contract(grad_values, hidden_sel, 0, 0).astype(BF)
    grad_first, gain_one, bias_one = norm_backward(grad_low, unit_one, inverse_one, gains[0])
    weight_grad = jnp.concatenate(
        [query_grad, key_grad, value_grad, out_grad, up_grad, down_grad], axis=0
    ).reshape(all_count, -1, width)
    weight_sum = lax.psum_scatter(weight_grad, ("dp", "seq"), scatter_dimension=0, tiled=True)[
        0
    ].astype(F32)
    norm_rows = jnp.stack([gain_one, gain_two, gain_final, bias_one, bias_two, bias_final])
    pad_rows = 16
    sent = jnp.concatenate(
        [
            (grad_one + grad_first).astype(BF),
            norm_rows.astype(BF),
            jnp.zeros((pad_rows - 6, width), BF),
        ]
    )
    stream_grads = lax.all_gather(sent[None], "seq", axis=0, tiled=True)
    row_grads = stream_grads[:, :own_rows].reshape(-1, width)
    norm_sum = jnp.sum(stream_grads[:, own_rows : own_rows + 6].astype(F32), axis=0)

    blocks = []
    for part in range(group_count):
        grad_part = contract(head_rows, logit_grads[part], 0, 0) + contract(
            row_grads, hits(row_slots, part).astype(BF), 0, 0
        )
        blocks.append(jnp.concatenate([grad_part, norm_sum.T], axis=1).astype(BF))
    summed_blocks = lax.psum_scatter(jnp.stack(blocks), "dp", scatter_dimension=0, tiled=True)[
        0
    ].astype(F32)
    embed_sum = summed_blocks[:, :vocab_dev]
    norm_all = summed_blocks[:, vocab_dev:].T.reshape(-1)
    norm_own = lax.dynamic_slice_in_dim(norm_all, device_rank * norm_dev, norm_dev, 0)
    squares = (
        jnp.sum(embed_sum * embed_sum)
        + jnp.sum(weight_sum * weight_sum)
        + jnp.sum(norm_own * norm_own)
    )
    square_total, loss_total = lax.psum((squares, loss / seq_count), ("dp", "seq"))
    grad_norm = jnp.sqrt(square_total)
    factor = jnp.minimum(1.0, CLIP_NORM / grad_norm)
    embed_out = adamw(
        table_t, embed_first.T, embed_second.T, embed_sum * factor, LEARN_RATE, WEIGHT_DECAY
    )
    layer_out = adamw(
        layer_weights.T,
        layer_first.T,
        layer_second.T,
        weight_sum * factor,
        LEARN_RATE,
        WEIGHT_DECAY,
    )
    norm_out = adamw(norm_params, norm_first, norm_second, norm_own * factor, NORM_RATE, 0.0)
    return (
        embed_out[0].T,
        embed_out[1].T,
        embed_out[2].T,
        embed_out[3].T,
        layer_out[0].T,
        layer_out[1].T,
        layer_out[2].T,
        layer_out[3].T,
        norm_out[0],
        norm_out[1],
        norm_out[2],
        norm_out[3],
        grad_norm,
        loss_total,
    )


def solution(mesh):
    return jax.shard_map(
        on_device,
        mesh=mesh,
        in_specs=(
            P(None, "dp", None, "seq"),
            P(None, "dp", "seq"),
            P(None, "dp", "seq"),
            P(),
            P(),
            P(),
            P(),
            P(("dp", "seq"), None),
            P(("dp", "seq"), None),
            P(("dp", "seq"), None),
            P(None, ("dp", "seq")),
            P(None, ("dp", "seq")),
            P(None, ("dp", "seq")),
            P(("dp", "seq")),
            P(("dp", "seq")),
            P(("dp", "seq")),
        ),
        out_specs=(
            P(("dp", "seq"), None),
            P(("dp", "seq"), None),
            P(("dp", "seq"), None),
            P(("dp", "seq"), None),
            P(None, ("dp", "seq")),
            P(None, ("dp", "seq")),
            P(None, ("dp", "seq")),
            P(None, ("dp", "seq")),
            P(("dp", "seq")),
            P(("dp", "seq")),
            P(("dp", "seq")),
            P(("dp", "seq")),
            P(),
            P(),
        ),
        check_vma=False,
    )
```

```python
import functools

import jax
import jax.numpy as jnp
from jax import lax
from jax.experimental import pallas as pl
from jax.experimental.pallas import tpu as pltpu
from jax.sharding import PartitionSpec as P

HEADS = 17
HD = 64
FF = 4352
PICK = 32
CLEN = 512
MB = 2
STEP = 10


EPS_NORM = 1e-05
DPO_BETA = 0.05
CLIP_NORM = 1.0
LEARN_RATE = 0.03
NORM_RATE = 0.4
WEIGHT_DECAY = 0.1
MOMENT_ONE = 0.9
MOMENT_TWO = 0.999
EPS_ADAM = 1e-08
MASKED = -1e30
BF = jnp.bfloat16
F32 = jnp.float32
MESH = pl.DeviceIdType.MESH
VMEM = pltpu.VMEM


def meet(peers):
    barrier = pltpu.get_barrier_semaphore()
    for there, peer in peers:

        @pl.when(there)
        def _():
            pl.semaphore_signal(barrier, inc=1, device_id=peer, device_id_type=MESH)

    pl.semaphore_wait(barrier, sum(jnp.where(there, 1, 0) for there, _ in peers))


def direct_kernel(whole, x_ref, o_ref, send_sem, recv_sem):
    seq_count = lax.axis_size("seq")
    group_rank = lax.axis_index("dp")
    me = lax.axis_index("seq")
    count = o_ref.shape[0]
    if whole:
        me = group_rank * seq_count + me

    def peer(step):
        other = lax.rem(me + step, count)
        if whole:
            return (other // seq_count, lax.rem(other, seq_count))
        return (group_rank, other)

    barrier = pltpu.get_barrier_semaphore()

    def greet(step, carry):
        pl.semaphore_signal(barrier, inc=1, device_id=peer(step), device_id_type=MESH)
        return carry

    lax.fori_loop(1, count, greet, 0)
    o_ref[me] = x_ref[...]
    pl.semaphore_wait(barrier, count - 1)

    def copy(step):
        return pltpu.make_async_remote_copy(
            src_ref=x_ref,
            dst_ref=o_ref.at[me],
            send_sem=send_sem.at[step],
            recv_sem=recv_sem.at[step],
            device_id=peer(step),
            device_id_type=MESH,
        )

    def begin(step, carry):
        copy(step).start()
        return carry

    def finish(step, carry):
        copy(step).wait()
        return carry

    lax.fori_loop(1, count, begin, 0)
    lax.fori_loop(1, count, finish, 0)


def direct_gather(x, whole, collective_id):
    count = lax.axis_size("seq") * (lax.axis_size("dp") if whole else 1)
    return pl.pallas_call(
        functools.partial(direct_kernel, whole),
        out_shape=jax.ShapeDtypeStruct((count,) + x.shape, x.dtype),
        in_specs=[pl.BlockSpec(memory_space=VMEM)],
        out_specs=pl.BlockSpec(memory_space=VMEM),
        scratch_shapes=[pltpu.SemaphoreType.DMA((count,)), pltpu.SemaphoreType.DMA((count,))],
        compiler_params=pltpu.CompilerParams(collective_id=collective_id, has_side_effects=True),
    )(x)


def place(rank):
    return (rank // 4, lax.rem(rank, 4) // 2, lax.rem(rank, 2))


def line_peers(at, side, core, group, line):
    return [
        (at > 0, (group, 4 * (at - 1) + 2 * side + core)),
        (at < line - 1, (group, 4 * (at + 1) + 2 * side + core)),
        (at >= 0, (group, 4 * at + 2 * (1 - side) + core)),
        (at >= 0, (group, 4 * at + 2 * side + 1 - core)),
    ]


def spread_kernel(parts, count, *refs):
    given, wanted, pieces = parts
    total = len(pieces)
    x_refs, o_refs = refs[:given], refs[given : given + wanted]
    local_sem, z_send, z_recv, b_send, b_recv, c_send, c_recv = refs[given + wanted :]
    spans = [piece[0] for piece in pieces]
    ins = [piece[1](x_refs) for piece in pieces]
    line = count // 4
    group = lax.axis_index("dp")
    at, side, core = place(lax.axis_index("seq"))
    peers = line_peers(at, side, core, group, line)
    below, above, beside, sibling = (peer for _, peer in peers)
    meet(peers)

    def seq_of(where, which_side, which_core):
        return 4 * where + 2 * which_side + which_core

    def remote(src, dst, send, recv, peer):
        return pltpu.make_async_remote_copy(
            src_ref=src, dst_ref=dst, send_sem=send, recv_sem=recv, device_id=peer, device_id_type=MESH
        )

    def low_high(span):
        low = at // span * span
        return low, low + span

    def view(part, where, which_side, which_core):
        return pieces[part][2](o_refs, seq_of(where, which_side, which_core))

    def where_of(item):
        far = (item + 1) // 2
        return at - far if item % 2 else at + far

    def valid(part, item):
        low, high = low_high(spans[part])
        where = where_of(item)
        return (where >= low) & (where < high)

    def z_copy(part, item, up):
        where = where_of(item)
        far = (item + 1) // 2 + 1
        mark = 2 * far - 1 if up else 2 * far
        src = ins[part] if item == 0 else view(part, where, side, core)
        return remote(
            src,
            view(part, where, side, core),
            z_send.at[part, mark],
            z_recv.at[part, mark],
            above if up else below,
        )

    def b_copy(part, item):
        where = where_of(item)
        src = ins[part] if item == 0 else view(part, where, side, core)
        return remote(
            src, view(part, where, side, core), b_send.at[part, item], b_recv.at[part, item], beside
        )

    def b_arrived(part, item):
        where = where_of(item)
        spot = view(part, where, 1 - side, core)
        return remote(spot, spot, b_send.at[part, item], b_recv.at[part, item], beside)

    def z_arrived(part, item):
        spot = view(part, where_of(item), side, core)
        return remote(spot, spot, z_send.at[part, item], z_recv.at[part, item], beside)

    def c_copy(part, item, from_side):
        where = where_of(item)
        mine = item == 0 and not from_side
        which = 1 - side if from_side else side
        src = ins[part] if mine else view(part, where, which, core)
        index = 2 * item + from_side
        return remote(
            src, view(part, where, which, core), c_send.at[part, index], c_recv.at[part, index], sibling
        )

    def c_arrived(part, item, from_side):
        which = 1 - side if from_side else side
        spot = view(part, where_of(item), which, 1 - core)
        index = 2 * item + from_side
        return remote(spot, spot, c_send.at[part, index], c_recv.at[part, index], sibling)

    items = 2 * line - 1

    def goes_up(part, item):
        low, high = low_high(spans[part])
        return at + 1 < high

    def goes_down(part, item):
        low, high = low_high(spans[part])
        return at - 1 >= low

    def active(part, item):
        return (item + 1) // 2 < spans[part]

    for part in range(total):
        pltpu.make_async_copy(
            ins[part], view(part, at, side, core), local_sem.at[part]
        ).start()

    def launch(part, item):
        @pl.when(valid(part, item))
        def _():
            if item == 0 or item % 2 == 1:
                if (item + 1) // 2 + 1 < spans[part]:
                    @pl.when(goes_up(part, item))
                    def _():
                        z_copy(part, item, True).start()
            if item == 0 or item % 2 == 0:
                if (item + 1) // 2 + 1 < spans[part]:
                    @pl.when(goes_down(part, item))
                    def _():
                        z_copy(part, item, False).start()
            b_copy(part, item).start()
            c_copy(part, item, 0).start()

    def relay(part, item):
        @pl.when(valid(part, item))
        def _():
            b_arrived(part, item).wait_recv()
            c_copy(part, item, 1).start()

    for part in range(total):
        launch(part, 0)
    for far in range(1, line + 1):
        for item in (2 * far - 1, 2 * far):
            for part in range(total):
                if far < line and active(part, item):
                    @pl.when(valid(part, item))
                    def _():
                        z_arrived(part, item).wait_recv()
                    launch(part, item)
        last = [0] if far == 1 else [2 * far - 3, 2 * far - 2]
        for item in last:
            for part in range(total):
                if active(part, item):
                    relay(part, item)
    for part in range(total):
        pltpu.make_async_copy(ins[part], view(part, at, side, core), local_sem.at[part]).wait()
        for item in range(items):
            if not active(part, item):
                continue

            @pl.when(valid(part, item))
            def _():
                if (item == 0 or item % 2 == 1) and (item + 1) // 2 + 1 < spans[part]:
                    @pl.when(goes_up(part, item))
                    def _():
                        z_copy(part, item, True).wait_send()
                if (item == 0 or item % 2 == 0) and (item + 1) // 2 + 1 < spans[part]:
                    @pl.when(goes_down(part, item))
                    def _():
                        z_copy(part, item, False).wait_send()
                b_copy(part, item).wait_send()
                c_copy(part, item, 0).wait_send()
                c_copy(part, item, 1).wait_send()
                c_arrived(part, item, 0).wait_recv()
                c_arrived(part, item, 1).wait_recv()


def spread(blocks, out_shapes, pieces, collective_id):
    count = lax.axis_size("seq")
    total = len(pieces)
    items = 2 * (count // 4) + 1
    sem = pltpu.SemaphoreType.DMA
    return pl.pallas_call(
        functools.partial(spread_kernel, (len(blocks), len(out_shapes), pieces), count),
        out_shape=out_shapes,
        in_specs=[pl.BlockSpec(memory_space=VMEM)] * len(blocks),
        out_specs=[pl.BlockSpec(memory_space=pl.ANY)] * len(out_shapes),
        scratch_shapes=[sem((total,))] + [sem((total, items))] * 4 + [sem((total, 2 * items))] * 2,
        compiler_params=pltpu.CompilerParams(collective_id=collective_id, has_side_effects=True),
    )(*blocks)


def fold_kernel(parts, count, *refs):
    given, wanted, pieces = parts
    total = len(pieces)
    spans = [piece[0] for piece in pieces]
    x_refs, o_refs = refs[:given], refs[given : given + wanted]
    scratch = refs[given + wanted :]
    outs = [piece[3](o_refs) for piece in pieces]
    c_bufs, s_bufs, b_bufs, u_bufs, d_bufs, t_bufs = (
        scratch[i * total : (i + 1) * total] for i in range(6)
    )
    c_send, c_recv, b_send, b_recv, u_send, u_recv, d_send, d_recv = scratch[6 * total :]
    line = count // 4
    group = lax.axis_index("dp")
    at, side, core = place(lax.axis_index("seq"))
    peers = line_peers(at, side, core, group, line)
    below, above, beside, sibling = (peer for _, peer in peers)
    meet(peers)

    def remote(src, dst, send, recv, peer):
        return pltpu.make_async_remote_copy(
            src_ref=src, dst_ref=dst, send_sem=send, recv_sem=recv, device_id=peer, device_id_type=MESH
        )

    def view(part, where, which_side, which_core):
        return pieces[part][2](x_refs, 4 * where + 2 * which_side + which_core)

    def valid(part, where):
        low = at // spans[part] * spans[part]
        return (where >= low) & (where < low + spans[part])

    def slot(part, where):
        return lax.rem(where, spans[part])

    order = []
    for far in range(line - 1, 0, -1):
        order += [(far, 1), (far, -1)]
    order.append((0, 1))

    def c_copy(part, where, other):
        which = 1 - side if other else side
        index = 2 * slot(part, where) + other
        return remote(
            view(part, where, which, 1 - core),
            c_bufs[part].at[index],
            c_send.at[part, index],
            c_recv.at[part, index],
            sibling,
        )

    def b_copy(part, where):
        index = slot(part, where)
        return remote(
            s_bufs[part].at[index], b_bufs[part].at[index], b_send.at[part, index], b_recv.at[part, index], beside
        )

    def u_copy(part, where):
        index = slot(part, where)
        return remote(
            t_bufs[part].at[index], u_bufs[part].at[index], u_send.at[part, index], u_recv.at[part, index], above
        )

    def d_copy(part, where):
        index = slot(part, where)
        return remote(
            t_bufs[part].at[index], d_bufs[part].at[index], d_send.at[part, index], d_recv.at[part, index], below
        )

    def each(action):
        for far, sign in order:
            for part in range(total):
                if far >= spans[part]:
                    continue
                where = at + sign * far

                @pl.when(valid(part, where))
                def _():
                    action(part, where, far, sign)

    each(lambda part, where, far, sign: c_copy(part, where, 1).start())
    each(lambda part, where, far, sign: c_copy(part, where, 0).start())

    def aside(part, where, far, sign):
        c_copy(part, where, 1).wait_recv()
        index = slot(part, where)
        mine = view(part, where, 1 - side, core)[...]
        s_bufs[part][index] = (
            mine.astype(F32) + c_bufs[part][2 * index + 1].astype(F32)
        ).astype(BF)
        b_copy(part, where).start()

    each(aside)

    def along(part, where, far, sign):
        c_copy(part, where, 0).wait_recv()
        b_copy(part, where).wait_recv()
        index = slot(part, where)
        here = slot(part, at)
        value = (
            view(part, where, side, core)[...].astype(F32)
            + c_bufs[part][2 * index].astype(F32)
            + b_bufs[part][index].astype(F32)
        )
        if far == 0:
            outs[part][...] = value

            @pl.when(here > 0)
            def _():
                u_copy(part, where).wait_recv()
                outs[part][...] += u_bufs[part][index].astype(F32)

            @pl.when(here < spans[part] - 1)
            def _():
                d_copy(part, where).wait_recv()
                outs[part][...] += d_bufs[part][index].astype(F32)
        elif sign > 0:
            t_bufs[part][index] = value.astype(BF)

            @pl.when(here > 0)
            def _():
                u_copy(part, where).wait_recv()
                t_bufs[part][index] = (value + u_bufs[part][index].astype(F32)).astype(BF)

            u_copy(part, where).start()
        else:
            t_bufs[part][index] = value.astype(BF)

            @pl.when(here < spans[part] - 1)
            def _():
                d_copy(part, where).wait_recv()
                t_bufs[part][index] = (value + d_bufs[part][index].astype(F32)).astype(BF)

            d_copy(part, where).start()

    each(along)

    def finish(part, where, far, sign):
        c_copy(part, where, 0).wait_send()
        c_copy(part, where, 1).wait_send()
        b_copy(part, where).wait_send()
        if far > 0:
            (u_copy if sign > 0 else d_copy)(part, where).wait_send()

    each(finish)


def fold(arrays, out_shapes, pieces, collective_id):
    count = lax.axis_size("seq")
    total = len(pieces)
    sem = pltpu.SemaphoreType.DMA
    line = count // 4
    bufs = []
    for times in (2, 1, 1, 1, 1, 1):
        bufs += [VMEM((times * piece[0],) + piece[1], BF) for piece in pieces]
    return pl.pallas_call(
        functools.partial(fold_kernel, (len(arrays), len(out_shapes), pieces), count),
        out_shape=[jax.ShapeDtypeStruct(shape, F32) for shape in out_shapes],
        in_specs=[pl.BlockSpec(memory_space=VMEM)] * len(arrays),
        out_specs=[pl.BlockSpec(memory_space=VMEM)] * len(out_shapes),
        scratch_shapes=bufs + [sem((total, 2 * line))] * 2 + [sem((total, line))] * 6,
        compiler_params=pltpu.CompilerParams(
            collective_id=collective_id, has_side_effects=True, vmem_limit_bytes=60 * 2**20
        ),
    )(*arrays)


def exchange_kernel(x_ref, o_ref, own_sem, z_send, z_recv, x_send, x_recv, y_send, y_recv, c_send, c_recv):
    count = o_ref.shape[1]
    line = count // 4
    group = lax.axis_index("dp")
    me = lax.axis_index("seq")
    at, side, core = place(me)
    peers = line_peers(at, side, core, group, line)
    below, above, beside, sibling = (peer for _, peer in peers)
    across = (1 - group, me)
    meet(peers + [(at >= 0, across)])

    def remote(src, dst, send, recv, index, peer):
        return pltpu.make_async_remote_copy(
            src_ref=src, dst_ref=dst, send_sem=send.at[index], recv_sem=recv.at[index],
            device_id=peer, device_id_type=MESH,
        )

    items = [(0, 0)] + [(far, turn) for far in range(1, line) for turn in range(2)]

    def where_of(item):
        return at + item[0] * (2 * item[1] - 1)

    def number(item):
        return 2 * item[0] + item[1]

    def given(item, action):
        @pl.when((where_of(item) >= 0) & (where_of(item) < line))
        def _():
            action()

    def spot(item, other_group, other_side, other_core):
        g = 1 - group if other_group else group
        s = 1 - side if other_side else side
        c = 1 - core if other_core else core
        return o_ref.at[g, 4 * where_of(item) + 2 * s + c]

    def here(item, other_group, other_side):
        if item == (0, 0) and not other_group and not other_side:
            return x_ref
        return spot(item, other_group, other_side, False)

    def z_copy(item, turn, peer):
        far = (item[0] + 1, turn)
        return remote(here(item, 0, 0), spot(item, 0, 0, 0), z_send, z_recv, number(far), peer)

    def side_copy(item, other_group, arrived):
        dst = spot(item, other_group, arrived, 0)
        src = dst if arrived else here(item, other_group, 0)
        return remote(src, dst, x_send, x_recv, 2 * number(item) + other_group, beside)

    def cross_copy(item, other_side, arrived):
        dst = spot(item, arrived, other_side, 0)
        src = dst if arrived else here(item, 0, other_side)
        return remote(src, dst, y_send, y_recv, 2 * number(item) + other_side, across)

    def core_copy(item, other_group, other_side, arrived):
        dst = spot(item, other_group, other_side, arrived)
        src = dst if arrived else here(item, other_group, other_side)
        index = 4 * number(item) + 2 * other_group + other_side
        return remote(src, dst, c_send, c_recv, index, sibling)

    def by_side(item):
        return lax.rem(where_of(item), 2) == 0

    def z_links(item, act):
        far, turn = item
        if far + 1 < line:
            if far == 0 or turn == 0:

                @pl.when(at + 1 < line)
                def _():
                    act(z_copy(item, 0, above))

            if far == 0 or turn == 1:

                @pl.when(at > 0)
                def _():
                    act(z_copy(item, 1, below))

    def start(copy):
        copy.start()

    def launch(item):
        z_links(item, start)
        side_copy(item, 0, False).start()
        cross_copy(item, 0, False).start()
        core_copy(item, 0, 0, False).start()

    def first(item):
        z = remote(spot(item, 0, 0, 0), spot(item, 0, 0, 0), z_send, z_recv, number(item), beside)
        z.wait_recv()
        launch(item)

    def second(item):
        side_copy(item, 0, True).wait_recv()

        @pl.when(jnp.logical_not(by_side(item)))
        def _():
            cross_copy(item, 1, False).start()

        core_copy(item, 0, 1, False).start()
        cross_copy(item, 0, True).wait_recv()

        @pl.when(by_side(item))
        def _():
            side_copy(item, 1, False).start()

        core_copy(item, 1, 0, False).start()

    def third(item):
        @pl.when(by_side(item))
        def _():
            side_copy(item, 1, True).wait_recv()

        @pl.when(jnp.logical_not(by_side(item)))
        def _():
            cross_copy(item, 1, True).wait_recv()

        core_copy(item, 1, 1, False).start()

    def at_far(far):
        return [item for item in items if item[0] == far]

    own = pltpu.make_async_copy(x_ref, spot((0, 0), 0, 0, 0), own_sem.at[0])
    own.start()
    launch((0, 0))
    for step in range(1, line + 2):
        for item in at_far(step):
            given(item, functools.partial(first, item))
        for item in at_far(step - 1):
            given(item, functools.partial(second, item))
        if step >= 2:
            for item in at_far(step - 2):
                given(item, functools.partial(third, item))
    own.wait()

    def finish(item):
        z_links(item, lambda copy: copy.wait_send())
        side_copy(item, 0, False).wait_send()
        cross_copy(item, 0, False).wait_send()

        @pl.when(by_side(item))
        def _():
            side_copy(item, 1, False).wait_send()

        @pl.when(jnp.logical_not(by_side(item)))
        def _():
            cross_copy(item, 1, False).wait_send()

        for other_group in range(2):
            for other_side in range(2):
                core_copy(item, other_group, other_side, False).wait_send()
                core_copy(item, other_group, other_side, True).wait_recv()

    for item in items:
        given(item, functools.partial(finish, item))


def exchange(x, collective_id):
    count = lax.axis_size("seq")
    marks = 2 * (count // 4) + 2
    sem = pltpu.SemaphoreType.DMA
    return pl.pallas_call(
        exchange_kernel,
        out_shape=jax.ShapeDtypeStruct((2, count) + x.shape, x.dtype),
        in_specs=[pl.BlockSpec(memory_space=VMEM)],
        out_specs=pl.BlockSpec(memory_space=pl.ANY),
        scratch_shapes=[sem((1,))] + [sem((marks,))] * 2 + [sem((2 * marks,))] * 4 + [sem((4 * marks,))] * 2,
        compiler_params=pltpu.CompilerParams(collective_id=collective_id, has_side_effects=True),
    )(x)


def row_gather(line, rows, cuts):
    size = rows // cuts
    return tuple(
        (
            line,
            lambda x, h=h: x[0].at[pl.ds(h * size, size)],
            lambda o, q, h=h: o[0].at[q, pl.ds(h * size, size)],
        )
        for h in range(cuts)
    )


def row_pieces(line, rows, width, cuts):
    size = rows // cuts
    return tuple(
        (
            line,
            (size, width),
            lambda x, q, h=h: x[0].at[q, pl.ds(h * size, size)],
            lambda o, h=h: o[0].at[pl.ds(h * size, size)],
        )
        for h in range(cuts)
    )


def visible_rows(kind, run_devs, rows_dev, half, q):
    first = half + rows_dev * lax.rem(q, run_devs) if kind else rows_dev * q
    return pl.multiple_of(first, 32)


def visible_gather(line, run_devs, rows_dev, half):
    size = rows_dev // 2
    return tuple(
        (
            run_devs // 4 if kind else line,
            lambda x, m=m, kind=kind, j=j: x[0].at[m, kind, pl.ds(size * j, size)],
            lambda o, q, m=m, kind=kind, j=j: o[0].at[
                m, pl.ds(visible_rows(kind, run_devs, rows_dev, half, q) + size * j, size)
            ],
        )
        for kind in range(2)
        for m in range(MB)
        for j in range(2)
    )


def visible_sum(line, run_devs, rows_dev, half, width):
    return tuple(
        (
            run_devs // 4 if kind else line,
            (MB, rows_dev, width),
            lambda x, q, kind=kind: x[0].at[
                :, pl.ds(visible_rows(kind, run_devs, rows_dev, half, q), rows_dev)
            ],
            lambda o, kind=kind: o[0].at[:, kind],
        )
        for kind in range(2)
    )


def place_kernel(l_ref, r_ref, *refs):
    refs[-1][...] = jnp.dot(l_ref[...], r_ref[...], preferred_element_type=F32).astype(BF)


def place_product(buffer, left, right, first, rows):
    depth, width = right.shape
    block = width // 2
    given = () if buffer is None else (buffer,)
    return pl.pallas_call(
        place_kernel,
        grid=(left.shape[0] // block,),
        out_shape=jax.ShapeDtypeStruct((rows, width), BF),
        in_specs=[
            pl.BlockSpec((block, depth), lambda i: (i, 0)),
            pl.BlockSpec((depth, width), lambda i: (0, 0)),
        ]
        + [pl.BlockSpec(memory_space=pl.ANY)] * len(given),
        out_specs=pl.BlockSpec((block, width), lambda i: (first // block + i, 0)),
        input_output_aliases={2: 0} if given else {},
    )(left, right, *given)


def contract(left, right, left_dim, right_dim):
    return lax.dot_general(
        left, right, (((left_dim,), (right_dim,)), ((), ())), preferred_element_type=F32
    )


def norm_forward(values, gain, bias):
    centred = values - jnp.mean(values, axis=-1, keepdims=True)
    inverse = lax.rsqrt(jnp.mean(centred * centred, axis=-1, keepdims=True) + EPS_NORM)
    unit = centred * inverse
    return (unit * gain + bias, unit, inverse)


def norm_backward(upstream, unit, inverse, gain):
    scaled = upstream * gain
    inner = (
        scaled
        - jnp.mean(scaled, axis=-1, keepdims=True)
        - unit * jnp.mean(scaled * unit, axis=-1, keepdims=True)
    )
    return (inverse * inner, jnp.sum(upstream * unit, axis=0), jnp.sum(upstream, axis=0))


def head_probs(pos_ref, q, k):
    scores = contract(q, k, 0, 0) * HD ** (-0.5)
    key_pos = lax.broadcasted_iota(jnp.int32, scores.shape, 1)
    scores = jnp.where(key_pos <= pos_ref[...], scores, MASKED)
    shifted = jnp.exp(scores - jnp.max(scores, axis=1, keepdims=True))
    return shifted * (1.0 / jnp.sum(shifted, axis=1, keepdims=True))


def attend_kernel(pos_ref, q_ref, kv_ref, o_ref):
    probs = head_probs(pos_ref, q_ref[...], kv_ref[0]).astype(BF)
    o_ref[...] = contract(kv_ref[1], probs, 1, 1).astype(BF)


def attend_back_kernel(pos_ref, q_ref, kv_ref, g_ref, dq_ref, dkv_ref):
    q, k, v, g = q_ref[...], kv_ref[0], kv_ref[1], g_ref[...]
    probs = head_probs(pos_ref, q, k)
    grad = contract(g, v, 0, 0)
    back = (probs * (grad - jnp.sum(probs * grad, axis=1, keepdims=True))).astype(BF)
    scale = HD ** (-0.5)
    dq_ref[...] = (contract(k, back, 1, 1) * scale).astype(BF)
    dkv_ref[0] = (contract(q, back, 1, 0) * scale).astype(BF)
    dkv_ref[1] = contract(g, probs.astype(BF), 1, 0).astype(BF)


def attend(query_pos, q, kv):
    rows, keys = query_pos.shape[0], kv.shape[2] * query_pos.shape[0] // q.shape[1]
    small = pl.BlockSpec((HD, rows), lambda m, h: (h, m))
    large = pl.BlockSpec((2, HD, keys), lambda m, h: (0, h, m))
    return pl.pallas_call(
        attend_kernel,
        grid=(q.shape[1] // rows, HEADS),
        out_shape=jax.ShapeDtypeStruct(q.shape, BF),
        in_specs=[pl.BlockSpec((rows, 1), lambda m, h: (0, 0)), small, large],
        out_specs=small,
    )(query_pos, q, kv)


def attend_back(query_pos, q, kv, grad_out):
    rows, keys = query_pos.shape[0], kv.shape[2] * query_pos.shape[0] // q.shape[1]
    small = pl.BlockSpec((HD, rows), lambda m, h: (h, m))
    large = pl.BlockSpec((2, HD, keys), lambda m, h: (0, h, m))
    return pl.pallas_call(
        attend_back_kernel,
        grid=(q.shape[1] // rows, HEADS),
        out_shape=[jax.ShapeDtypeStruct(q.shape, BF), jax.ShapeDtypeStruct(kv.shape, BF)],
        in_specs=[pl.BlockSpec((rows, 1), lambda m, h: (0, 0)), small, large, small],
        out_specs=[small, large],
    )(query_pos, q, kv, grad_out)


def lookup_kernel(first_ref, slot_ref, table_ref, *refs):
    slots = slot_ref[...] - first_ref[0]
    ids = lax.broadcasted_iota(jnp.int32, (slots.shape[0], table_ref.shape[1]), 1)
    rows = contract(jnp.where(slots == ids, 1.0, 0.0).astype(BF), table_ref[...], 1, 1).astype(BF)
    refs[-1][...] = rows if len(refs) == 1 else refs[0][...] + rows


def lookup(first, slots, table, others, block):
    width, held = table.shape
    rows = pl.BlockSpec((block, width), lambda i: (i, 0))
    given = () if others is None else (others,)
    return pl.pallas_call(
        lookup_kernel,
        grid=(slots.shape[0] // block,),
        out_shape=jax.ShapeDtypeStruct((slots.shape[0], width), BF),
        in_specs=[
            pl.BlockSpec(memory_space=pltpu.SMEM),
            pl.BlockSpec((block, 1), lambda i: (i, 0)),
            pl.BlockSpec((width, held), lambda i: (0, 0)),
        ]
        + [rows] * len(given),
        out_specs=rows,
    )(first, slots, table, *given)


def adamw(weight, moment_a, moment_b, gradient, rate, decay):
    moment_a = MOMENT_ONE * moment_a + (1.0 - MOMENT_ONE) * gradient
    moment_b = MOMENT_TWO * moment_b + (1.0 - MOMENT_TWO) * gradient * gradient
    update = (
        moment_a
        / (1.0 - MOMENT_ONE**STEP)
        / (jnp.sqrt(moment_b / (1.0 - MOMENT_TWO**STEP)) + EPS_ADAM)
    )
    weight = weight - rate * (update + decay * weight)
    return (weight, moment_a, moment_b, weight.astype(BF))


def on_device(
    tokens,
    targets,
    counted,
    cont_label,
    pair_map,
    ref_logp,
    vocab_slot,
    embed_table,
    embed_first,
    embed_second,
    layer_weights,
    layer_first,
    layer_second,
    norm_params,
    norm_first,
    norm_second,
):
    seq_count = lax.axis_size("seq")
    group_count = lax.axis_size("dp")
    all_count = seq_count * group_count
    seq_rank = lax.axis_index("seq")
    group_rank = lax.axis_index("dp")
    device_rank = group_rank * seq_count + seq_rank
    rows_dev = tokens.shape[3]
    half = rows_dev * seq_count
    vocab_dev, width = embed_table.shape
    run_count = half // CLEN
    run_devs = CLEN // rows_dev
    own_rows = MB * 2 * rows_dev

    table_t = embed_table.T
    norm_dev = norm_params.shape[0]
    norm_parts = [norm_params]
    for step in range(1, group_count):
        norm_parts.append(
            lax.ppermute(
                norm_params, "dp", [(i, (i - step) % group_count) for i in range(group_count)]
            )
        )
    sent, *norm_parts = lax.optimization_barrier((table_t.astype(BF), *norm_parts))
    norm_all = jnp.zeros((group_count, norm_dev), F32)
    for step in range(group_count):
        norm_all = lax.dynamic_update_index_in_dim(
            norm_all, norm_parts[step], lax.rem(group_rank + step, group_count), 0
        )
    slab_t = [sent]
    for step in range(1, group_count):
        slab_t.append(
            lax.ppermute(
                slab_t[0], "dp", [(i, (i - step) % group_count) for i in range(group_count)]
            )
        )
    weights = lax.all_gather(
        layer_weights.T.astype(BF)[None], ("dp", "seq"), axis=0, tiled=True
    ).reshape(-1, width)
    w_q = weights[:width]
    w_o = weights[3 * width : 4 * width]
    w_kv = weights[width : 3 * width]
    w_up = weights[4 * width : 4 * width + FF]
    w_dn = weights[4 * width + FF :]

    marks = counted[:, 0]
    spots = jnp.arange(rows_dev, dtype=jnp.int32)
    ranks = (
        jnp.sum(jnp.where(spots[None, :, None] <= spots[None, None, :], marks[:, :, None], 0), axis=1)
        - 1
    )
    pick_ids = jnp.arange(PICK, dtype=jnp.int32)
    pick_hit = (ranks[:, None, :] == pick_ids[None, :, None]) & (marks[:, None, :] == 1)
    pick_targets = jnp.sum(jnp.where(pick_hit, targets[:, 0][:, None, :], 0), axis=2)
    pick_low = pick_hit.astype(BF)
    slots = vocab_slot[jnp.concatenate([tokens[:, 0].reshape(-1), pick_targets.reshape(-1)])]
    small = jnp.concatenate([slots.astype(F32), norm_all.reshape(-1)])
    small = jnp.pad(small, (0, -small.shape[0] % 1024)).reshape(-1, 128)
    small_all = direct_gather(small, False, 1).reshape(seq_count, -1)
    slots_all = small_all[:, : own_rows + MB * PICK].astype(jnp.int32)
    gains = (
        small_all[:, own_rows + MB * PICK :][:, : group_count * norm_dev]
        .reshape(seq_count, group_count, norm_dev)
        .transpose(1, 0, 2)
        .astype(BF)
        .astype(F32)
        .reshape(6, width)
    )
    row_slots = slots_all[:, :own_rows].reshape(-1)
    target_slots = slots_all[:, own_rows:].reshape(-1)
    vocab_ids = jnp.arange(vocab_dev, dtype=jnp.int32)

    def hits(slot_ids, step):
        part = lax.rem(group_rank + step, group_count)
        first = (part * seq_count + seq_rank) * vocab_dev
        return (slot_ids - first)[:, None] == vocab_ids[None, :]

    partial = None
    for step in range(group_count):
        part = lax.rem(group_rank + step, group_count)
        first = (part * seq_count + seq_rank) * vocab_dev
        partial = lookup(first[None], row_slots[:, None], slab_t[step], partial, own_rows)
    line = seq_count // 4
    (stream,) = fold(
        [partial.reshape(seq_count, own_rows, width)],
        [(own_rows, width)],
        row_pieces(line, own_rows, width, 2),
        2,
    )

    normed, unit_one, inverse_one = norm_forward(stream, gains[0], gains[3])
    hidden_one = normed.astype(BF)
    run_dev = seq_rank // run_devs * run_devs
    key_rows = half + CLEN
    (hidden_sel,) = spread(
        [hidden_one.reshape(MB, 2, rows_dev, width)],
        [jax.ShapeDtypeStruct((MB, key_rows, width), BF)],
        visible_gather(line, run_devs, rows_dev, half),
        3,
    )
    hidden_sel = hidden_sel.reshape(MB * key_rows, width)
    pairs = contract(w_kv, hidden_sel, 1, 1).astype(BF).reshape(2, width, MB * key_rows)
    queries = contract(w_q, hidden_one, 1, 1).astype(BF)
    start = seq_rank * rows_dev
    query_pos = jnp.concatenate([start + spots, half + (start - run_dev * rows_dev) + spots])[:, None]
    attended = attend(query_pos, queries, pairs)
    stream_one = stream + contract(attended, w_o, 0, 0)
    normed, unit_two, inverse_two = norm_forward(stream_one, gains[1], gains[4])
    hidden_two = normed.astype(BF)
    up_proj = contract(w_up, hidden_two, 1, 1)
    activated = jax.nn.gelu(up_proj, approximate=False).astype(BF)
    stream_two = stream_one + contract(activated, w_dn, 0, 0)
    normed, unit_final, inverse_final = norm_forward(stream_two, gains[2], gains[5])
    final = normed.astype(BF).reshape(MB, 2, rows_dev, width)[:, 1]
    picked = jnp.einsum("mpr,mrd->mpd", pick_low, final, preferred_element_type=F32).astype(BF)

    (head_rows,) = spread(
        [picked.reshape(MB * PICK, width)],
        [jax.ShapeDtypeStruct((seq_count, MB * PICK, width), BF)],
        row_gather(line, MB * PICK, 1),
        4,
    )
    head_rows = head_rows.reshape(seq_count * MB * PICK, width)
    logits = [contract(head_rows, slab_t[part], 1, 0) for part in range(group_count)]
    target_hits = [hits(target_slots, part) for part in range(group_count)]
    highest = jnp.max(logits[0], axis=1)
    for part in range(1, group_count):
        highest = jnp.maximum(highest, jnp.max(logits[part], axis=1))
    summed = jnp.zeros_like(highest)
    target_logit = jnp.zeros_like(highest)
    for part in range(group_count):
        summed = summed + jnp.sum(jnp.exp(logits[part] - highest[:, None]), axis=1)
        target_logit = target_logit + jnp.sum(jnp.where(target_hits[part], logits[part], 0.0), axis=1)
    stats = direct_gather(
        jnp.stack([highest, summed, target_logit]).reshape(-1, 128), False, 5
    ).reshape(seq_count, 3, -1)
    overall = jnp.max(stats[:, 0], axis=0)
    total = jnp.sum(stats[:, 1] * jnp.exp(stats[:, 0] - overall[None]), axis=0)
    log_total = overall + jnp.log(total)
    token_lp = jnp.sum(stats[:, 2], axis=0) - log_total

    run_ids = jnp.arange(run_count, dtype=jnp.int32)
    run_of_dev = jnp.arange(seq_count, dtype=jnp.int32) * rows_dev // CLEN
    run_match = run_of_dev[:, None] == run_ids[None, :]
    dev_lp = jnp.sum(token_lp.reshape(seq_count, MB, PICK), axis=2)
    run_lp = jnp.sum(jnp.where(run_match[:, None, :], dev_lp[:, :, None], 0.0), axis=0)
    labels = lax.dynamic_index_in_dim(cont_label, group_rank, 1, keepdims=False)
    pairing = lax.dynamic_index_in_dim(pair_map, group_rank, 1, keepdims=False)
    reference_lp = lax.dynamic_index_in_dim(ref_logp, group_rank, 1, keepdims=False)
    label_match = labels[:, :, None] == run_ids[None, None, :]
    label_lp = jnp.sum(jnp.where(label_match, run_lp[:, :, None], 0.0), axis=1)
    margin = label_lp - reference_lp
    chosen = pairing[:, 0::2, None] == run_ids[None, None, :]
    rejected = pairing[:, 1::2, None] == run_ids[None, None, :]
    delta = jnp.sum(jnp.where(chosen, margin[:, None, :], 0.0), axis=2) - jnp.sum(
        jnp.where(rejected, margin[:, None, :], 0.0), axis=2
    )
    loss = jnp.sum(jax.nn.softplus(-DPO_BETA * delta))
    pair_grad = -DPO_BETA * jax.nn.sigmoid(-DPO_BETA * delta)
    label_grad = jnp.sum(
        jnp.where(chosen, pair_grad[:, :, None], 0.0)
        - jnp.where(rejected, pair_grad[:, :, None], 0.0),
        axis=1,
    )
    run_grad = jnp.sum(jnp.where(label_match, label_grad[:, None, :], 0.0), axis=2)
    dev_grad = jnp.sum(jnp.where(run_match[:, None, :], run_grad[None], 0.0), axis=2)
    row_grad = jnp.broadcast_to(dev_grad[:, :, None], (seq_count, MB, PICK)).reshape(-1)

    head_back = 0.0
    logit_grads = []
    for part in range(group_count):
        logit_grad = (
            row_grad[:, None]
            * (target_hits[part].astype(F32) - jnp.exp(logits[part] - log_total[:, None]))
        ).astype(BF)
        logit_grads.append(logit_grad)
        head_back = head_back + contract(logit_grad, slab_t[part], 1, 1)
    head_back = head_back.astype(BF)
    moved = [(i, (i + 1) % group_count) for i in range(group_count)]
    if group_count == 2:
        head_back, head_part = lax.optimization_barrier(
            (head_back, contract(head_rows, logit_grads[1], 0, 0).astype(BF))
        )
        head_other = lax.ppermute(head_part, "dp", moved)
    (row_back,) = fold(
        [head_back.reshape(seq_count, MB * PICK, width)],
        [(MB * PICK, width)],
        row_pieces(line, MB * PICK, width, 1),
        6,
    )
    row_back = row_back.astype(BF).reshape(MB, PICK, width)
    cont_back = jnp.einsum("mpr,mpd->mrd", pick_low, row_back, preferred_element_type=F32)
    upstream = jnp.concatenate(
        [jnp.zeros((MB, 1, rows_dev, width), F32), cont_back[:, None]], axis=1
    ).reshape(own_rows, width)

    grad_two, gain_final, bias_final = norm_backward(upstream, unit_final, inverse_final, gains[2])
    grad_ffn = grad_two.astype(BF)
    columns = weights.shape[0]
    weight_grad = place_product(None, activated, grad_ffn, 4 * width + FF, columns)
    grad_act = contract(w_dn, grad_ffn, 1, 1)
    _, gelu_pull = jax.vjp(lambda pre_act: jax.nn.gelu(pre_act, approximate=False), up_proj)
    grad_up = gelu_pull(grad_act)[0].astype(BF)
    weight_grad = place_product(weight_grad, grad_up, hidden_two, 4 * width, columns)
    grad_hidden = contract(grad_up, w_up, 0, 0)
    grad_mid, gain_two, bias_two = norm_backward(grad_hidden, unit_two, inverse_two, gains[1])
    grad_one = grad_two + grad_mid
    grad_branch = grad_one.astype(BF)
    weight_grad = place_product(weight_grad, attended, grad_branch, 3 * width, columns)
    grad_attended = contract(w_o, grad_branch, 1, 1).astype(BF)
    grad_query, grad_pairs = attend_back(query_pos, queries, pairs, grad_attended)
    grad_pairs = grad_pairs.reshape(2 * width, MB * key_rows)
    weight_grad = place_product(weight_grad, grad_query, hidden_one, 0, columns)
    weight_grad = place_product(weight_grad, grad_pairs, hidden_sel, width, columns)
    low_sel = contract(grad_pairs, w_kv, 0, 0).astype(BF).reshape(MB, key_rows, width)
    weight_sum = lax.psum_scatter(
        weight_grad.reshape(all_count, -1, width), ("dp", "seq"), scatter_dimension=0, tiled=True
    )[0].astype(F32)
    (low_own,) = fold(
        [low_sel],
        [(MB, 2, rows_dev, width)],
        visible_sum(line, run_devs, rows_dev, half, width),
        7,
    )
    grad_low = low_own.reshape(own_rows, width) + contract(grad_query, w_q, 0, 0)
    grad_first, gain_one, bias_one = norm_backward(grad_low, unit_one, inverse_one, gains[0])
    norm_rows = jnp.stack([gain_one, gain_two, gain_final, bias_one, bias_two, bias_final])
    if group_count == 2:
        head_own = contract(head_rows, logit_grads[0], 0, 0)
        pad_rows = 8
        all_rows = exchange(
            jnp.concatenate(
                [grad_one + grad_first, norm_rows, jnp.zeros((pad_rows - 6, width), F32)]
            ).astype(BF),
            8,
        )
        other_slots = lax.ppermute(row_slots, "dp", moved)
        all_slots = jnp.where(
            group_rank == 0,
            jnp.stack([row_slots, other_slots]),
            jnp.stack([other_slots, row_slots]),
        ).reshape(all_count, own_rows)
        all_slots = jnp.pad(all_slots, ((0, 0), (0, pad_rows)), constant_values=-1).reshape(-1)
        embed_sum = (
            contract(all_rows.reshape(-1, width), hits(all_slots, 0).astype(BF), 0, 0)
            + head_own
            + head_other.astype(F32)
        )
        norm_all = jnp.sum(
            all_rows.reshape(all_count, own_rows + pad_rows, width)[
                :, own_rows : own_rows + 6
            ].astype(F32),
            axis=0,
        )
    else:
        row_grads, norm_grads = spread(
            [
                (grad_one + grad_first).astype(BF),
                jnp.concatenate([norm_rows, jnp.zeros((10, width), F32)]).astype(BF),
            ],
            [
                jax.ShapeDtypeStruct((seq_count, own_rows, width), BF),
                jax.ShapeDtypeStruct((seq_count, 16, width), BF),
            ],
            row_gather(line, own_rows, 2)
            + ((line, lambda x: x[1], lambda o, q: o[1].at[q]),),
            8,
        )
        row_grads = row_grads.reshape(-1, width)
        norm_sum = jnp.sum(norm_grads[:, :6].astype(F32), axis=0)
        norm_all = norm_sum
        for step in range(1, group_count):
            norm_all = norm_all + lax.ppermute(
                norm_sum, "dp", [(i, (i + step) % group_count) for i in range(group_count)]
            )

        def table_grad(step):
            return contract(head_rows, logit_grads[step], 0, 0) + contract(
                row_grads, hits(row_slots, step).astype(BF), 0, 0
            )

        arrived = [
            lax.ppermute(
                table_grad(step).astype(BF),
                "dp",
                [(i, (i + step) % group_count) for i in range(group_count)],
            )
            for step in range(1, group_count)
        ]
        embed_sum = table_grad(0)
        for block in arrived:
            embed_sum = embed_sum + block.astype(F32)
    norm_own = lax.dynamic_slice_in_dim(norm_all.reshape(-1), device_rank * norm_dev, norm_dev, 0)
    squares = (
        jnp.sum(embed_sum * embed_sum)
        + jnp.sum(weight_sum * weight_sum)
        + jnp.sum(norm_own * norm_own)
    )
    lanes = lax.broadcasted_iota(jnp.int32, (8, 128), 1)
    scalars = direct_gather(
        jnp.where(lanes == 0, squares, jnp.where(lanes == 1, loss, 0.0)), True, 9
    )
    square_total = jnp.sum(scalars[:, 0, 0])
    loss_total = jnp.sum(scalars[::seq_count, 0, 1])
    grad_norm = jnp.sqrt(square_total)
    factor = jnp.minimum(1.0, CLIP_NORM / grad_norm)
    embed_out = adamw(
        table_t, embed_first.T, embed_second.T, embed_sum * factor, LEARN_RATE, WEIGHT_DECAY
    )
    layer_out = adamw(
        layer_weights.T,
        layer_first.T,
        layer_second.T,
        weight_sum * factor,
        LEARN_RATE,
        WEIGHT_DECAY,
    )
    norm_out = adamw(norm_params, norm_first, norm_second, norm_own * factor, NORM_RATE, 0.0)
    return (
        embed_out[0].T,
        embed_out[1].T,
        embed_out[2].T,
        embed_out[3].T,
        layer_out[0].T,
        layer_out[1].T,
        layer_out[2].T,
        layer_out[3].T,
        norm_out[0],
        norm_out[1],
        norm_out[2],
        norm_out[3],
        grad_norm,
        loss_total,
    )


def solution(mesh):
    return jax.shard_map(
        on_device,
        mesh=mesh,
        in_specs=(
            P(None, "dp", None, "seq"),
            P(None, "dp", "seq"),
            P(None, "dp", "seq"),
            P(),
            P(),
            P(),
            P(),
            P(("dp", "seq"), None),
            P(("dp", "seq"), None),
            P(("dp", "seq"), None),
            P(None, ("dp", "seq")),
            P(None, ("dp", "seq")),
            P(None, ("dp", "seq")),
            P(("dp", "seq")),
            P(("dp", "seq")),
            P(("dp", "seq")),
        ),
        out_specs=(
            P(("dp", "seq"), None),
            P(("dp", "seq"), None),
            P(("dp", "seq"), None),
            P(("dp", "seq"), None),
            P(None, ("dp", "seq")),
            P(None, ("dp", "seq")),
            P(None, ("dp", "seq")),
            P(None, ("dp", "seq")),
            P(("dp", "seq")),
            P(("dp", "seq")),
            P(("dp", "seq")),
            P(("dp", "seq")),
            P(),
            P(),
        ),
        check_vma=False,
    )
```

```python
import functools

import jax
import jax.numpy as jnp
from jax import lax
from jax.experimental import pallas as pl
from jax.experimental.pallas import tpu as pltpu
from jax.sharding import PartitionSpec as P


HEADS = 17
HD = 64
FF = 4352
PICK = 32
CLEN = 512
MB = 2
STEP = 10


EPS_NORM = 1e-05
DPO_BETA = 0.05
CLIP_NORM = 1.0
LEARN_RATE = 0.03
NORM_RATE = 0.4
WEIGHT_DECAY = 0.1
MOMENT_ONE = 0.9
MOMENT_TWO = 0.999
EPS_ADAM = 1e-08
MASKED = -1e30
BF = jnp.bfloat16
F32 = jnp.float32
MESH = pl.DeviceIdType.MESH
VMEM = pltpu.VMEM


def meet(peers):
    barrier = pltpu.get_barrier_semaphore()
    for there, peer in peers:

        @pl.when(there)
        def _():
            pl.semaphore_signal(barrier, inc=1, device_id=peer, device_id_type=MESH)

    pl.semaphore_wait(barrier, sum(jnp.where(there, 1, 0) for there, _ in peers))


def direct_kernel(whole, x_ref, o_ref, send_sem, recv_sem):
    seq_count = lax.axis_size("seq")
    group_rank = lax.axis_index("dp")
    me = lax.axis_index("seq")
    count = o_ref.shape[0]
    if whole:
        me = group_rank * seq_count + me

    def peer(step):
        other = lax.rem(me + step, count)
        if whole:
            return (other // seq_count, lax.rem(other, seq_count))
        return (group_rank, other)

    barrier = pltpu.get_barrier_semaphore()

    def greet(step, carry):
        pl.semaphore_signal(barrier, inc=1, device_id=peer(step), device_id_type=MESH)
        return carry

    lax.fori_loop(1, count, greet, 0)
    o_ref[me] = x_ref[...]
    pl.semaphore_wait(barrier, count - 1)

    def copy(step):
        return pltpu.make_async_remote_copy(
            src_ref=x_ref,
            dst_ref=o_ref.at[me],
            send_sem=send_sem.at[step],
            recv_sem=recv_sem.at[step],
            device_id=peer(step),
            device_id_type=MESH,
        )

    def begin(step, carry):
        copy(step).start()
        return carry

    def finish(step, carry):
        copy(step).wait()
        return carry

    lax.fori_loop(1, count, begin, 0)
    lax.fori_loop(1, count, finish, 0)


def direct_gather(x, whole, collective_id):
    count = lax.axis_size("seq") * (lax.axis_size("dp") if whole else 1)
    return pl.pallas_call(
        functools.partial(direct_kernel, whole),
        out_shape=jax.ShapeDtypeStruct((count,) + x.shape, x.dtype),
        in_specs=[pl.BlockSpec(memory_space=VMEM)],
        out_specs=pl.BlockSpec(memory_space=VMEM),
        scratch_shapes=[pltpu.SemaphoreType.DMA((count,)), pltpu.SemaphoreType.DMA((count,))],
        compiler_params=pltpu.CompilerParams(collective_id=collective_id, has_side_effects=True),
    )(x)


def place(rank):
    return (rank // 4, lax.rem(rank, 4) // 2, lax.rem(rank, 2))


def line_peers(at, side, core, group, line):
    return [
        (at > 0, (group, 4 * (at - 1) + 2 * side + core)),
        (at < line - 1, (group, 4 * (at + 1) + 2 * side + core)),
        (at >= 0, (group, 4 * at + 2 * (1 - side) + core)),
        (at >= 0, (group, 4 * at + 2 * side + 1 - core)),
    ]


def spread_kernel(parts, count, *refs):
    given, wanted, pieces = parts
    total = len(pieces)
    x_refs, o_refs = refs[:given], refs[given : given + wanted]
    local_sem, z_send, z_recv, b_send, b_recv, c_send, c_recv = refs[given + wanted :]
    spans = [piece[0] for piece in pieces]
    ins = [piece[1](x_refs) for piece in pieces]
    line = count // 4
    group = lax.axis_index("dp")
    at, side, core = place(lax.axis_index("seq"))
    peers = line_peers(at, side, core, group, line)
    below, above, beside, sibling = (peer for _, peer in peers)
    meet(peers)

    def seq_of(where, which_side, which_core):
        return 4 * where + 2 * which_side + which_core

    def remote(src, dst, send, recv, peer):
        return pltpu.make_async_remote_copy(
            src_ref=src, dst_ref=dst, send_sem=send, recv_sem=recv, device_id=peer, device_id_type=MESH
        )

    def low_high(span):
        low = at // span * span
        return low, low + span

    def view(part, where, which_side, which_core):
        return pieces[part][2](o_refs, seq_of(where, which_side, which_core))

    def where_of(item):
        far = (item + 1) // 2
        return at - far if item % 2 else at + far

    def valid(part, item):
        low, high = low_high(spans[part])
        where = where_of(item)
        return (where >= low) & (where < high)

    def z_copy(part, item, up):
        where = where_of(item)
        far = (item + 1) // 2 + 1
        mark = 2 * far - 1 if up else 2 * far
        src = ins[part] if item == 0 else view(part, where, side, core)
        return remote(
            src,
            view(part, where, side, core),
            z_send.at[part, mark],
            z_recv.at[part, mark],
            above if up else below,
        )

    def b_copy(part, item):
        where = where_of(item)
        src = ins[part] if item == 0 else view(part, where, side, core)
        return remote(
            src, view(part, where, side, core), b_send.at[part, item], b_recv.at[part, item], beside
        )

    def b_arrived(part, item):
        where = where_of(item)
        spot = view(part, where, 1 - side, core)
        return remote(spot, spot, b_send.at[part, item], b_recv.at[part, item], beside)

    def z_arrived(part, item):
        spot = view(part, where_of(item), side, core)
        return remote(spot, spot, z_send.at[part, item], z_recv.at[part, item], beside)

    def c_copy(part, item, from_side):
        where = where_of(item)
        mine = item == 0 and not from_side
        which = 1 - side if from_side else side
        src = ins[part] if mine else view(part, where, which, core)
        index = 2 * item + from_side
        return remote(
            src, view(part, where, which, core), c_send.at[part, index], c_recv.at[part, index], sibling
        )

    def c_arrived(part, item, from_side):
        which = 1 - side if from_side else side
        spot = view(part, where_of(item), which, 1 - core)
        index = 2 * item + from_side
        return remote(spot, spot, c_send.at[part, index], c_recv.at[part, index], sibling)

    items = 2 * line - 1

    def goes_up(part):
        _, high = low_high(spans[part])
        return at + 1 < high

    def goes_down(part):
        low, _ = low_high(spans[part])
        return at - 1 >= low

    def active(part, item):
        return (item + 1) // 2 < spans[part]

    for part in range(total):
        pltpu.make_async_copy(
            ins[part], view(part, at, side, core), local_sem.at[part]
        ).start()

    def launch(part, item):
        @pl.when(valid(part, item))
        def _():
            if item == 0 or item % 2 == 1:
                if (item + 1) // 2 + 1 < spans[part]:
                    @pl.when(goes_up(part))
                    def _():
                        z_copy(part, item, True).start()
            if item == 0 or item % 2 == 0:
                if (item + 1) // 2 + 1 < spans[part]:
                    @pl.when(goes_down(part))
                    def _():
                        z_copy(part, item, False).start()
            b_copy(part, item).start()
            c_copy(part, item, 0).start()

    def relay(part, item):
        @pl.when(valid(part, item))
        def _():
            b_arrived(part, item).wait_recv()
            c_copy(part, item, 1).start()

    for part in range(total):
        launch(part, 0)
    for far in range(1, line + 1):
        for item in (2 * far - 1, 2 * far):
            for part in range(total):
                if far < line and active(part, item):
                    @pl.when(valid(part, item))
                    def _():
                        z_arrived(part, item).wait_recv()

                    launch(part, item)
        last = [0] if far == 1 else [2 * far - 3, 2 * far - 2]
        for item in last:
            for part in range(total):
                if active(part, item):
                    relay(part, item)
    for part in range(total):
        pltpu.make_async_copy(ins[part], view(part, at, side, core), local_sem.at[part]).wait()
        for item in range(items):
            if not active(part, item):
                continue

            @pl.when(valid(part, item))
            def _():
                if (item == 0 or item % 2 == 1) and (item + 1) // 2 + 1 < spans[part]:
                    @pl.when(goes_up(part))
                    def _():
                        z_copy(part, item, True).wait_send()
                if (item == 0 or item % 2 == 0) and (item + 1) // 2 + 1 < spans[part]:
                    @pl.when(goes_down(part))
                    def _():
                        z_copy(part, item, False).wait_send()
                b_copy(part, item).wait_send()
                c_copy(part, item, 0).wait_send()
                c_copy(part, item, 1).wait_send()
                c_arrived(part, item, 0).wait_recv()
                c_arrived(part, item, 1).wait_recv()


def spread(blocks, out_shapes, pieces, collective_id):
    count = lax.axis_size("seq")
    total = len(pieces)
    items = 2 * (count // 4) + 1
    sem = pltpu.SemaphoreType.DMA
    return pl.pallas_call(
        functools.partial(spread_kernel, (len(blocks), len(out_shapes), pieces), count),
        out_shape=out_shapes,
        in_specs=[pl.BlockSpec(memory_space=VMEM)] * len(blocks),
        out_specs=[pl.BlockSpec(memory_space=pl.ANY)] * len(out_shapes),
        scratch_shapes=[sem((total,))] + [sem((total, items))] * 4 + [sem((total, 2 * items))] * 2,
        compiler_params=pltpu.CompilerParams(collective_id=collective_id, has_side_effects=True),
    )(*blocks)


def fold_kernel(parts, count, *refs):
    given, wanted, pieces = parts
    total = len(pieces)
    spans = [piece[0] for piece in pieces]
    x_refs, o_refs = refs[:given], refs[given : given + wanted]
    scratch = refs[given + wanted :]
    outs = [piece[3](o_refs) for piece in pieces]
    c_bufs, s_bufs, b_bufs, u_bufs, d_bufs, t_bufs = (
        scratch[i * total : (i + 1) * total] for i in range(6)
    )
    c_send, c_recv, b_send, b_recv, u_send, u_recv, d_send, d_recv = scratch[6 * total :]
    line = count // 4
    group = lax.axis_index("dp")
    at, side, core = place(lax.axis_index("seq"))
    peers = line_peers(at, side, core, group, line)
    below, above, beside, sibling = (peer for _, peer in peers)
    meet(peers)

    def remote(src, dst, send, recv, peer):
        return pltpu.make_async_remote_copy(
            src_ref=src, dst_ref=dst, send_sem=send, recv_sem=recv, device_id=peer, device_id_type=MESH
        )

    def view(part, where, which_side, which_core):
        return pieces[part][2](x_refs, 4 * where + 2 * which_side + which_core)

    def valid(part, where):
        low = at // spans[part] * spans[part]
        return (where >= low) & (where < low + spans[part])

    def slot(part, where):
        return lax.rem(where, spans[part])

    order = []
    for far in range(line - 1, 0, -1):
        order += [(far, 1), (far, -1)]
    order.append((0, 1))

    def c_copy(part, where, other):
        which = 1 - side if other else side
        index = 2 * slot(part, where) + other
        return remote(
            view(part, where, which, 1 - core),
            c_bufs[part].at[index],
            c_send.at[part, index],
            c_recv.at[part, index],
            sibling,
        )

    def b_copy(part, where):
        index = slot(part, where)
        return remote(
            s_bufs[part].at[index], b_bufs[part].at[index], b_send.at[part, index], b_recv.at[part, index], beside
        )

    def u_copy(part, where):
        index = slot(part, where)
        return remote(
            t_bufs[part].at[index], u_bufs[part].at[index], u_send.at[part, index], u_recv.at[part, index], above
        )

    def d_copy(part, where):
        index = slot(part, where)
        return remote(
            t_bufs[part].at[index], d_bufs[part].at[index], d_send.at[part, index], d_recv.at[part, index], below
        )

    def each(action):
        for far, sign in order:
            for part in range(total):
                if far >= spans[part]:
                    continue
                where = at + sign * far

                @pl.when(valid(part, where))
                def _():
                    action(part, where, far, sign)

    each(lambda part, where, far, sign: c_copy(part, where, 1).start())
    each(lambda part, where, far, sign: c_copy(part, where, 0).start())

    def aside(part, where, far, sign):
        c_copy(part, where, 1).wait_recv()
        index = slot(part, where)
        mine = view(part, where, 1 - side, core)[...]
        s_bufs[part][index] = (
            mine.astype(F32) + c_bufs[part][2 * index + 1].astype(F32)
        ).astype(BF)
        b_copy(part, where).start()

    each(aside)

    def along(part, where, far, sign):
        c_copy(part, where, 0).wait_recv()
        b_copy(part, where).wait_recv()
        index = slot(part, where)
        here = slot(part, at)
        value = (
            view(part, where, side, core)[...].astype(F32)
            + c_bufs[part][2 * index].astype(F32)
            + b_bufs[part][index].astype(F32)
        )
        if far == 0:
            outs[part][...] = value

            @pl.when(here > 0)
            def _():
                u_copy(part, where).wait_recv()
                outs[part][...] += u_bufs[part][index].astype(F32)

            @pl.when(here < spans[part] - 1)
            def _():
                d_copy(part, where).wait_recv()
                outs[part][...] += d_bufs[part][index].astype(F32)
        elif sign > 0:
            t_bufs[part][index] = value.astype(BF)

            @pl.when(here > 0)
            def _():
                u_copy(part, where).wait_recv()
                t_bufs[part][index] = (value + u_bufs[part][index].astype(F32)).astype(BF)

            u_copy(part, where).start()
        else:
            t_bufs[part][index] = value.astype(BF)

            @pl.when(here < spans[part] - 1)
            def _():
                d_copy(part, where).wait_recv()
                t_bufs[part][index] = (value + d_bufs[part][index].astype(F32)).astype(BF)

            d_copy(part, where).start()

    each(along)

    def finish(part, where, far, sign):
        c_copy(part, where, 0).wait_send()
        c_copy(part, where, 1).wait_send()
        b_copy(part, where).wait_send()
        if far > 0:
            (u_copy if sign > 0 else d_copy)(part, where).wait_send()

    each(finish)


def fold(arrays, out_shapes, pieces, collective_id):
    count = lax.axis_size("seq")
    total = len(pieces)
    sem = pltpu.SemaphoreType.DMA
    line = count // 4
    bufs = []
    for times in (2, 1, 1, 1, 1, 1):
        bufs += [VMEM((times * piece[0],) + piece[1], BF) for piece in pieces]
    return pl.pallas_call(
        functools.partial(fold_kernel, (len(arrays), len(out_shapes), pieces), count),
        out_shape=[jax.ShapeDtypeStruct(shape, F32) for shape in out_shapes],
        in_specs=[pl.BlockSpec(memory_space=VMEM)] * len(arrays),
        out_specs=[pl.BlockSpec(memory_space=VMEM)] * len(out_shapes),
        scratch_shapes=bufs + [sem((total, 2 * line))] * 2 + [sem((total, line))] * 6,
        compiler_params=pltpu.CompilerParams(
            collective_id=collective_id, has_side_effects=True, vmem_limit_bytes=60 * 2**20
        ),
    )(*arrays)


def exchange_kernel(x_ref, o_ref, own_sem, z_send, z_recv, x_send, x_recv, y_send, y_recv, c_send, c_recv):
    count = o_ref.shape[1]
    line = count // 4
    group = lax.axis_index("dp")
    me = lax.axis_index("seq")
    at, side, core = place(me)
    peers = line_peers(at, side, core, group, line)
    below, above, beside, sibling = (peer for _, peer in peers)
    across = (1 - group, me)
    meet(peers + [(at >= 0, across)])

    def remote(src, dst, send, recv, index, peer):
        return pltpu.make_async_remote_copy(
            src_ref=src, dst_ref=dst, send_sem=send.at[index], recv_sem=recv.at[index],
            device_id=peer, device_id_type=MESH,
        )

    items = [(0, 0)] + [(far, turn) for far in range(1, line) for turn in range(2)]

    def where_of(item):
        return at + item[0] * (2 * item[1] - 1)

    def number(item):
        return 2 * item[0] + item[1]

    def given(item, action):
        @pl.when((where_of(item) >= 0) & (where_of(item) < line))
        def _():
            action()

    def spot(item, other_group, other_side, other_core):
        g = 1 - group if other_group else group
        s = 1 - side if other_side else side
        c = 1 - core if other_core else core
        return o_ref.at[g, 4 * where_of(item) + 2 * s + c]

    def here(item, other_group, other_side):
        if item == (0, 0) and not other_group and not other_side:
            return x_ref
        return spot(item, other_group, other_side, False)

    def z_copy(item, turn, peer):
        far = (item[0] + 1, turn)
        return remote(here(item, 0, 0), spot(item, 0, 0, 0), z_send, z_recv, number(far), peer)

    def side_copy(item, other_group, arrived):
        dst = spot(item, other_group, arrived, 0)
        src = dst if arrived else here(item, other_group, 0)
        return remote(src, dst, x_send, x_recv, 2 * number(item) + other_group, beside)

    def cross_copy(item, other_side, arrived):
        dst = spot(item, arrived, other_side, 0)
        src = dst if arrived else here(item, 0, other_side)
        return remote(src, dst, y_send, y_recv, 2 * number(item) + other_side, across)

    def core_copy(item, other_group, other_side, arrived):
        dst = spot(item, other_group, other_side, arrived)
        src = dst if arrived else here(item, other_group, other_side)
        index = 4 * number(item) + 2 * other_group + other_side
        return remote(src, dst, c_send, c_recv, index, sibling)

    def by_side(item):
        return lax.rem(where_of(item), 2) == 0

    def z_links(item, act):
        far, turn = item
        if far + 1 < line:
            if far == 0 or turn == 0:

                @pl.when(at + 1 < line)
                def _():
                    act(z_copy(item, 0, above))

            if far == 0 or turn == 1:

                @pl.when(at > 0)
                def _():
                    act(z_copy(item, 1, below))

    def start(copy):
        copy.start()

    def launch(item):
        z_links(item, start)
        side_copy(item, 0, False).start()
        cross_copy(item, 0, False).start()
        core_copy(item, 0, 0, False).start()

    def first(item):
        z = remote(spot(item, 0, 0, 0), spot(item, 0, 0, 0), z_send, z_recv, number(item), beside)
        z.wait_recv()
        launch(item)

    def second(item):
        side_copy(item, 0, True).wait_recv()

        @pl.when(jnp.logical_not(by_side(item)))
        def _():
            cross_copy(item, 1, False).start()

        core_copy(item, 0, 1, False).start()
        cross_copy(item, 0, True).wait_recv()

        @pl.when(by_side(item))
        def _():
            side_copy(item, 1, False).start()

        core_copy(item, 1, 0, False).start()

    def third(item):
        @pl.when(by_side(item))
        def _():
            side_copy(item, 1, True).wait_recv()

        @pl.when(jnp.logical_not(by_side(item)))
        def _():
            cross_copy(item, 1, True).wait_recv()

        core_copy(item, 1, 1, False).start()

    def at_far(far):
        return [item for item in items if item[0] == far]

    own = pltpu.make_async_copy(x_ref, spot((0, 0), 0, 0, 0), own_sem.at[0])
    own.start()
    launch((0, 0))
    for step in range(1, line + 2):
        for item in at_far(step):
            given(item, functools.partial(first, item))
        for item in at_far(step - 1):
            given(item, functools.partial(second, item))
        if step >= 2:
            for item in at_far(step - 2):
                given(item, functools.partial(third, item))
    own.wait()

    def finish(item):
        z_links(item, lambda copy: copy.wait_send())
        side_copy(item, 0, False).wait_send()
        cross_copy(item, 0, False).wait_send()

        @pl.when(by_side(item))
        def _():
            side_copy(item, 1, False).wait_send()

        @pl.when(jnp.logical_not(by_side(item)))
        def _():
            cross_copy(item, 1, False).wait_send()

        for other_group in range(2):
            for other_side in range(2):
                core_copy(item, other_group, other_side, False).wait_send()
                core_copy(item, other_group, other_side, True).wait_recv()

    for item in items:
        given(item, functools.partial(finish, item))


def exchange(x, collective_id):
    count = lax.axis_size("seq")
    marks = 2 * (count // 4) + 2
    sem = pltpu.SemaphoreType.DMA
    return pl.pallas_call(
        exchange_kernel,
        out_shape=jax.ShapeDtypeStruct((2, count) + x.shape, x.dtype),
        in_specs=[pl.BlockSpec(memory_space=VMEM)],
        out_specs=pl.BlockSpec(memory_space=pl.ANY),
        scratch_shapes=[sem((1,))] + [sem((marks,))] * 2 + [sem((2 * marks,))] * 4 + [sem((4 * marks,))] * 2,
        compiler_params=pltpu.CompilerParams(collective_id=collective_id, has_side_effects=True),
    )(x)


def row_gather(line, rows, cuts):
    size = rows // cuts
    return tuple(
        (
            line,
            lambda x, h=h: x[0].at[pl.ds(h * size, size)],
            lambda o, q, h=h: o[0].at[q, pl.ds(h * size, size)],
        )
        for h in range(cuts)
    )


def row_pieces(line, rows, width, cuts):
    size = rows // cuts
    return tuple(
        (
            line,
            (size, width),
            lambda x, q, h=h: x[0].at[q, pl.ds(h * size, size)],
            lambda o, h=h: o[0].at[pl.ds(h * size, size)],
        )
        for h in range(cuts)
    )


def visible_rows(kind, run_devs, rows_dev, half, q):
    first = half + rows_dev * lax.rem(q, run_devs) if kind else rows_dev * q
    return pl.multiple_of(first, 32)


def visible_gather(line, run_devs, rows_dev, half):
    size = rows_dev // 2
    return tuple(
        (
            run_devs // 4 if kind else line,
            lambda x, m=m, kind=kind, j=j: x[0].at[m, kind, pl.ds(size * j, size)],
            lambda o, q, m=m, kind=kind, j=j: o[0].at[
                m, pl.ds(visible_rows(kind, run_devs, rows_dev, half, q) + size * j, size)
            ],
        )
        for kind in range(2)
        for m in range(MB)
        for j in range(2)
    )


def visible_sum(line, run_devs, rows_dev, half, width):
    return tuple(
        (
            run_devs // 4 if kind else line,
            (MB, rows_dev, width),
            lambda x, q, kind=kind: x[0].at[
                :, pl.ds(visible_rows(kind, run_devs, rows_dev, half, q), rows_dev)
            ],
            lambda o, kind=kind: o[0].at[:, kind],
        )
        for kind in range(2)
    )


def place_kernel(l_ref, r_ref, *refs):
    refs[-1][...] = jnp.dot(l_ref[...], r_ref[...], preferred_element_type=F32).astype(BF)


def place_product(buffer, left, right, first, rows):
    depth, width = right.shape
    block = width // 2
    given = () if buffer is None else (buffer,)
    return pl.pallas_call(
        place_kernel,
        grid=(left.shape[0] // block,),
        out_shape=jax.ShapeDtypeStruct((rows, width), BF),
        in_specs=[
            pl.BlockSpec((block, depth), lambda i: (i, 0)),
            pl.BlockSpec((depth, width), lambda i: (0, 0)),
        ]
        + [pl.BlockSpec(memory_space=pl.ANY)] * len(given),
        out_specs=pl.BlockSpec((block, width), lambda i: (first // block + i, 0)),
        input_output_aliases={2: 0} if given else {},
    )(left, right, *given)


def contract(left, right, left_dim, right_dim):
    return lax.dot_general(
        left, right, (((left_dim,), (right_dim,)), ((), ())), preferred_element_type=F32
    )


def norm_forward(values, gain, bias):
    centred = values - jnp.mean(values, axis=-1, keepdims=True)
    inverse = lax.rsqrt(jnp.mean(centred * centred, axis=-1, keepdims=True) + EPS_NORM)
    unit = centred * inverse
    return (unit * gain + bias, unit, inverse)


def norm_backward(upstream, unit, inverse, gain):
    scaled = upstream * gain
    inner = (
        scaled
        - jnp.mean(scaled, axis=-1, keepdims=True)
        - unit * jnp.mean(scaled * unit, axis=-1, keepdims=True)
    )
    return (inverse * inner, jnp.sum(upstream * unit, axis=0), jnp.sum(upstream, axis=0))


def head_probs(pos_ref, q, k):
    scores = contract(q, k, 0, 0) * HD ** (-0.5)
    key_pos = lax.broadcasted_iota(jnp.int32, scores.shape, 1)
    scores = jnp.where(key_pos <= pos_ref[...], scores, MASKED)
    shifted = jnp.exp(scores - jnp.max(scores, axis=1, keepdims=True))
    return shifted * (1.0 / jnp.sum(shifted, axis=1, keepdims=True))


def attend_kernel(pos_ref, q_ref, kv_ref, o_ref):
    probs = head_probs(pos_ref, q_ref[...], kv_ref[0]).astype(BF)
    o_ref[...] = contract(kv_ref[1], probs, 1, 1).astype(BF)


def attend_back_kernel(pos_ref, q_ref, kv_ref, g_ref, dq_ref, dkv_ref):
    q, k, v, g = q_ref[...], kv_ref[0], kv_ref[1], g_ref[...]
    probs = head_probs(pos_ref, q, k)
    grad = contract(g, v, 0, 0)
    back = (probs * (grad - jnp.sum(probs * grad, axis=1, keepdims=True))).astype(BF)
    scale = HD ** (-0.5)
    dq_ref[...] = (contract(k, back, 1, 1) * scale).astype(BF)
    dkv_ref[0] = (contract(q, back, 1, 0) * scale).astype(BF)
    dkv_ref[1] = contract(g, probs.astype(BF), 1, 0).astype(BF)


def attend(query_pos, q, kv):
    rows, keys = query_pos.shape[0], kv.shape[2] * query_pos.shape[0] // q.shape[1]
    small = pl.BlockSpec((HD, rows), lambda m, h: (h, m))
    large = pl.BlockSpec((2, HD, keys), lambda m, h: (0, h, m))
    return pl.pallas_call(
        attend_kernel,
        grid=(q.shape[1] // rows, HEADS),
        out_shape=jax.ShapeDtypeStruct(q.shape, BF),
        in_specs=[pl.BlockSpec((rows, 1), lambda m, h: (0, 0)), small, large],
        out_specs=small,
    )(query_pos, q, kv)


def attend_back(query_pos, q, kv, grad_out):
    rows, keys = query_pos.shape[0], kv.shape[2] * query_pos.shape[0] // q.shape[1]
    small = pl.BlockSpec((HD, rows), lambda m, h: (h, m))
    large = pl.BlockSpec((2, HD, keys), lambda m, h: (0, h, m))
    return pl.pallas_call(
        attend_back_kernel,
        grid=(q.shape[1] // rows, HEADS),
        out_shape=[jax.ShapeDtypeStruct(q.shape, BF), jax.ShapeDtypeStruct(kv.shape, BF)],
        in_specs=[pl.BlockSpec((rows, 1), lambda m, h: (0, 0)), small, large, small],
        out_specs=[small, large],
    )(query_pos, q, kv, grad_out)


def lookup_kernel(first_ref, slot_ref, table_ref, *refs):
    slots = slot_ref[...] - first_ref[0]
    ids = lax.broadcasted_iota(jnp.int32, (slots.shape[0], table_ref.shape[1]), 1)
    rows = contract(jnp.where(slots == ids, 1.0, 0.0).astype(BF), table_ref[...], 1, 1).astype(BF)
    refs[-1][...] = rows if len(refs) == 1 else refs[0][...] + rows


def lookup(first, slots, table, others, block):
    width, held = table.shape
    rows = pl.BlockSpec((block, width), lambda i: (i, 0))
    given = () if others is None else (others,)
    return pl.pallas_call(
        lookup_kernel,
        grid=(slots.shape[0] // block,),
        out_shape=jax.ShapeDtypeStruct((slots.shape[0], width), BF),
        in_specs=[
            pl.BlockSpec(memory_space=pltpu.SMEM),
            pl.BlockSpec((block, 1), lambda i: (i, 0)),
            pl.BlockSpec((width, held), lambda i: (0, 0)),
        ]
        + [rows] * len(given),
        out_specs=rows,
    )(first, slots, table, *given)


def own_columns(early, late, rank, count):
    size = early.shape[0]
    pieces = []
    for turn in range(3):
        units = [(3 * owner + turn, owner) for owner in range(count)]
        from_early = lax.ppermute(
            early, ("dp", "seq"), [(unit, owner) for unit, owner in units if unit < count]
        )
        first = lax.rem(2 * rank + 3 * count + count - turn, 3) == 0
        from_late = lax.ppermute(
            jnp.where(first, late[:size], late[size:]),
            ("dp", "seq"),
            [((unit - count) // 2, owner) for unit, owner in units if unit >= count],
        )
        pieces.append(jnp.where(3 * rank + turn < count, from_early, from_late))
    return jnp.concatenate(pieces)


def adamw(weight, moment_a, moment_b, gradient, rate, decay):
    moment_a = MOMENT_ONE * moment_a + (1.0 - MOMENT_ONE) * gradient
    moment_b = MOMENT_TWO * moment_b + (1.0 - MOMENT_TWO) * gradient * gradient
    update = (
        moment_a
        / (1.0 - MOMENT_ONE**STEP)
        / (jnp.sqrt(moment_b / (1.0 - MOMENT_TWO**STEP)) + EPS_ADAM)
    )
    weight = weight - rate * (update + decay * weight)
    return (weight, moment_a, moment_b, weight.astype(BF))


def on_device(
    tokens,
    targets,
    counted,
    cont_label,
    pair_map,
    ref_logp,
    vocab_slot,
    embed_table,
    embed_first,
    embed_second,
    layer_weights,
    layer_first,
    layer_second,
    norm_params,
    norm_first,
    norm_second,
):
    seq_count = lax.axis_size("seq")
    group_count = lax.axis_size("dp")
    all_count = seq_count * group_count
    seq_rank = lax.axis_index("seq")
    group_rank = lax.axis_index("dp")
    device_rank = group_rank * seq_count + seq_rank
    rows_dev = tokens.shape[3]
    half = rows_dev * seq_count
    vocab_dev, width = embed_table.shape
    run_count = half // CLEN
    run_devs = CLEN // rows_dev
    own_rows = MB * 2 * rows_dev

    table_t = embed_table.T
    norm_dev = norm_params.shape[0]
    norm_parts = [norm_params]
    for step in range(1, group_count):
        norm_parts.append(
            lax.ppermute(
                norm_params, "dp", [(i, (i - step) % group_count) for i in range(group_count)]
            )
        )
    sent, *norm_parts = lax.optimization_barrier((table_t.astype(BF), *norm_parts))
    norm_all = jnp.zeros((group_count, norm_dev), F32)
    for step in range(group_count):
        norm_all = lax.dynamic_update_index_in_dim(
            norm_all, norm_parts[step], lax.rem(group_rank + step, group_count), 0
        )
    slab_t = [sent]
    for step in range(1, group_count):
        slab_t.append(
            lax.ppermute(
                slab_t[0], "dp", [(i, (i - step) % group_count) for i in range(group_count)]
            )
        )
    weights = lax.all_gather(
        layer_weights.T.astype(BF)[None], ("dp", "seq"), axis=0, tiled=True
    ).reshape(-1, width)
    w_q = weights[:width]
    w_o = weights[3 * width : 4 * width]
    w_kv = weights[width : 3 * width]
    w_up = weights[4 * width : 4 * width + FF]
    w_dn = weights[4 * width + FF :]

    marks = counted[:, 0]
    spots = jnp.arange(rows_dev, dtype=jnp.int32)
    ranks = (
        jnp.sum(jnp.where(spots[None, :, None] <= spots[None, None, :], marks[:, :, None], 0), axis=1)
        - 1
    )
    pick_ids = jnp.arange(PICK, dtype=jnp.int32)
    pick_hit = (ranks[:, None, :] == pick_ids[None, :, None]) & (marks[:, None, :] == 1)
    pick_targets = jnp.sum(jnp.where(pick_hit, targets[:, 0][:, None, :], 0), axis=2)
    pick_low = pick_hit.astype(BF)
    slots = vocab_slot[jnp.concatenate([tokens[:, 0].reshape(-1), pick_targets.reshape(-1)])]
    small = jnp.concatenate([slots.astype(F32), norm_all.reshape(-1)])
    small = jnp.pad(small, (0, -small.shape[0] % 1024)).reshape(-1, 128)
    small_all = direct_gather(small, False, 1).reshape(seq_count, -1)
    slots_all = small_all[:, : own_rows + MB * PICK].astype(jnp.int32)
    gains = (
        small_all[:, own_rows + MB * PICK :][:, : group_count * norm_dev]
        .reshape(seq_count, group_count, norm_dev)
        .transpose(1, 0, 2)
        .astype(BF)
        .astype(F32)
        .reshape(6, width)
    )
    row_slots = slots_all[:, :own_rows].reshape(-1)
    target_slots = slots_all[:, own_rows:].reshape(-1)
    vocab_ids = jnp.arange(vocab_dev, dtype=jnp.int32)

    def hits(slot_ids, step):
        part = lax.rem(group_rank + step, group_count)
        first = (part * seq_count + seq_rank) * vocab_dev
        return (slot_ids - first)[:, None] == vocab_ids[None, :]

    partial = None
    for step in range(group_count):
        part = lax.rem(group_rank + step, group_count)
        first = (part * seq_count + seq_rank) * vocab_dev
        partial = lookup(first[None], row_slots[:, None], slab_t[step], partial, own_rows)
    line = seq_count // 4
    (stream,) = fold(
        [partial.reshape(seq_count, own_rows, width)],
        [(own_rows, width)],
        row_pieces(line, own_rows, width, 2),
        2,
    )

    normed, unit_one, inverse_one = norm_forward(stream, gains[0], gains[3])
    hidden_one = normed.astype(BF)
    run_dev = seq_rank // run_devs * run_devs
    key_rows = half + CLEN
    (hidden_sel,) = spread(
        [hidden_one.reshape(MB, 2, rows_dev, width)],
        [jax.ShapeDtypeStruct((MB, key_rows, width), BF)],
        visible_gather(line, run_devs, rows_dev, half),
        3,
    )
    hidden_sel = hidden_sel.reshape(MB * key_rows, width)
    pairs = contract(w_kv, hidden_sel, 1, 1).astype(BF).reshape(2, width, MB * key_rows)
    queries = contract(w_q, hidden_one, 1, 1).astype(BF)
    start = seq_rank * rows_dev
    query_pos = jnp.concatenate([start + spots, half + (start - run_dev * rows_dev) + spots])[:, None]
    attended = attend(query_pos, queries, pairs)
    stream_one = stream + contract(attended, w_o, 0, 0)
    normed, unit_two, inverse_two = norm_forward(stream_one, gains[1], gains[4])
    hidden_two = normed.astype(BF)
    up_proj = contract(w_up, hidden_two, 1, 1)
    activated = jax.nn.gelu(up_proj, approximate=False).astype(BF)
    stream_two = stream_one + contract(activated, w_dn, 0, 0)
    normed, unit_final, inverse_final = norm_forward(stream_two, gains[2], gains[5])
    final = normed.astype(BF).reshape(MB, 2, rows_dev, width)[:, 1]
    picked = jnp.einsum("mpr,mrd->mpd", pick_low, final, preferred_element_type=F32).astype(BF)

    (head_rows,) = spread(
        [picked.reshape(MB * PICK, width)],
        [jax.ShapeDtypeStruct((seq_count, MB * PICK, width), BF)],
        row_gather(line, MB * PICK, 1),
        4,
    )
    head_rows = head_rows.reshape(seq_count * MB * PICK, width)
    logits = [contract(head_rows, slab_t[part], 1, 0) for part in range(group_count)]
    target_hits = [hits(target_slots, part) for part in range(group_count)]
    highest = jnp.max(logits[0], axis=1)
    for part in range(1, group_count):
        highest = jnp.maximum(highest, jnp.max(logits[part], axis=1))
    summed = jnp.zeros_like(highest)
    target_logit = jnp.zeros_like(highest)
    for part in range(group_count):
        summed = summed + jnp.sum(jnp.exp(logits[part] - highest[:, None]), axis=1)
        target_logit = target_logit + jnp.sum(jnp.where(target_hits[part], logits[part], 0.0), axis=1)
    stats = direct_gather(
        jnp.stack([highest, summed, target_logit]).reshape(-1, 128), False, 5
    ).reshape(seq_count, 3, -1)
    overall = jnp.max(stats[:, 0], axis=0)
    total = jnp.sum(stats[:, 1] * jnp.exp(stats[:, 0] - overall[None]), axis=0)
    log_total = overall + jnp.log(total)
    token_lp = jnp.sum(stats[:, 2], axis=0) - log_total

    run_ids = jnp.arange(run_count, dtype=jnp.int32)
    run_of_dev = jnp.arange(seq_count, dtype=jnp.int32) * rows_dev // CLEN
    run_match = run_of_dev[:, None] == run_ids[None, :]
    dev_lp = jnp.sum(token_lp.reshape(seq_count, MB, PICK), axis=2)
    run_lp = jnp.sum(jnp.where(run_match[:, None, :], dev_lp[:, :, None], 0.0), axis=0)
    labels = lax.dynamic_index_in_dim(cont_label, group_rank, 1, keepdims=False)
    pairing = lax.dynamic_index_in_dim(pair_map, group_rank, 1, keepdims=False)
    reference_lp = lax.dynamic_index_in_dim(ref_logp, group_rank, 1, keepdims=False)
    label_match = labels[:, :, None] == run_ids[None, None, :]
    label_lp = jnp.sum(jnp.where(label_match, run_lp[:, :, None], 0.0), axis=1)
    margin = label_lp - reference_lp
    chosen = pairing[:, 0::2, None] == run_ids[None, None, :]
    rejected = pairing[:, 1::2, None] == run_ids[None, None, :]
    delta = jnp.sum(jnp.where(chosen, margin[:, None, :], 0.0), axis=2) - jnp.sum(
        jnp.where(rejected, margin[:, None, :], 0.0), axis=2
    )
    loss = jnp.sum(jax.nn.softplus(-DPO_BETA * delta))
    pair_grad = -DPO_BETA * jax.nn.sigmoid(-DPO_BETA * delta)
    label_grad = jnp.sum(
        jnp.where(chosen, pair_grad[:, :, None], 0.0)
        - jnp.where(rejected, pair_grad[:, :, None], 0.0),
        axis=1,
    )
    run_grad = jnp.sum(jnp.where(label_match, label_grad[:, None, :], 0.0), axis=2)
    dev_grad = jnp.sum(jnp.where(run_match[:, None, :], run_grad[None], 0.0), axis=2)
    row_grad = jnp.broadcast_to(dev_grad[:, :, None], (seq_count, MB, PICK)).reshape(-1)

    head_back = 0.0
    logit_grads = []
    for part in range(group_count):
        logit_grad = (
            row_grad[:, None]
            * (target_hits[part].astype(F32) - jnp.exp(logits[part] - log_total[:, None]))
        ).astype(BF)
        logit_grads.append(logit_grad)
        head_back = head_back + contract(logit_grad, slab_t[part], 1, 1)
    head_back = head_back.astype(BF)
    moved = [(i, (i + 1) % group_count) for i in range(group_count)]
    if group_count == 2:
        head_back, head_part = lax.optimization_barrier(
            (head_back, contract(head_rows, logit_grads[1], 0, 0).astype(BF))
        )
        head_other = lax.ppermute(head_part, "dp", moved)
    (row_back,) = fold(
        [head_back.reshape(seq_count, MB * PICK, width)],
        [(MB * PICK, width)],
        row_pieces(line, MB * PICK, width, 1),
        6,
    )
    row_back = row_back.astype(BF).reshape(MB, PICK, width)
    cont_back = jnp.einsum("mpr,mpd->mrd", pick_low, row_back, preferred_element_type=F32)
    upstream = jnp.concatenate(
        [jnp.zeros((MB, 1, rows_dev, width), F32), cont_back[:, None]], axis=1
    ).reshape(own_rows, width)

    grad_two, gain_final, bias_final = norm_backward(upstream, unit_final, inverse_final, gains[2])
    grad_ffn = grad_two.astype(BF)
    weight_late = place_product(None, activated, grad_ffn, FF, 2 * FF)
    grad_act = contract(w_dn, grad_ffn, 1, 1)
    _, gelu_pull = jax.vjp(lambda pre_act: jax.nn.gelu(pre_act, approximate=False), up_proj)
    grad_up = gelu_pull(grad_act)[0].astype(BF)
    weight_late = place_product(weight_late, grad_up, hidden_two, 0, 2 * FF)
    grad_hidden = contract(grad_up, w_up, 0, 0)
    grad_mid, gain_two, bias_two = norm_backward(grad_hidden, unit_two, inverse_two, gains[1])
    grad_one = grad_two + grad_mid
    grad_branch = grad_one.astype(BF)
    grad_attended = contract(w_o, grad_branch, 1, 1).astype(BF)
    weight_late, grad_attended = lax.optimization_barrier((weight_late, grad_attended))
    late_sum = lax.psum_scatter(
        weight_late.reshape(all_count, -1, width), ("dp", "seq"), scatter_dimension=0, tiled=True
    )[0]
    grad_query, grad_pairs = attend_back(query_pos, queries, pairs, grad_attended)
    if group_count == 2:
        grad_query, head_other = lax.optimization_barrier((grad_query, head_other))
    grad_pairs = grad_pairs.reshape(2 * width, MB * key_rows)
    weight_early = place_product(None, attended, grad_branch, 3 * width, 4 * width)
    weight_early = place_product(weight_early, grad_query, hidden_one, 0, 4 * width)
    weight_early = place_product(weight_early, grad_pairs, hidden_sel, width, 4 * width)
    low_sel = contract(grad_pairs, w_kv, 0, 0).astype(BF).reshape(MB, key_rows, width)
    low_sel, late_sum, weight_early = lax.optimization_barrier((low_sel, late_sum, weight_early))
    early_sum = lax.psum_scatter(
        weight_early.reshape(all_count, -1, width), ("dp", "seq"), scatter_dimension=0, tiled=True
    )[0]
    weight_sum = own_columns(early_sum, late_sum, device_rank, all_count).astype(F32)
    (low_own,) = fold(
        [low_sel],
        [(MB, 2, rows_dev, width)],
        visible_sum(line, run_devs, rows_dev, half, width),
        7,
    )
    grad_low = low_own.reshape(own_rows, width) + contract(grad_query, w_q, 0, 0)
    grad_first, gain_one, bias_one = norm_backward(grad_low, unit_one, inverse_one, gains[0])
    norm_rows = jnp.stack([gain_one, gain_two, gain_final, bias_one, bias_two, bias_final])
    if group_count == 2:
        head_own = contract(head_rows, logit_grads[0], 0, 0)
        pad_rows = 8
        all_rows = exchange(
            jnp.concatenate(
                [grad_one + grad_first, norm_rows, jnp.zeros((pad_rows - 6, width), F32)]
            ).astype(BF),
            8,
        )
        other_slots = lax.ppermute(row_slots, "dp", moved)
        embed_sum = lax.optimization_barrier(head_own + head_other.astype(F32))
        for part in range(group_count):
            part_slots = jnp.where(group_rank == part, row_slots, other_slots)
            part_slots = jnp.pad(
                part_slots.reshape(seq_count, own_rows), ((0, 0), (0, pad_rows)), constant_values=-1
            ).reshape(-1)
            embed_sum = embed_sum + contract(
                all_rows[part].reshape(-1, width), hits(part_slots, 0).astype(BF), 0, 0
            )
        norm_all = jnp.sum(
            all_rows.reshape(all_count, own_rows + pad_rows, width)[
                :, own_rows : own_rows + 6
            ].astype(F32),
            axis=0,
        )
    else:
        row_grads, norm_grads = spread(
            [
                (grad_one + grad_first).astype(BF),
                jnp.concatenate([norm_rows, jnp.zeros((10, width), F32)]).astype(BF),
            ],
            [
                jax.ShapeDtypeStruct((seq_count, own_rows, width), BF),
                jax.ShapeDtypeStruct((seq_count, 16, width), BF),
            ],
            row_gather(line, own_rows, 2)
            + ((line, lambda x: x[1], lambda o, q: o[1].at[q]),),
            8,
        )
        row_grads = row_grads.reshape(-1, width)
        norm_sum = jnp.sum(norm_grads[:, :6].astype(F32), axis=0)
        norm_all = norm_sum
        for step in range(1, group_count):
            norm_all = norm_all + lax.ppermute(
                norm_sum, "dp", [(i, (i + step) % group_count) for i in range(group_count)]
            )

        def table_grad(step):
            return contract(head_rows, logit_grads[step], 0, 0) + contract(
                row_grads, hits(row_slots, step).astype(BF), 0, 0
            )

        arrived = [
            lax.ppermute(
                table_grad(step).astype(BF),
                "dp",
                [(i, (i + step) % group_count) for i in range(group_count)],
            )
            for step in range(1, group_count)
        ]
        embed_sum = table_grad(0)
        for block in arrived:
            embed_sum = embed_sum + block.astype(F32)
    norm_own = lax.dynamic_slice_in_dim(norm_all.reshape(-1), device_rank * norm_dev, norm_dev, 0)
    squares = (
        jnp.sum(embed_sum * embed_sum)
        + jnp.sum(jnp.square(early_sum.astype(F32)))
        + jnp.sum(jnp.square(late_sum.astype(F32)))
        + jnp.sum(norm_own * norm_own)
    )
    lanes = lax.broadcasted_iota(jnp.int32, (8, 128), 1)
    scalars = direct_gather(
        jnp.where(lanes == 0, squares, jnp.where(lanes == 1, loss, 0.0)), True, 9
    )
    square_total = jnp.sum(scalars[:, 0, 0])
    loss_total = jnp.sum(scalars[::seq_count, 0, 1])
    grad_norm = jnp.sqrt(square_total)
    factor = jnp.minimum(1.0, CLIP_NORM / grad_norm)
    embed_out = adamw(
        table_t, embed_first.T, embed_second.T, embed_sum * factor, LEARN_RATE, WEIGHT_DECAY
    )
    layer_out = adamw(
        layer_weights.T,
        layer_first.T,
        layer_second.T,
        weight_sum * factor,
        LEARN_RATE,
        WEIGHT_DECAY,
    )
    norm_out = adamw(norm_params, norm_first, norm_second, norm_own * factor, NORM_RATE, 0.0)
    return (
        embed_out[0].T,
        embed_out[1].T,
        embed_out[2].T,
        embed_out[3].T,
        layer_out[0].T,
        layer_out[1].T,
        layer_out[2].T,
        layer_out[3].T,
        norm_out[0],
        norm_out[1],
        norm_out[2],
        norm_out[3],
        grad_norm,
        loss_total,
    )


def solution(mesh):
    return jax.shard_map(
        on_device,
        mesh=mesh,
        in_specs=(
            P(None, "dp", None, "seq"),
            P(None, "dp", "seq"),
            P(None, "dp", "seq"),
            P(),
            P(),
            P(),
            P(),
            P(("dp", "seq"), None),
            P(("dp", "seq"), None),
            P(("dp", "seq"), None),
            P(None, ("dp", "seq")),
            P(None, ("dp", "seq")),
            P(None, ("dp", "seq")),
            P(("dp", "seq")),
            P(("dp", "seq")),
            P(("dp", "seq")),
        ),
        out_specs=(
            P(("dp", "seq"), None),
            P(("dp", "seq"), None),
            P(("dp", "seq"), None),
            P(("dp", "seq"), None),
            P(None, ("dp", "seq")),
            P(None, ("dp", "seq")),
            P(None, ("dp", "seq")),
            P(None, ("dp", "seq")),
            P(("dp", "seq")),
            P(("dp", "seq")),
            P(("dp", "seq")),
            P(("dp", "seq")),
            P(),
            P(),
        ),
        check_vma=False,
    )
```

```python
import functools

import jax
import jax.numpy as jnp
from jax import lax
from jax.experimental import pallas as pl
from jax.experimental.pallas import tpu as pltpu
from jax.sharding import PartitionSpec as P


HEADS = 17
HD = 64
FF = 4352
PICK = 32
CLEN = 512
MB = 2
STEP = 10


EPS_NORM = 1e-05
DPO_BETA = 0.05
CLIP_NORM = 1.0
LEARN_RATE = 0.03
NORM_RATE = 0.4
WEIGHT_DECAY = 0.1
MOMENT_ONE = 0.9
MOMENT_TWO = 0.999
EPS_ADAM = 1e-08
MASKED = -1e30
BF = jnp.bfloat16
F32 = jnp.float32
MESH = pl.DeviceIdType.MESH
VMEM = pltpu.VMEM


def meet(peers):
    barrier = pltpu.get_barrier_semaphore()
    for there, peer in peers:

        @pl.when(there)
        def _():
            pl.semaphore_signal(barrier, inc=1, device_id=peer, device_id_type=MESH)

    pl.semaphore_wait(barrier, sum(jnp.where(there, 1, 0) for there, _ in peers))


def direct_kernel(whole, x_ref, o_ref, send_sem, recv_sem):
    seq_count = lax.axis_size("seq")
    group_rank = lax.axis_index("dp")
    me = lax.axis_index("seq")
    count = o_ref.shape[0]
    if whole:
        me = group_rank * seq_count + me

    def peer(step):
        other = lax.rem(me + step, count)
        if whole:
            return (other // seq_count, lax.rem(other, seq_count))
        return (group_rank, other)

    barrier = pltpu.get_barrier_semaphore()

    def greet(step, carry):
        pl.semaphore_signal(barrier, inc=1, device_id=peer(step), device_id_type=MESH)
        return carry

    lax.fori_loop(1, count, greet, 0)
    o_ref[me] = x_ref[...]
    pl.semaphore_wait(barrier, count - 1)

    def copy(step):
        return pltpu.make_async_remote_copy(
            src_ref=x_ref,
            dst_ref=o_ref.at[me],
            send_sem=send_sem.at[step],
            recv_sem=recv_sem.at[step],
            device_id=peer(step),
            device_id_type=MESH,
        )

    def begin(step, carry):
        copy(step).start()
        return carry

    def finish(step, carry):
        copy(step).wait()
        return carry

    lax.fori_loop(1, count, begin, 0)
    lax.fori_loop(1, count, finish, 0)


def direct_gather(x, whole, collective_id):
    count = lax.axis_size("seq") * (lax.axis_size("dp") if whole else 1)
    return pl.pallas_call(
        functools.partial(direct_kernel, whole),
        out_shape=jax.ShapeDtypeStruct((count,) + x.shape, x.dtype),
        in_specs=[pl.BlockSpec(memory_space=VMEM)],
        out_specs=pl.BlockSpec(memory_space=VMEM),
        scratch_shapes=[pltpu.SemaphoreType.DMA((count,)), pltpu.SemaphoreType.DMA((count,))],
        compiler_params=pltpu.CompilerParams(collective_id=collective_id, has_side_effects=True),
    )(x)


def place(rank):
    return (rank // 4, lax.rem(rank, 4) // 2, lax.rem(rank, 2))


def line_peers(at, side, core, group, line):
    return [
        (at > 0, (group, 4 * (at - 1) + 2 * side + core)),
        (at < line - 1, (group, 4 * (at + 1) + 2 * side + core)),
        (at >= 0, (group, 4 * at + 2 * (1 - side) + core)),
        (at >= 0, (group, 4 * at + 2 * side + 1 - core)),
    ]


def spread_kernel(parts, count, *refs):
    given, wanted, pieces = parts
    total = len(pieces)
    x_refs, o_refs = refs[:given], refs[given : given + wanted]
    local_sem, z_send, z_recv, b_send, b_recv, c_send, c_recv = refs[given + wanted :]
    spans = [piece[0] for piece in pieces]
    ins = [piece[1](x_refs) for piece in pieces]
    line = count // 4
    group = lax.axis_index("dp")
    at, side, core = place(lax.axis_index("seq"))
    peers = line_peers(at, side, core, group, line)
    below, above, beside, sibling = (peer for _, peer in peers)
    meet(peers)

    def seq_of(where, which_side, which_core):
        return 4 * where + 2 * which_side + which_core

    def remote(src, dst, send, recv, peer):
        return pltpu.make_async_remote_copy(
            src_ref=src, dst_ref=dst, send_sem=send, recv_sem=recv, device_id=peer, device_id_type=MESH
        )

    def low_high(span):
        low = at // span * span
        return low, low + span

    def view(part, where, which_side, which_core):
        return pieces[part][2](o_refs, seq_of(where, which_side, which_core))

    def where_of(item):
        far = (item + 1) // 2
        return at - far if item % 2 else at + far

    def valid(part, item):
        low, high = low_high(spans[part])
        where = where_of(item)
        return (where >= low) & (where < high)

    def z_copy(part, item, up):
        where = where_of(item)
        far = (item + 1) // 2 + 1
        mark = 2 * far - 1 if up else 2 * far
        src = ins[part] if item == 0 else view(part, where, side, core)
        return remote(
            src,
            view(part, where, side, core),
            z_send.at[part, mark],
            z_recv.at[part, mark],
            above if up else below,
        )

    def b_copy(part, item):
        where = where_of(item)
        src = ins[part] if item == 0 else view(part, where, side, core)
        return remote(
            src, view(part, where, side, core), b_send.at[part, item], b_recv.at[part, item], beside
        )

    def b_arrived(part, item):
        where = where_of(item)
        spot = view(part, where, 1 - side, core)
        return remote(spot, spot, b_send.at[part, item], b_recv.at[part, item], beside)

    def z_arrived(part, item):
        spot = view(part, where_of(item), side, core)
        return remote(spot, spot, z_send.at[part, item], z_recv.at[part, item], beside)

    def c_copy(part, item, from_side):
        where = where_of(item)
        mine = item == 0 and not from_side
        which = 1 - side if from_side else side
        src = ins[part] if mine else view(part, where, which, core)
        index = 2 * item + from_side
        return remote(
            src, view(part, where, which, core), c_send.at[part, index], c_recv.at[part, index], sibling
        )

    def c_arrived(part, item, from_side):
        which = 1 - side if from_side else side
        spot = view(part, where_of(item), which, 1 - core)
        index = 2 * item + from_side
        return remote(spot, spot, c_send.at[part, index], c_recv.at[part, index], sibling)

    items = 2 * line - 1

    def goes_up(part):
        _, high = low_high(spans[part])
        return at + 1 < high

    def goes_down(part):
        low, _ = low_high(spans[part])
        return at - 1 >= low

    def active(part, item):
        return (item + 1) // 2 < spans[part]

    for part in range(total):
        pltpu.make_async_copy(
            ins[part], view(part, at, side, core), local_sem.at[part]
        ).start()

    def launch(part, item):
        @pl.when(valid(part, item))
        def _():
            if item == 0 or item % 2 == 1:
                if (item + 1) // 2 + 1 < spans[part]:
                    @pl.when(goes_up(part))
                    def _():
                        z_copy(part, item, True).start()
            if item == 0 or item % 2 == 0:
                if (item + 1) // 2 + 1 < spans[part]:
                    @pl.when(goes_down(part))
                    def _():
                        z_copy(part, item, False).start()
            b_copy(part, item).start()
            c_copy(part, item, 0).start()

    def relay(part, item):
        @pl.when(valid(part, item))
        def _():
            b_arrived(part, item).wait_recv()
            c_copy(part, item, 1).start()

    for part in range(total):
        launch(part, 0)
    for far in range(1, line + 1):
        for item in (2 * far - 1, 2 * far):
            for part in range(total):
                if far < line and active(part, item):
                    @pl.when(valid(part, item))
                    def _():
                        z_arrived(part, item).wait_recv()

                    launch(part, item)
        last = [0] if far == 1 else [2 * far - 3, 2 * far - 2]
        for item in last:
            for part in range(total):
                if active(part, item):
                    relay(part, item)
    for part in range(total):
        pltpu.make_async_copy(ins[part], view(part, at, side, core), local_sem.at[part]).wait()
        for item in range(items):
            if not active(part, item):
                continue

            @pl.when(valid(part, item))
            def _():
                if (item == 0 or item % 2 == 1) and (item + 1) // 2 + 1 < spans[part]:
                    @pl.when(goes_up(part))
                    def _():
                        z_copy(part, item, True).wait_send()
                if (item == 0 or item % 2 == 0) and (item + 1) // 2 + 1 < spans[part]:
                    @pl.when(goes_down(part))
                    def _():
                        z_copy(part, item, False).wait_send()
                b_copy(part, item).wait_send()
                c_copy(part, item, 0).wait_send()
                c_copy(part, item, 1).wait_send()
                c_arrived(part, item, 0).wait_recv()
                c_arrived(part, item, 1).wait_recv()


def spread(blocks, out_shapes, pieces, collective_id):
    count = lax.axis_size("seq")
    total = len(pieces)
    items = 2 * (count // 4) + 1
    sem = pltpu.SemaphoreType.DMA
    return pl.pallas_call(
        functools.partial(spread_kernel, (len(blocks), len(out_shapes), pieces), count),
        out_shape=out_shapes,
        in_specs=[pl.BlockSpec(memory_space=VMEM)] * len(blocks),
        out_specs=[pl.BlockSpec(memory_space=pl.ANY)] * len(out_shapes),
        scratch_shapes=[sem((total,))] + [sem((total, items))] * 4 + [sem((total, 2 * items))] * 2,
        compiler_params=pltpu.CompilerParams(collective_id=collective_id, has_side_effects=True),
    )(*blocks)


def fold_kernel(parts, count, *refs):
    given, wanted, pieces = parts
    total = len(pieces)
    spans = [piece[0] for piece in pieces]
    x_refs, o_refs = refs[:given], refs[given : given + wanted]
    scratch = refs[given + wanted :]
    outs = [piece[3](o_refs) for piece in pieces]
    c_bufs, s_bufs, b_bufs, u_bufs, d_bufs, t_bufs = (
        scratch[i * total : (i + 1) * total] for i in range(6)
    )
    c_send, c_recv, b_send, b_recv, u_send, u_recv, d_send, d_recv = scratch[6 * total :]
    line = count // 4
    group = lax.axis_index("dp")
    at, side, core = place(lax.axis_index("seq"))
    peers = line_peers(at, side, core, group, line)
    below, above, beside, sibling = (peer for _, peer in peers)
    meet(peers)

    def remote(src, dst, send, recv, peer):
        return pltpu.make_async_remote_copy(
            src_ref=src, dst_ref=dst, send_sem=send, recv_sem=recv, device_id=peer, device_id_type=MESH
        )

    def view(part, where, which_side, which_core):
        return pieces[part][2](x_refs, 4 * where + 2 * which_side + which_core)

    def valid(part, where):
        low = at // spans[part] * spans[part]
        return (where >= low) & (where < low + spans[part])

    def slot(part, where):
        return lax.rem(where, spans[part])

    order = []
    for far in range(line - 1, 0, -1):
        order += [(far, 1), (far, -1)]
    order.append((0, 1))

    def c_copy(part, where, other):
        which = 1 - side if other else side
        index = 2 * slot(part, where) + other
        return remote(
            view(part, where, which, 1 - core),
            c_bufs[part].at[index],
            c_send.at[part, index],
            c_recv.at[part, index],
            sibling,
        )

    def b_copy(part, where):
        index = slot(part, where)
        return remote(
            s_bufs[part].at[index], b_bufs[part].at[index], b_send.at[part, index], b_recv.at[part, index], beside
        )

    def u_copy(part, where):
        index = slot(part, where)
        return remote(
            t_bufs[part].at[index], u_bufs[part].at[index], u_send.at[part, index], u_recv.at[part, index], above
        )

    def d_copy(part, where):
        index = slot(part, where)
        return remote(
            t_bufs[part].at[index], d_bufs[part].at[index], d_send.at[part, index], d_recv.at[part, index], below
        )

    def each(action):
        for far, sign in order:
            for part in range(total):
                if far >= spans[part]:
                    continue
                where = at + sign * far

                @pl.when(valid(part, where))
                def _():
                    action(part, where, far, sign)

    each(lambda part, where, far, sign: c_copy(part, where, 1).start())
    each(lambda part, where, far, sign: c_copy(part, where, 0).start())

    def aside(part, where, far, sign):
        c_copy(part, where, 1).wait_recv()
        index = slot(part, where)
        mine = view(part, where, 1 - side, core)[...]
        s_bufs[part][index] = (
            mine.astype(F32) + c_bufs[part][2 * index + 1].astype(F32)
        ).astype(BF)
        b_copy(part, where).start()

    each(aside)

    def along(part, where, far, sign):
        c_copy(part, where, 0).wait_recv()
        b_copy(part, where).wait_recv()
        index = slot(part, where)
        here = slot(part, at)
        value = (
            view(part, where, side, core)[...].astype(F32)
            + c_bufs[part][2 * index].astype(F32)
            + b_bufs[part][index].astype(F32)
        )
        if far == 0:
            outs[part][...] = value

            @pl.when(here > 0)
            def _():
                u_copy(part, where).wait_recv()
                outs[part][...] += u_bufs[part][index].astype(F32)

            @pl.when(here < spans[part] - 1)
            def _():
                d_copy(part, where).wait_recv()
                outs[part][...] += d_bufs[part][index].astype(F32)
        elif sign > 0:
            t_bufs[part][index] = value.astype(BF)

            @pl.when(here > 0)
            def _():
                u_copy(part, where).wait_recv()
                t_bufs[part][index] = (value + u_bufs[part][index].astype(F32)).astype(BF)

            u_copy(part, where).start()
        else:
            t_bufs[part][index] = value.astype(BF)

            @pl.when(here < spans[part] - 1)
            def _():
                d_copy(part, where).wait_recv()
                t_bufs[part][index] = (value + d_bufs[part][index].astype(F32)).astype(BF)

            d_copy(part, where).start()

    each(along)

    def finish(part, where, far, sign):
        c_copy(part, where, 0).wait_send()
        c_copy(part, where, 1).wait_send()
        b_copy(part, where).wait_send()
        if far > 0:
            (u_copy if sign > 0 else d_copy)(part, where).wait_send()

    each(finish)


def fold(arrays, out_shapes, pieces, collective_id):
    count = lax.axis_size("seq")
    total = len(pieces)
    sem = pltpu.SemaphoreType.DMA
    line = count // 4
    bufs = []
    for times in (2, 1, 1, 1, 1, 1):
        bufs += [VMEM((times * piece[0],) + piece[1], BF) for piece in pieces]
    return pl.pallas_call(
        functools.partial(fold_kernel, (len(arrays), len(out_shapes), pieces), count),
        out_shape=[jax.ShapeDtypeStruct(shape, F32) for shape in out_shapes],
        in_specs=[pl.BlockSpec(memory_space=VMEM)] * len(arrays),
        out_specs=[pl.BlockSpec(memory_space=VMEM)] * len(out_shapes),
        scratch_shapes=bufs + [sem((total, 2 * line))] * 2 + [sem((total, line))] * 6,
        compiler_params=pltpu.CompilerParams(
            collective_id=collective_id, has_side_effects=True, vmem_limit_bytes=60 * 2**20
        ),
    )(*arrays)


def exchange_kernel(x_ref, o_ref, own_sem, z_send, z_recv, x_send, x_recv, y_send, y_recv, c_send, c_recv):
    count = o_ref.shape[1]
    line = count // 4
    group = lax.axis_index("dp")
    me = lax.axis_index("seq")
    at, side, core = place(me)
    peers = line_peers(at, side, core, group, line)
    below, above, beside, sibling = (peer for _, peer in peers)
    across = (1 - group, me)
    meet(peers + [(at >= 0, across)])

    def remote(src, dst, send, recv, index, peer):
        return pltpu.make_async_remote_copy(
            src_ref=src, dst_ref=dst, send_sem=send.at[index], recv_sem=recv.at[index],
            device_id=peer, device_id_type=MESH,
        )

    items = [(0, 0)] + [(far, turn) for far in range(1, line) for turn in range(2)]

    def where_of(item):
        return at + item[0] * (2 * item[1] - 1)

    def number(item):
        return 2 * item[0] + item[1]

    def given(item, action):
        @pl.when((where_of(item) >= 0) & (where_of(item) < line))
        def _():
            action()

    def spot(item, other_group, other_side, other_core):
        g = 1 - group if other_group else group
        s = 1 - side if other_side else side
        c = 1 - core if other_core else core
        return o_ref.at[g, 4 * where_of(item) + 2 * s + c]

    def here(item, other_group, other_side):
        if item == (0, 0) and not other_group and not other_side:
            return x_ref
        return spot(item, other_group, other_side, False)

    def z_copy(item, turn, peer):
        far = (item[0] + 1, turn)
        return remote(here(item, 0, 0), spot(item, 0, 0, 0), z_send, z_recv, number(far), peer)

    def side_copy(item, other_group, arrived):
        dst = spot(item, other_group, arrived, 0)
        src = dst if arrived else here(item, other_group, 0)
        return remote(src, dst, x_send, x_recv, 2 * number(item) + other_group, beside)

    def cross_copy(item, other_side, arrived):
        dst = spot(item, arrived, other_side, 0)
        src = dst if arrived else here(item, 0, other_side)
        return remote(src, dst, y_send, y_recv, 2 * number(item) + other_side, across)

    def core_copy(item, other_group, other_side, arrived):
        dst = spot(item, other_group, other_side, arrived)
        src = dst if arrived else here(item, other_group, other_side)
        index = 4 * number(item) + 2 * other_group + other_side
        return remote(src, dst, c_send, c_recv, index, sibling)

    def by_side(item):
        return lax.rem(where_of(item), 2) == 0

    def z_links(item, act):
        far, turn = item
        if far + 1 < line:
            if far == 0 or turn == 0:

                @pl.when(at + 1 < line)
                def _():
                    act(z_copy(item, 0, above))

            if far == 0 or turn == 1:

                @pl.when(at > 0)
                def _():
                    act(z_copy(item, 1, below))

    def start(copy):
        copy.start()

    def launch(item):
        z_links(item, start)
        side_copy(item, 0, False).start()
        cross_copy(item, 0, False).start()
        core_copy(item, 0, 0, False).start()

    def first(item):
        z = remote(spot(item, 0, 0, 0), spot(item, 0, 0, 0), z_send, z_recv, number(item), beside)
        z.wait_recv()
        launch(item)

    def second(item):
        side_copy(item, 0, True).wait_recv()

        @pl.when(jnp.logical_not(by_side(item)))
        def _():
            cross_copy(item, 1, False).start()

        core_copy(item, 0, 1, False).start()
        cross_copy(item, 0, True).wait_recv()

        @pl.when(by_side(item))
        def _():
            side_copy(item, 1, False).start()

        core_copy(item, 1, 0, False).start()

    def third(item):
        @pl.when(by_side(item))
        def _():
            side_copy(item, 1, True).wait_recv()

        @pl.when(jnp.logical_not(by_side(item)))
        def _():
            cross_copy(item, 1, True).wait_recv()

        core_copy(item, 1, 1, False).start()

    def at_far(far):
        return [item for item in items if item[0] == far]

    own = pltpu.make_async_copy(x_ref, spot((0, 0), 0, 0, 0), own_sem.at[0])
    own.start()
    launch((0, 0))
    for step in range(1, line + 2):
        for item in at_far(step):
            given(item, functools.partial(first, item))
        for item in at_far(step - 1):
            given(item, functools.partial(second, item))
        if step >= 2:
            for item in at_far(step - 2):
                given(item, functools.partial(third, item))
    own.wait()

    def finish(item):
        z_links(item, lambda copy: copy.wait_send())
        side_copy(item, 0, False).wait_send()
        cross_copy(item, 0, False).wait_send()

        @pl.when(by_side(item))
        def _():
            side_copy(item, 1, False).wait_send()

        @pl.when(jnp.logical_not(by_side(item)))
        def _():
            cross_copy(item, 1, False).wait_send()

        for other_group in range(2):
            for other_side in range(2):
                core_copy(item, other_group, other_side, False).wait_send()
                core_copy(item, other_group, other_side, True).wait_recv()

    for item in items:
        given(item, functools.partial(finish, item))


def exchange(x, collective_id):
    count = lax.axis_size("seq")
    marks = 2 * (count // 4) + 2
    sem = pltpu.SemaphoreType.DMA
    return pl.pallas_call(
        exchange_kernel,
        out_shape=jax.ShapeDtypeStruct((2, count) + x.shape, x.dtype),
        in_specs=[pl.BlockSpec(memory_space=VMEM)],
        out_specs=pl.BlockSpec(memory_space=pl.ANY),
        scratch_shapes=[sem((1,))] + [sem((marks,))] * 2 + [sem((2 * marks,))] * 4 + [sem((4 * marks,))] * 2,
        compiler_params=pltpu.CompilerParams(collective_id=collective_id, has_side_effects=True),
    )(x)


def row_gather(line, rows, cuts):
    size = rows // cuts
    return tuple(
        (
            line,
            lambda x, h=h: x[0].at[pl.ds(h * size, size)],
            lambda o, q, h=h: o[0].at[q, pl.ds(h * size, size)],
        )
        for h in range(cuts)
    )


def row_pieces(line, rows, width, cuts):
    size = rows // cuts
    return tuple(
        (
            line,
            (size, width),
            lambda x, q, h=h: x[0].at[q, pl.ds(h * size, size)],
            lambda o, h=h: o[0].at[pl.ds(h * size, size)],
        )
        for h in range(cuts)
    )


def visible_rows(kind, run_devs, rows_dev, half, q):
    first = half + rows_dev * lax.rem(q, run_devs) if kind else rows_dev * q
    return pl.multiple_of(first, 32)


def visible_gather(line, run_devs, rows_dev, half):
    size = rows_dev // 2
    return tuple(
        (
            run_devs // 4 if kind else line,
            lambda x, m=m, kind=kind, j=j: x[0].at[m, kind, pl.ds(size * j, size)],
            lambda o, q, m=m, kind=kind, j=j: o[0].at[
                m, pl.ds(visible_rows(kind, run_devs, rows_dev, half, q) + size * j, size)
            ],
        )
        for kind in range(2)
        for m in range(MB)
        for j in range(2)
    )


def visible_sum(line, run_devs, rows_dev, half, width):
    return tuple(
        (
            run_devs // 4 if kind else line,
            (MB, rows_dev, width),
            lambda x, q, kind=kind: x[0].at[
                :, pl.ds(visible_rows(kind, run_devs, rows_dev, half, q), rows_dev)
            ],
            lambda o, kind=kind: o[0].at[:, kind],
        )
        for kind in range(2)
    )


def place_kernel(l_ref, r_ref, *refs):
    refs[-1][...] = jnp.dot(l_ref[...], r_ref[...], preferred_element_type=F32).astype(BF)


def place_product(buffer, left, right, first, rows):
    depth, width = right.shape
    block = width // 2
    given = () if buffer is None else (buffer,)
    return pl.pallas_call(
        place_kernel,
        grid=(left.shape[0] // block,),
        out_shape=jax.ShapeDtypeStruct((rows, width), BF),
        in_specs=[
            pl.BlockSpec((block, depth), lambda i: (i, 0)),
            pl.BlockSpec((depth, width), lambda i: (0, 0)),
        ]
        + [pl.BlockSpec(memory_space=pl.ANY)] * len(given),
        out_specs=pl.BlockSpec((block, width), lambda i: (first // block + i, 0)),
        input_output_aliases={2: 0} if given else {},
    )(left, right, *given)


def contract(left, right, left_dim, right_dim):
    return lax.dot_general(
        left, right, (((left_dim,), (right_dim,)), ((), ())), preferred_element_type=F32
    )


def norm_forward(values, gain, bias):
    centred = values - jnp.mean(values, axis=-1, keepdims=True)
    inverse = lax.rsqrt(jnp.mean(centred * centred, axis=-1, keepdims=True) + EPS_NORM)
    unit = centred * inverse
    return (unit * gain + bias, unit, inverse)


def norm_backward(upstream, unit, inverse, gain):
    scaled = upstream * gain
    inner = (
        scaled
        - jnp.mean(scaled, axis=-1, keepdims=True)
        - unit * jnp.mean(scaled * unit, axis=-1, keepdims=True)
    )
    return (inverse * inner, jnp.sum(upstream * unit, axis=0), jnp.sum(upstream, axis=0))


def head_probs(pos_ref, q, k):
    scores = contract(q, k, 0, 0) * HD ** (-0.5)
    key_pos = lax.broadcasted_iota(jnp.int32, scores.shape, 1)
    scores = jnp.where(key_pos <= pos_ref[...], scores, MASKED)
    shifted = jnp.exp(scores - jnp.max(scores, axis=1, keepdims=True))
    return shifted * (1.0 / jnp.sum(shifted, axis=1, keepdims=True))


def attend_kernel(pos_ref, q_ref, kv_ref, o_ref):
    probs = head_probs(pos_ref, q_ref[...], kv_ref[0]).astype(BF)
    o_ref[...] = contract(kv_ref[1], probs, 1, 1).astype(BF)


def attend_back_kernel(pos_ref, q_ref, kv_ref, g_ref, dq_ref, dkv_ref):
    q, k, v, g = q_ref[...], kv_ref[0], kv_ref[1], g_ref[...]
    probs = head_probs(pos_ref, q, k)
    grad = contract(g, v, 0, 0)
    back = (probs * (grad - jnp.sum(probs * grad, axis=1, keepdims=True))).astype(BF)
    scale = HD ** (-0.5)
    dq_ref[...] = (contract(k, back, 1, 1) * scale).astype(BF)
    dkv_ref[0] = (contract(q, back, 1, 0) * scale).astype(BF)
    dkv_ref[1] = contract(g, probs.astype(BF), 1, 0).astype(BF)


def attend(query_pos, q, kv):
    rows, keys = query_pos.shape[0], kv.shape[2] * query_pos.shape[0] // q.shape[1]
    small = pl.BlockSpec((HD, rows), lambda m, h: (h, m))
    large = pl.BlockSpec((2, HD, keys), lambda m, h: (0, h, m))
    return pl.pallas_call(
        attend_kernel,
        grid=(q.shape[1] // rows, HEADS),
        out_shape=jax.ShapeDtypeStruct(q.shape, BF),
        in_specs=[pl.BlockSpec((rows, 1), lambda m, h: (0, 0)), small, large],
        out_specs=small,
    )(query_pos, q, kv)


def attend_back(query_pos, q, kv, grad_out):
    rows, keys = query_pos.shape[0], kv.shape[2] * query_pos.shape[0] // q.shape[1]
    small = pl.BlockSpec((HD, rows), lambda m, h: (h, m))
    large = pl.BlockSpec((2, HD, keys), lambda m, h: (0, h, m))
    return pl.pallas_call(
        attend_back_kernel,
        grid=(q.shape[1] // rows, HEADS),
        out_shape=[jax.ShapeDtypeStruct(q.shape, BF), jax.ShapeDtypeStruct(kv.shape, BF)],
        in_specs=[pl.BlockSpec((rows, 1), lambda m, h: (0, 0)), small, large, small],
        out_specs=[small, large],
    )(query_pos, q, kv, grad_out)


def lookup_kernel(first_ref, slot_ref, table_ref, *refs):
    slots = slot_ref[...] - first_ref[0]
    ids = lax.broadcasted_iota(jnp.int32, (slots.shape[0], table_ref.shape[1]), 1)
    rows = contract(jnp.where(slots == ids, 1.0, 0.0).astype(BF), table_ref[...], 1, 1).astype(BF)
    refs[-1][...] = rows if len(refs) == 1 else refs[0][...] + rows


def lookup(first, slots, table, others, block):
    width, held = table.shape
    rows = pl.BlockSpec((block, width), lambda i: (i, 0))
    given = () if others is None else (others,)
    return pl.pallas_call(
        lookup_kernel,
        grid=(slots.shape[0] // block,),
        out_shape=jax.ShapeDtypeStruct((slots.shape[0], width), BF),
        in_specs=[
            pl.BlockSpec(memory_space=pltpu.SMEM),
            pl.BlockSpec((block, 1), lambda i: (i, 0)),
            pl.BlockSpec((width, held), lambda i: (0, 0)),
        ]
        + [rows] * len(given),
        out_specs=rows,
    )(first, slots, table, *given)


def adamw(weight, moment_a, moment_b, gradient, rate, decay):
    moment_a = MOMENT_ONE * moment_a + (1.0 - MOMENT_ONE) * gradient
    moment_b = MOMENT_TWO * moment_b + (1.0 - MOMENT_TWO) * gradient * gradient
    update = (
        moment_a
        / (1.0 - MOMENT_ONE**STEP)
        / (jnp.sqrt(moment_b / (1.0 - MOMENT_TWO**STEP)) + EPS_ADAM)
    )
    weight = weight - rate * (update + decay * weight)
    return (weight, moment_a, moment_b, weight.astype(BF))


def on_device(
    tokens,
    targets,
    counted,
    cont_label,
    pair_map,
    ref_logp,
    vocab_slot,
    embed_table,
    embed_first,
    embed_second,
    layer_weights,
    layer_first,
    layer_second,
    norm_params,
    norm_first,
    norm_second,
):
    seq_count = lax.axis_size("seq")
    group_count = lax.axis_size("dp")
    all_count = seq_count * group_count
    seq_rank = lax.axis_index("seq")
    group_rank = lax.axis_index("dp")
    device_rank = group_rank * seq_count + seq_rank
    rows_dev = tokens.shape[3]
    half = rows_dev * seq_count
    vocab_dev, width = embed_table.shape
    run_count = half // CLEN
    run_devs = CLEN // rows_dev
    own_rows = MB * 2 * rows_dev

    table_t = embed_table.T
    norm_dev = norm_params.shape[0]
    norm_parts = [norm_params]
    for step in range(1, group_count):
        norm_parts.append(
            lax.ppermute(
                norm_params, "dp", [(i, (i - step) % group_count) for i in range(group_count)]
            )
        )
    sent, *norm_parts = lax.optimization_barrier((table_t.astype(BF), *norm_parts))
    norm_all = jnp.zeros((group_count, norm_dev), F32)
    for step in range(group_count):
        norm_all = lax.dynamic_update_index_in_dim(
            norm_all, norm_parts[step], lax.rem(group_rank + step, group_count), 0
        )
    slab_t = [sent]
    for step in range(1, group_count):
        slab_t.append(
            lax.ppermute(
                slab_t[0], "dp", [(i, (i - step) % group_count) for i in range(group_count)]
            )
        )
    weights = lax.all_gather(
        layer_weights.T.astype(BF)[None], ("dp", "seq"), axis=0, tiled=True
    ).reshape(-1, width)
    w_q = weights[:width]
    w_o = weights[3 * width : 4 * width]
    w_kv = weights[width : 3 * width]
    w_up = weights[4 * width : 4 * width + FF]
    w_dn = weights[4 * width + FF :]

    marks = counted[:, 0]
    spots = jnp.arange(rows_dev, dtype=jnp.int32)
    ranks = (
        jnp.sum(jnp.where(spots[None, :, None] <= spots[None, None, :], marks[:, :, None], 0), axis=1)
        - 1
    )
    pick_ids = jnp.arange(PICK, dtype=jnp.int32)
    pick_hit = (ranks[:, None, :] == pick_ids[None, :, None]) & (marks[:, None, :] == 1)
    pick_targets = jnp.sum(jnp.where(pick_hit, targets[:, 0][:, None, :], 0), axis=2)
    pick_low = pick_hit.astype(BF)
    slots = vocab_slot[jnp.concatenate([tokens[:, 0].reshape(-1), pick_targets.reshape(-1)])]
    small = jnp.concatenate([slots.astype(F32), norm_all.reshape(-1)])
    small = jnp.pad(small, (0, -small.shape[0] % 1024)).reshape(-1, 128)
    small_all = direct_gather(small, False, 1).reshape(seq_count, -1)
    slots_all = small_all[:, : own_rows + MB * PICK].astype(jnp.int32)
    gains = (
        small_all[:, own_rows + MB * PICK :][:, : group_count * norm_dev]
        .reshape(seq_count, group_count, norm_dev)
        .transpose(1, 0, 2)
        .astype(BF)
        .astype(F32)
        .reshape(6, width)
    )
    row_slots = slots_all[:, :own_rows].reshape(-1)
    target_slots = slots_all[:, own_rows:].reshape(-1)
    vocab_ids = jnp.arange(vocab_dev, dtype=jnp.int32)

    def hits(slot_ids, step):
        part = lax.rem(group_rank + step, group_count)
        first = (part * seq_count + seq_rank) * vocab_dev
        return (slot_ids - first)[:, None] == vocab_ids[None, :]

    partial = None
    for step in range(group_count):
        part = lax.rem(group_rank + step, group_count)
        first = (part * seq_count + seq_rank) * vocab_dev
        partial = lookup(first[None], row_slots[:, None], slab_t[step], partial, own_rows)
    line = seq_count // 4
    (stream,) = fold(
        [partial.reshape(seq_count, own_rows, width)],
        [(own_rows, width)],
        row_pieces(line, own_rows, width, 2),
        2,
    )

    normed, unit_one, inverse_one = norm_forward(stream, gains[0], gains[3])
    hidden_one = normed.astype(BF)
    run_dev = seq_rank // run_devs * run_devs
    key_rows = half + CLEN
    (hidden_sel,) = spread(
        [hidden_one.reshape(MB, 2, rows_dev, width)],
        [jax.ShapeDtypeStruct((MB, key_rows, width), BF)],
        visible_gather(line, run_devs, rows_dev, half),
        3,
    )
    hidden_sel = hidden_sel.reshape(MB * key_rows, width)
    pairs = contract(w_kv, hidden_sel, 1, 1).astype(BF).reshape(2, width, MB * key_rows)
    queries = contract(w_q, hidden_one, 1, 1).astype(BF)
    start = seq_rank * rows_dev
    query_pos = jnp.concatenate([start + spots, half + (start - run_dev * rows_dev) + spots])[:, None]
    attended = attend(query_pos, queries, pairs)
    stream_one = stream + contract(attended, w_o, 0, 0)
    normed, unit_two, inverse_two = norm_forward(stream_one, gains[1], gains[4])
    hidden_two = normed.astype(BF)
    up_proj = contract(w_up, hidden_two, 1, 1)
    activated = jax.nn.gelu(up_proj, approximate=False).astype(BF)
    stream_two = stream_one + contract(activated, w_dn, 0, 0)
    normed, unit_final, inverse_final = norm_forward(stream_two, gains[2], gains[5])
    final = normed.astype(BF).reshape(MB, 2, rows_dev, width)[:, 1]
    picked = jnp.einsum("mpr,mrd->mpd", pick_low, final, preferred_element_type=F32).astype(BF)

    (head_rows,) = spread(
        [picked.reshape(MB * PICK, width)],
        [jax.ShapeDtypeStruct((seq_count, MB * PICK, width), BF)],
        row_gather(line, MB * PICK, 1),
        4,
    )
    head_rows = head_rows.reshape(seq_count * MB * PICK, width)
    logits = [contract(head_rows, slab_t[part], 1, 0) for part in range(group_count)]
    target_hits = [hits(target_slots, part) for part in range(group_count)]
    highest = jnp.max(logits[0], axis=1)
    for part in range(1, group_count):
        highest = jnp.maximum(highest, jnp.max(logits[part], axis=1))
    summed = jnp.zeros_like(highest)
    target_logit = jnp.zeros_like(highest)
    for part in range(group_count):
        summed = summed + jnp.sum(jnp.exp(logits[part] - highest[:, None]), axis=1)
        target_logit = target_logit + jnp.sum(jnp.where(target_hits[part], logits[part], 0.0), axis=1)
    stats = direct_gather(
        jnp.stack([highest, summed, target_logit]).reshape(-1, 128), False, 5
    ).reshape(seq_count, 3, -1)
    overall = jnp.max(stats[:, 0], axis=0)
    total = jnp.sum(stats[:, 1] * jnp.exp(stats[:, 0] - overall[None]), axis=0)
    log_total = overall + jnp.log(total)
    token_lp = jnp.sum(stats[:, 2], axis=0) - log_total

    run_ids = jnp.arange(run_count, dtype=jnp.int32)
    run_of_dev = jnp.arange(seq_count, dtype=jnp.int32) * rows_dev // CLEN
    run_match = run_of_dev[:, None] == run_ids[None, :]
    dev_lp = jnp.sum(token_lp.reshape(seq_count, MB, PICK), axis=2)
    run_lp = jnp.sum(jnp.where(run_match[:, None, :], dev_lp[:, :, None], 0.0), axis=0)
    labels = lax.dynamic_index_in_dim(cont_label, group_rank, 1, keepdims=False)
    pairing = lax.dynamic_index_in_dim(pair_map, group_rank, 1, keepdims=False)
    reference_lp = lax.dynamic_index_in_dim(ref_logp, group_rank, 1, keepdims=False)
    label_match = labels[:, :, None] == run_ids[None, None, :]
    label_lp = jnp.sum(jnp.where(label_match, run_lp[:, :, None], 0.0), axis=1)
    margin = label_lp - reference_lp
    chosen = pairing[:, 0::2, None] == run_ids[None, None, :]
    rejected = pairing[:, 1::2, None] == run_ids[None, None, :]
    delta = jnp.sum(jnp.where(chosen, margin[:, None, :], 0.0), axis=2) - jnp.sum(
        jnp.where(rejected, margin[:, None, :], 0.0), axis=2
    )
    loss = jnp.sum(jax.nn.softplus(-DPO_BETA * delta))
    pair_grad = -DPO_BETA * jax.nn.sigmoid(-DPO_BETA * delta)
    label_grad = jnp.sum(
        jnp.where(chosen, pair_grad[:, :, None], 0.0)
        - jnp.where(rejected, pair_grad[:, :, None], 0.0),
        axis=1,
    )
    run_grad = jnp.sum(jnp.where(label_match, label_grad[:, None, :], 0.0), axis=2)
    dev_grad = jnp.sum(jnp.where(run_match[:, None, :], run_grad[None], 0.0), axis=2)
    row_grad = jnp.broadcast_to(dev_grad[:, :, None], (seq_count, MB, PICK)).reshape(-1)

    head_back = 0.0
    logit_grads = []
    for part in range(group_count):
        logit_grad = (
            row_grad[:, None]
            * (target_hits[part].astype(F32) - jnp.exp(logits[part] - log_total[:, None]))
        ).astype(BF)
        logit_grads.append(logit_grad)
        head_back = head_back + contract(logit_grad, slab_t[part], 1, 1)
    head_back = head_back.astype(BF)
    moved = [(i, (i + 1) % group_count) for i in range(group_count)]
    if group_count == 2:
        head_back, head_part = lax.optimization_barrier(
            (head_back, contract(head_rows, logit_grads[1], 0, 0).astype(BF))
        )
        head_other = lax.ppermute(head_part, "dp", moved)
    (row_back,) = fold(
        [head_back.reshape(seq_count, MB * PICK, width)],
        [(MB * PICK, width)],
        row_pieces(line, MB * PICK, width, 1),
        6,
    )
    row_back = row_back.astype(BF).reshape(MB, PICK, width)
    cont_back = jnp.einsum("mpr,mpd->mrd", pick_low, row_back, preferred_element_type=F32)
    upstream = jnp.concatenate(
        [jnp.zeros((MB, 1, rows_dev, width), F32), cont_back[:, None]], axis=1
    ).reshape(own_rows, width)

    grad_two, gain_final, bias_final = norm_backward(upstream, unit_final, inverse_final, gains[2])
    grad_ffn = grad_two.astype(BF)
    columns = weights.shape[0]
    weight_grad = place_product(None, activated, grad_ffn, 4 * width + FF, columns)
    grad_act = contract(w_dn, grad_ffn, 1, 1)
    _, gelu_pull = jax.vjp(lambda pre_act: jax.nn.gelu(pre_act, approximate=False), up_proj)
    grad_up = gelu_pull(grad_act)[0].astype(BF)
    weight_grad = place_product(weight_grad, grad_up, hidden_two, 4 * width, columns)
    grad_hidden = contract(grad_up, w_up, 0, 0)
    grad_mid, gain_two, bias_two = norm_backward(grad_hidden, unit_two, inverse_two, gains[1])
    grad_one = grad_two + grad_mid
    grad_branch = grad_one.astype(BF)
    weight_grad = place_product(weight_grad, attended, grad_branch, 3 * width, columns)
    grad_attended = contract(w_o, grad_branch, 1, 1).astype(BF)
    grad_query, grad_pairs = attend_back(query_pos, queries, pairs, grad_attended)
    if group_count == 2:
        grad_query, head_other = lax.optimization_barrier((grad_query, head_other))
    grad_pairs = grad_pairs.reshape(2 * width, MB * key_rows)
    weight_grad = place_product(weight_grad, grad_query, hidden_one, 0, columns)
    weight_grad = place_product(weight_grad, grad_pairs, hidden_sel, width, columns)
    low_sel = contract(grad_pairs, w_kv, 0, 0).astype(BF).reshape(MB, key_rows, width)
    weight_sum = lax.psum_scatter(
        weight_grad.reshape(all_count, -1, width), ("dp", "seq"), scatter_dimension=0, tiled=True
    )[0].astype(F32)
    (low_own,) = fold(
        [low_sel],
        [(MB, 2, rows_dev, width)],
        visible_sum(line, run_devs, rows_dev, half, width),
        7,
    )
    grad_low = low_own.reshape(own_rows, width) + contract(grad_query, w_q, 0, 0)
    grad_first, gain_one, bias_one = norm_backward(grad_low, unit_one, inverse_one, gains[0])
    norm_rows = jnp.stack([gain_one, gain_two, gain_final, bias_one, bias_two, bias_final])
    if group_count == 2:
        head_own = contract(head_rows, logit_grads[0], 0, 0)
        pad_rows = 8
        all_rows = exchange(
            jnp.concatenate(
                [grad_one + grad_first, norm_rows, jnp.zeros((pad_rows - 6, width), F32)]
            ).astype(BF),
            8,
        )
        other_slots = lax.ppermute(row_slots, "dp", moved)
        embed_sum = lax.optimization_barrier(head_own + head_other.astype(F32))
        for part in range(group_count):
            part_slots = jnp.where(group_rank == part, row_slots, other_slots)
            part_slots = jnp.pad(
                part_slots.reshape(seq_count, own_rows), ((0, 0), (0, pad_rows)), constant_values=-1
            ).reshape(-1)
            embed_sum = embed_sum + contract(
                all_rows[part].reshape(-1, width), hits(part_slots, 0).astype(BF), 0, 0
            )
        norm_all = jnp.sum(
            all_rows.reshape(all_count, own_rows + pad_rows, width)[
                :, own_rows : own_rows + 6
            ].astype(F32),
            axis=0,
        )
    else:
        row_grads, norm_grads = spread(
            [
                (grad_one + grad_first).astype(BF),
                jnp.concatenate([norm_rows, jnp.zeros((10, width), F32)]).astype(BF),
            ],
            [
                jax.ShapeDtypeStruct((seq_count, own_rows, width), BF),
                jax.ShapeDtypeStruct((seq_count, 16, width), BF),
            ],
            row_gather(line, own_rows, 2)
            + ((line, lambda x: x[1], lambda o, q: o[1].at[q]),),
            8,
        )
        row_grads = row_grads.reshape(-1, width)
        norm_sum = jnp.sum(norm_grads[:, :6].astype(F32), axis=0)
        norm_all = norm_sum
        for step in range(1, group_count):
            norm_all = norm_all + lax.ppermute(
                norm_sum, "dp", [(i, (i + step) % group_count) for i in range(group_count)]
            )

        def table_grad(step):
            return contract(head_rows, logit_grads[step], 0, 0) + contract(
                row_grads, hits(row_slots, step).astype(BF), 0, 0
            )

        arrived = [
            lax.ppermute(
                table_grad(step).astype(BF),
                "dp",
                [(i, (i + step) % group_count) for i in range(group_count)],
            )
            for step in range(1, group_count)
        ]
        embed_sum = table_grad(0)
        for block in arrived:
            embed_sum = embed_sum + block.astype(F32)
    norm_own = lax.dynamic_slice_in_dim(norm_all.reshape(-1), device_rank * norm_dev, norm_dev, 0)
    squares = (
        jnp.sum(embed_sum * embed_sum)
        + jnp.sum(weight_sum * weight_sum)
        + jnp.sum(norm_own * norm_own)
    )
    lanes = lax.broadcasted_iota(jnp.int32, (8, 128), 1)
    scalars = direct_gather(
        jnp.where(lanes == 0, squares, jnp.where(lanes == 1, loss, 0.0)), True, 9
    )
    square_total = jnp.sum(scalars[:, 0, 0])
    loss_total = jnp.sum(scalars[::seq_count, 0, 1])
    grad_norm = jnp.sqrt(square_total)
    factor = jnp.minimum(1.0, CLIP_NORM / grad_norm)
    embed_out = adamw(
        table_t, embed_first.T, embed_second.T, embed_sum * factor, LEARN_RATE, WEIGHT_DECAY
    )
    layer_out = adamw(
        layer_weights.T,
        layer_first.T,
        layer_second.T,
        weight_sum * factor,
        LEARN_RATE,
        WEIGHT_DECAY,
    )
    norm_out = adamw(norm_params, norm_first, norm_second, norm_own * factor, NORM_RATE, 0.0)
    return (
        embed_out[0].T,
        embed_out[1].T,
        embed_out[2].T,
        embed_out[3].T,
        layer_out[0].T,
        layer_out[1].T,
        layer_out[2].T,
        layer_out[3].T,
        norm_out[0],
        norm_out[1],
        norm_out[2],
        norm_out[3],
        grad_norm,
        loss_total,
    )


def solution(mesh):
    return jax.shard_map(
        on_device,
        mesh=mesh,
        in_specs=(
            P(None, "dp", None, "seq"),
            P(None, "dp", "seq"),
            P(None, "dp", "seq"),
            P(),
            P(),
            P(),
            P(),
            P(("dp", "seq"), None),
            P(("dp", "seq"), None),
            P(("dp", "seq"), None),
            P(None, ("dp", "seq")),
            P(None, ("dp", "seq")),
            P(None, ("dp", "seq")),
            P(("dp", "seq")),
            P(("dp", "seq")),
            P(("dp", "seq")),
        ),
        out_specs=(
            P(("dp", "seq"), None),
            P(("dp", "seq"), None),
            P(("dp", "seq"), None),
            P(("dp", "seq"), None),
            P(None, ("dp", "seq")),
            P(None, ("dp", "seq")),
            P(None, ("dp", "seq")),
            P(None, ("dp", "seq")),
            P(("dp", "seq")),
            P(("dp", "seq")),
            P(("dp", "seq")),
            P(("dp", "seq")),
            P(),
            P(),
        ),
        check_vma=False,
    )
```

```python
import functools

import jax
import jax.numpy as jnp
from jax import lax
from jax.experimental import pallas as pl
from jax.experimental.pallas import tpu as pltpu
from jax.sharding import PartitionSpec as P


HEADS = 17
HD = 64
FF = 4352
PICK = 32
CLEN = 512
MB = 2
STEP = 10


EPS_NORM = 1e-05
DPO_BETA = 0.05
CLIP_NORM = 1.0
LEARN_RATE = 0.03
NORM_RATE = 0.4
WEIGHT_DECAY = 0.1
MOMENT_ONE = 0.9
MOMENT_TWO = 0.999
EPS_ADAM = 1e-08
MASKED = -1e30
BF = jnp.bfloat16
F32 = jnp.float32
MESH = pl.DeviceIdType.MESH
VMEM = pltpu.VMEM


def meet(peers):
    barrier = pltpu.get_barrier_semaphore()
    for there, peer in peers:

        @pl.when(there)
        def _():
            pl.semaphore_signal(barrier, inc=1, device_id=peer, device_id_type=MESH)

    pl.semaphore_wait(barrier, sum(jnp.where(there, 1, 0) for there, _ in peers))


def direct_kernel(whole, x_ref, o_ref, send_sem, recv_sem):
    seq_count = lax.axis_size("seq")
    group_rank = lax.axis_index("dp")
    me = lax.axis_index("seq")
    count = o_ref.shape[0]
    if whole:
        me = group_rank * seq_count + me

    def peer(step):
        other = lax.rem(me + step, count)
        if whole:
            return (other // seq_count, lax.rem(other, seq_count))
        return (group_rank, other)

    barrier = pltpu.get_barrier_semaphore()

    def greet(step, carry):
        pl.semaphore_signal(barrier, inc=1, device_id=peer(step), device_id_type=MESH)
        return carry

    lax.fori_loop(1, count, greet, 0)
    o_ref[me] = x_ref[...]
    pl.semaphore_wait(barrier, count - 1)

    def copy(step):
        return pltpu.make_async_remote_copy(
            src_ref=x_ref,
            dst_ref=o_ref.at[me],
            send_sem=send_sem.at[step],
            recv_sem=recv_sem.at[step],
            device_id=peer(step),
            device_id_type=MESH,
        )

    def begin(step, carry):
        copy(step).start()
        return carry

    def finish(step, carry):
        copy(step).wait()
        return carry

    lax.fori_loop(1, count, begin, 0)
    lax.fori_loop(1, count, finish, 0)


def direct_gather(x, whole, collective_id):
    count = lax.axis_size("seq") * (lax.axis_size("dp") if whole else 1)
    return pl.pallas_call(
        functools.partial(direct_kernel, whole),
        out_shape=jax.ShapeDtypeStruct((count,) + x.shape, x.dtype),
        in_specs=[pl.BlockSpec(memory_space=VMEM)],
        out_specs=pl.BlockSpec(memory_space=VMEM),
        scratch_shapes=[pltpu.SemaphoreType.DMA((count,)), pltpu.SemaphoreType.DMA((count,))],
        compiler_params=pltpu.CompilerParams(collective_id=collective_id, has_side_effects=True),
    )(x)


def place(rank):
    return (rank // 4, lax.rem(rank, 4) // 2, lax.rem(rank, 2))


def line_peers(at, side, core, group, line):
    return [
        (at > 0, (group, 4 * (at - 1) + 2 * side + core)),
        (at < line - 1, (group, 4 * (at + 1) + 2 * side + core)),
        (at >= 0, (group, 4 * at + 2 * (1 - side) + core)),
        (at >= 0, (group, 4 * at + 2 * side + 1 - core)),
    ]


def spread_kernel(parts, count, *refs):
    given, wanted, pieces = parts
    total = len(pieces)
    x_refs, o_refs = refs[:given], refs[given : given + wanted]
    local_sem, z_send, z_recv, b_send, b_recv, c_send, c_recv = refs[given + wanted :]
    spans = [piece[0] for piece in pieces]
    ins = [piece[1](x_refs) for piece in pieces]
    line = count // 4
    group = lax.axis_index("dp")
    at, side, core = place(lax.axis_index("seq"))
    peers = line_peers(at, side, core, group, line)
    below, above, beside, sibling = (peer for _, peer in peers)
    meet(peers)

    def seq_of(where, which_side, which_core):
        return 4 * where + 2 * which_side + which_core

    def remote(src, dst, send, recv, peer):
        return pltpu.make_async_remote_copy(
            src_ref=src, dst_ref=dst, send_sem=send, recv_sem=recv, device_id=peer, device_id_type=MESH
        )

    def low_high(span):
        low = at // span * span
        return low, low + span

    def view(part, where, which_side, which_core):
        return pieces[part][2](o_refs, seq_of(where, which_side, which_core))

    def where_of(item):
        far = (item + 1) // 2
        return at - far if item % 2 else at + far

    def valid(part, item):
        low, high = low_high(spans[part])
        where = where_of(item)
        return (where >= low) & (where < high)

    def z_copy(part, item, up):
        where = where_of(item)
        far = (item + 1) // 2 + 1
        mark = 2 * far - 1 if up else 2 * far
        src = ins[part] if item == 0 else view(part, where, side, core)
        return remote(
            src,
            view(part, where, side, core),
            z_send.at[part, mark],
            z_recv.at[part, mark],
            above if up else below,
        )

    def b_copy(part, item):
        where = where_of(item)
        src = ins[part] if item == 0 else view(part, where, side, core)
        return remote(
            src, view(part, where, side, core), b_send.at[part, item], b_recv.at[part, item], beside
        )

    def b_arrived(part, item):
        where = where_of(item)
        spot = view(part, where, 1 - side, core)
        return remote(spot, spot, b_send.at[part, item], b_recv.at[part, item], beside)

    def z_arrived(part, item):
        spot = view(part, where_of(item), side, core)
        return remote(spot, spot, z_send.at[part, item], z_recv.at[part, item], beside)

    def c_copy(part, item, from_side):
        where = where_of(item)
        mine = item == 0 and not from_side
        which = 1 - side if from_side else side
        src = ins[part] if mine else view(part, where, which, core)
        index = 2 * item + from_side
        return remote(
            src, view(part, where, which, core), c_send.at[part, index], c_recv.at[part, index], sibling
        )

    def c_arrived(part, item, from_side):
        which = 1 - side if from_side else side
        spot = view(part, where_of(item), which, 1 - core)
        index = 2 * item + from_side
        return remote(spot, spot, c_send.at[part, index], c_recv.at[part, index], sibling)

    items = 2 * line - 1

    def goes_up(part):
        _, high = low_high(spans[part])
        return at + 1 < high

    def goes_down(part):
        low, _ = low_high(spans[part])
        return at - 1 >= low

    def active(part, item):
        return (item + 1) // 2 < spans[part]

    for part in range(total):
        pltpu.make_async_copy(
            ins[part], view(part, at, side, core), local_sem.at[part]
        ).start()

    def launch(part, item):
        @pl.when(valid(part, item))
        def _():
            if item == 0 or item % 2 == 1:
                if (item + 1) // 2 + 1 < spans[part]:
                    @pl.when(goes_up(part))
                    def _():
                        z_copy(part, item, True).start()
            if item == 0 or item % 2 == 0:
                if (item + 1) // 2 + 1 < spans[part]:
                    @pl.when(goes_down(part))
                    def _():
                        z_copy(part, item, False).start()
            b_copy(part, item).start()
            c_copy(part, item, 0).start()

    def relay(part, item):
        @pl.when(valid(part, item))
        def _():
            b_arrived(part, item).wait_recv()
            c_copy(part, item, 1).start()

    for part in range(total):
        launch(part, 0)
    for far in range(1, line + 1):
        for item in (2 * far - 1, 2 * far):
            for part in range(total):
                if far < line and active(part, item):
                    @pl.when(valid(part, item))
                    def _():
                        z_arrived(part, item).wait_recv()

                    launch(part, item)
        last = [0] if far == 1 else [2 * far - 3, 2 * far - 2]
        for item in last:
            for part in range(total):
                if active(part, item):
                    relay(part, item)
    for part in range(total):
        pltpu.make_async_copy(ins[part], view(part, at, side, core), local_sem.at[part]).wait()
        for item in range(items):
            if not active(part, item):
                continue

            @pl.when(valid(part, item))
            def _():
                if (item == 0 or item % 2 == 1) and (item + 1) // 2 + 1 < spans[part]:
                    @pl.when(goes_up(part))
                    def _():
                        z_copy(part, item, True).wait_send()
                if (item == 0 or item % 2 == 0) and (item + 1) // 2 + 1 < spans[part]:
                    @pl.when(goes_down(part))
                    def _():
                        z_copy(part, item, False).wait_send()
                b_copy(part, item).wait_send()
                c_copy(part, item, 0).wait_send()
                c_copy(part, item, 1).wait_send()
                c_arrived(part, item, 0).wait_recv()
                c_arrived(part, item, 1).wait_recv()


def spread(blocks, out_shapes, pieces, collective_id):
    count = lax.axis_size("seq")
    total = len(pieces)
    items = 2 * (count // 4) + 1
    sem = pltpu.SemaphoreType.DMA
    return pl.pallas_call(
        functools.partial(spread_kernel, (len(blocks), len(out_shapes), pieces), count),
        out_shape=out_shapes,
        in_specs=[pl.BlockSpec(memory_space=VMEM)] * len(blocks),
        out_specs=[pl.BlockSpec(memory_space=pl.ANY)] * len(out_shapes),
        scratch_shapes=[sem((total,))] + [sem((total, items))] * 4 + [sem((total, 2 * items))] * 2,
        compiler_params=pltpu.CompilerParams(collective_id=collective_id, has_side_effects=True),
    )(*blocks)


def fold_kernel(parts, count, *refs):
    given, wanted, pieces = parts
    total = len(pieces)
    spans = [piece[0] for piece in pieces]
    x_refs, o_refs = refs[:given], refs[given : given + wanted]
    scratch = refs[given + wanted :]
    outs = [piece[3](o_refs) for piece in pieces]
    c_bufs, s_bufs, b_bufs, u_bufs, d_bufs, t_bufs = (
        scratch[i * total : (i + 1) * total] for i in range(6)
    )
    c_send, c_recv, b_send, b_recv, u_send, u_recv, d_send, d_recv = scratch[6 * total :]
    line = count // 4
    group = lax.axis_index("dp")
    at, side, core = place(lax.axis_index("seq"))
    peers = line_peers(at, side, core, group, line)
    below, above, beside, sibling = (peer for _, peer in peers)
    meet(peers)

    def remote(src, dst, send, recv, peer):
        return pltpu.make_async_remote_copy(
            src_ref=src, dst_ref=dst, send_sem=send, recv_sem=recv, device_id=peer, device_id_type=MESH
        )

    def view(part, where, which_side, which_core):
        return pieces[part][2](x_refs, 4 * where + 2 * which_side + which_core)

    def valid(part, where):
        low = at // spans[part] * spans[part]
        return (where >= low) & (where < low + spans[part])

    def slot(part, where):
        return lax.rem(where, spans[part])

    order = []
    for far in range(line - 1, 0, -1):
        order += [(far, 1), (far, -1)]
    order.append((0, 1))

    def c_copy(part, where, other):
        which = 1 - side if other else side
        index = 2 * slot(part, where) + other
        return remote(
            view(part, where, which, 1 - core),
            c_bufs[part].at[index],
            c_send.at[part, index],
            c_recv.at[part, index],
            sibling,
        )

    def b_copy(part, where):
        index = slot(part, where)
        return remote(
            s_bufs[part].at[index], b_bufs[part].at[index], b_send.at[part, index], b_recv.at[part, index], beside
        )

    def u_copy(part, where):
        index = slot(part, where)
        return remote(
            t_bufs[part].at[index], u_bufs[part].at[index], u_send.at[part, index], u_recv.at[part, index], above
        )

    def d_copy(part, where):
        index = slot(part, where)
        return remote(
            t_bufs[part].at[index], d_bufs[part].at[index], d_send.at[part, index], d_recv.at[part, index], below
        )

    def each(action):
        for far, sign in order:
            for part in range(total):
                if far >= spans[part]:
                    continue
                where = at + sign * far

                @pl.when(valid(part, where))
                def _():
                    action(part, where, far, sign)

    each(lambda part, where, far, sign: c_copy(part, where, 1).start())
    each(lambda part, where, far, sign: c_copy(part, where, 0).start())

    def aside(part, where, far, sign):
        c_copy(part, where, 1).wait_recv()
        index = slot(part, where)
        mine = view(part, where, 1 - side, core)[...]
        s_bufs[part][index] = (
            mine.astype(F32) + c_bufs[part][2 * index + 1].astype(F32)
        ).astype(BF)
        b_copy(part, where).start()

    each(aside)

    def along(part, where, far, sign):
        c_copy(part, where, 0).wait_recv()
        b_copy(part, where).wait_recv()
        index = slot(part, where)
        here = slot(part, at)
        value = (
            view(part, where, side, core)[...].astype(F32)
            + c_bufs[part][2 * index].astype(F32)
            + b_bufs[part][index].astype(F32)
        )
        if far == 0:
            outs[part][...] = value

            @pl.when(here > 0)
            def _():
                u_copy(part, where).wait_recv()
                outs[part][...] += u_bufs[part][index].astype(F32)

            @pl.when(here < spans[part] - 1)
            def _():
                d_copy(part, where).wait_recv()
                outs[part][...] += d_bufs[part][index].astype(F32)
        elif sign > 0:
            t_bufs[part][index] = value.astype(BF)

            @pl.when(here > 0)
            def _():
                u_copy(part, where).wait_recv()
                t_bufs[part][index] = (value + u_bufs[part][index].astype(F32)).astype(BF)

            u_copy(part, where).start()
        else:
            t_bufs[part][index] = value.astype(BF)

            @pl.when(here < spans[part] - 1)
            def _():
                d_copy(part, where).wait_recv()
                t_bufs[part][index] = (value + d_bufs[part][index].astype(F32)).astype(BF)

            d_copy(part, where).start()

    each(along)

    def finish(part, where, far, sign):
        c_copy(part, where, 0).wait_send()
        c_copy(part, where, 1).wait_send()
        b_copy(part, where).wait_send()
        if far > 0:
            (u_copy if sign > 0 else d_copy)(part, where).wait_send()

    each(finish)


def fold(arrays, out_shapes, pieces, collective_id):
    count = lax.axis_size("seq")
    total = len(pieces)
    sem = pltpu.SemaphoreType.DMA
    line = count // 4
    bufs = []
    for times in (2, 1, 1, 1, 1, 1):
        bufs += [VMEM((times * piece[0],) + piece[1], BF) for piece in pieces]
    return pl.pallas_call(
        functools.partial(fold_kernel, (len(arrays), len(out_shapes), pieces), count),
        out_shape=[jax.ShapeDtypeStruct(shape, F32) for shape in out_shapes],
        in_specs=[pl.BlockSpec(memory_space=VMEM)] * len(arrays),
        out_specs=[pl.BlockSpec(memory_space=VMEM)] * len(out_shapes),
        scratch_shapes=bufs + [sem((total, 2 * line))] * 2 + [sem((total, line))] * 6,
        compiler_params=pltpu.CompilerParams(
            collective_id=collective_id, has_side_effects=True, vmem_limit_bytes=60 * 2**20
        ),
    )(*arrays)


def exchange_kernel(x_ref, own_ref, other_ref, own_sem, z_send, z_recv, x_send, x_recv, y_send, y_recv, c_send, c_recv):
    count = own_ref.shape[0]
    line = count // 4
    group = lax.axis_index("dp")
    me = lax.axis_index("seq")
    at, side, core = place(me)
    peers = line_peers(at, side, core, group, line)
    below, above, beside, sibling = (peer for _, peer in peers)
    across = (1 - group, me)
    meet(peers + [(at >= 0, across)])

    def remote(src, dst, send, recv, index, peer):
        return pltpu.make_async_remote_copy(
            src_ref=src, dst_ref=dst, send_sem=send.at[index], recv_sem=recv.at[index],
            device_id=peer, device_id_type=MESH,
        )

    items = [(0, 0)] + [(far, turn) for far in range(1, line) for turn in range(2)]

    def where_of(item):
        return at + item[0] * (2 * item[1] - 1)

    def number(item):
        return 2 * item[0] + item[1]

    def given(item, action):
        @pl.when((where_of(item) >= 0) & (where_of(item) < line))
        def _():
            action()

    def spot(item, other_group, other_side, other_core):
        ref = other_ref if other_group else own_ref
        s = 1 - side if other_side else side
        c = 1 - core if other_core else core
        return ref.at[4 * where_of(item) + 2 * s + c]

    def here(item, other_group, other_side):
        if item == (0, 0) and not other_group and not other_side:
            return x_ref
        return spot(item, other_group, other_side, False)

    def z_copy(item, turn, peer):
        far = (item[0] + 1, turn)
        return remote(here(item, 0, 0), spot(item, 0, 0, 0), z_send, z_recv, number(far), peer)

    def side_copy(item, other_group, arrived):
        dst = spot(item, other_group, arrived, 0)
        src = dst if arrived else here(item, other_group, 0)
        return remote(src, dst, x_send, x_recv, 2 * number(item) + other_group, beside)

    def cross_copy(item, other_side, arrived):
        dst = spot(item, 1, other_side, 0)
        src = dst if arrived else here(item, 0, other_side)
        return remote(src, dst, y_send, y_recv, 2 * number(item) + other_side, across)

    def core_copy(item, other_group, other_side, arrived):
        dst = spot(item, other_group, other_side, arrived)
        src = dst if arrived else here(item, other_group, other_side)
        index = 4 * number(item) + 2 * other_group + other_side
        return remote(src, dst, c_send, c_recv, index, sibling)

    def by_side(item):
        return lax.rem(where_of(item), 2) == 0

    def z_links(item, act):
        far, turn = item
        if far + 1 < line:
            if far == 0 or turn == 0:

                @pl.when(at + 1 < line)
                def _():
                    act(z_copy(item, 0, above))

            if far == 0 or turn == 1:

                @pl.when(at > 0)
                def _():
                    act(z_copy(item, 1, below))

    def start(copy):
        copy.start()

    def launch(item):
        z_links(item, start)
        side_copy(item, 0, False).start()
        cross_copy(item, 0, False).start()
        core_copy(item, 0, 0, False).start()

    def first(item):
        z = remote(spot(item, 0, 0, 0), spot(item, 0, 0, 0), z_send, z_recv, number(item), beside)
        z.wait_recv()
        launch(item)

    def second(item):
        side_copy(item, 0, True).wait_recv()
        core_copy(item, 0, 1, False).start()
        cross_copy(item, 0, True).wait_recv()
        core_copy(item, 1, 0, False).start()

    def diagonal(item):
        @pl.when(by_side(item))
        def _():
            side_copy(item, 1, False).start()

        @pl.when(jnp.logical_not(by_side(item)))
        def _():
            cross_copy(item, 1, False).start()

    def third(item):
        @pl.when(by_side(item))
        def _():
            side_copy(item, 1, True).wait_recv()

        @pl.when(jnp.logical_not(by_side(item)))
        def _():
            cross_copy(item, 1, True).wait_recv()

        core_copy(item, 1, 1, False).start()

    def at_far(far):
        return [item for item in items if item[0] == far]

    own = pltpu.make_async_copy(x_ref, spot((0, 0), 0, 0, 0), own_sem.at[0])
    own.start()
    launch((0, 0))
    for step in range(1, line + 1):
        for item in at_far(step):
            given(item, functools.partial(first, item))
        for item in at_far(step - 1):
            given(item, functools.partial(second, item))
        if step >= line - 1:
            for far in range(line - 1) if step == line - 1 else [line - 1]:
                for item in at_far(far):
                    given(item, functools.partial(diagonal, item))
    for item in items:
        given(item, functools.partial(third, item))
    own.wait()

    def finish(item):
        z_links(item, lambda copy: copy.wait_send())
        side_copy(item, 0, False).wait_send()
        cross_copy(item, 0, False).wait_send()

        @pl.when(by_side(item))
        def _():
            side_copy(item, 1, False).wait_send()

        @pl.when(jnp.logical_not(by_side(item)))
        def _():
            cross_copy(item, 1, False).wait_send()

        for other_group in range(2):
            for other_side in range(2):
                core_copy(item, other_group, other_side, False).wait_send()
                core_copy(item, other_group, other_side, True).wait_recv()

    for item in items:
        given(item, functools.partial(finish, item))


def exchange(x, collective_id):
    count = lax.axis_size("seq")
    marks = 2 * (count // 4) + 2
    sem = pltpu.SemaphoreType.DMA
    return pl.pallas_call(
        exchange_kernel,
        out_shape=[jax.ShapeDtypeStruct((count,) + x.shape, x.dtype)] * 2,
        in_specs=[pl.BlockSpec(memory_space=VMEM)],
        out_specs=[pl.BlockSpec(memory_space=pl.ANY)] * 2,
        scratch_shapes=[sem((1,))] + [sem((marks,))] * 2 + [sem((2 * marks,))] * 4 + [sem((4 * marks,))] * 2,
        compiler_params=pltpu.CompilerParams(collective_id=collective_id, has_side_effects=True),
    )(x)


def row_gather(line, rows, cuts):
    size = rows // cuts
    return tuple(
        (
            line,
            lambda x, h=h: x[0].at[pl.ds(h * size, size)],
            lambda o, q, h=h: o[0].at[q, pl.ds(h * size, size)],
        )
        for h in range(cuts)
    )


def row_pieces(line, rows, width, cuts):
    size = rows // cuts
    return tuple(
        (
            line,
            (size, width),
            lambda x, q, h=h: x[0].at[q, pl.ds(h * size, size)],
            lambda o, h=h: o[0].at[pl.ds(h * size, size)],
        )
        for h in range(cuts)
    )


def turned_kernel(l_ref, r_ref, o_ref):
    o_ref[...] = contract(l_ref[...], r_ref[...], 0, 0).astype(BF)


def turned_product(left, right, block):
    depth, rows = left.shape
    width = right.shape[1]
    return pl.pallas_call(
        turned_kernel,
        grid=(rows // block,),
        out_shape=jax.ShapeDtypeStruct((rows, width), BF),
        in_specs=[
            pl.BlockSpec((depth, block), lambda i: (0, i)),
            pl.BlockSpec((depth, width), lambda i: (0, 0)),
        ],
        out_specs=pl.BlockSpec((block, width), lambda i: (i, 0)),
    )(left, right)


def visible_rows(kind, run_devs, rows_dev, half, q):
    first = half + rows_dev * lax.rem(q, run_devs) if kind else rows_dev * q
    return pl.multiple_of(first, 32)


def visible_gather(line, run_devs, rows_dev, half):
    size = rows_dev // 2
    return tuple(
        (
            run_devs // 4 if kind else line,
            lambda x, m=m, kind=kind, j=j: x[0].at[m, kind, pl.ds(size * j, size)],
            lambda o, q, m=m, kind=kind, j=j: o[0].at[
                m, pl.ds(visible_rows(kind, run_devs, rows_dev, half, q) + size * j, size)
            ],
        )
        for kind in range(2)
        for m in range(MB)
        for j in range(2)
    )


def visible_sum(line, run_devs, rows_dev, half, width):
    return tuple(
        (
            run_devs // 4 if kind else line,
            (MB, rows_dev, width),
            lambda x, q, kind=kind: x[0].at[
                :, pl.ds(visible_rows(kind, run_devs, rows_dev, half, q), rows_dev)
            ],
            lambda o, kind=kind: o[0].at[:, kind],
        )
        for kind in range(2)
    )


def place_kernel(l_ref, r_ref, *refs):
    refs[-1][...] = jnp.dot(l_ref[...], r_ref[...], preferred_element_type=F32).astype(BF)


def place_product(buffer, left, right, first, rows):
    depth, width = right.shape
    block = width // 2
    given = () if buffer is None else (buffer,)
    return pl.pallas_call(
        place_kernel,
        grid=(left.shape[0] // block,),
        out_shape=jax.ShapeDtypeStruct((rows, width), BF),
        in_specs=[
            pl.BlockSpec((block, depth), lambda i: (i, 0)),
            pl.BlockSpec((depth, width), lambda i: (0, 0)),
        ]
        + [pl.BlockSpec(memory_space=pl.ANY)] * len(given),
        out_specs=pl.BlockSpec((block, width), lambda i: (first // block + i, 0)),
        input_output_aliases={2: 0} if given else {},
    )(left, right, *given)


def contract(left, right, left_dim, right_dim):
    return lax.dot_general(
        left, right, (((left_dim,), (right_dim,)), ((), ())), preferred_element_type=F32
    )


def norm_forward(values, gain, bias):
    centred = values - jnp.mean(values, axis=-1, keepdims=True)
    inverse = lax.rsqrt(jnp.mean(centred * centred, axis=-1, keepdims=True) + EPS_NORM)
    unit = centred * inverse
    return (unit * gain + bias, unit, inverse)


def norm_backward(upstream, unit, inverse, gain):
    scaled = upstream * gain
    inner = (
        scaled
        - jnp.mean(scaled, axis=-1, keepdims=True)
        - unit * jnp.mean(scaled * unit, axis=-1, keepdims=True)
    )
    return (inverse * inner, jnp.sum(upstream * unit, axis=0), jnp.sum(upstream, axis=0))


def head_probs(pos_ref, q, k):
    scores = contract(q, k, 0, 0) * HD ** (-0.5)
    key_pos = lax.broadcasted_iota(jnp.int32, scores.shape, 1)
    scores = jnp.where(key_pos <= pos_ref[...], scores, MASKED)
    shifted = jnp.exp(scores - jnp.max(scores, axis=1, keepdims=True))
    return shifted * (1.0 / jnp.sum(shifted, axis=1, keepdims=True))


def attend_kernel(pos_ref, q_ref, kv_ref, o_ref):
    probs = head_probs(pos_ref, q_ref[...], kv_ref[0]).astype(BF)
    o_ref[...] = contract(kv_ref[1], probs, 1, 1).astype(BF)


def attend_back_kernel(pos_ref, q_ref, kv_ref, g_ref, dq_ref, dkv_ref):
    q, k, v, g = q_ref[...], kv_ref[0], kv_ref[1], g_ref[...]
    probs = head_probs(pos_ref, q, k)
    grad = contract(g, v, 0, 0)
    back = (probs * (grad - jnp.sum(probs * grad, axis=1, keepdims=True))).astype(BF)
    scale = HD ** (-0.5)
    dq_ref[...] = (contract(k, back, 1, 1) * scale).astype(BF)
    dkv_ref[0] = (contract(q, back, 1, 0) * scale).astype(BF)
    dkv_ref[1] = contract(g, probs.astype(BF), 1, 0).astype(BF)


def attend(query_pos, q, kv):
    rows, keys = query_pos.shape[0], kv.shape[2] * query_pos.shape[0] // q.shape[1]
    small = pl.BlockSpec((HD, rows), lambda m, h: (h, m))
    large = pl.BlockSpec((2, HD, keys), lambda m, h: (0, h, m))
    return pl.pallas_call(
        attend_kernel,
        grid=(q.shape[1] // rows, HEADS),
        out_shape=jax.ShapeDtypeStruct(q.shape, BF),
        in_specs=[pl.BlockSpec((rows, 1), lambda m, h: (0, 0)), small, large],
        out_specs=small,
    )(query_pos, q, kv)


def attend_back(query_pos, q, kv, grad_out):
    rows, keys = query_pos.shape[0], kv.shape[2] * query_pos.shape[0] // q.shape[1]
    small = pl.BlockSpec((HD, rows), lambda m, h: (h, m))
    large = pl.BlockSpec((2, HD, keys), lambda m, h: (0, h, m))
    return pl.pallas_call(
        attend_back_kernel,
        grid=(q.shape[1] // rows, HEADS),
        out_shape=[jax.ShapeDtypeStruct(q.shape, BF), jax.ShapeDtypeStruct(kv.shape, BF)],
        in_specs=[pl.BlockSpec((rows, 1), lambda m, h: (0, 0)), small, large, small],
        out_specs=[small, large],
    )(query_pos, q, kv, grad_out)


def lookup_kernel(first_ref, slot_ref, table_ref, *refs):
    slots = slot_ref[...] - first_ref[0]
    ids = lax.broadcasted_iota(jnp.int32, (slots.shape[0], table_ref.shape[1]), 1)
    rows = contract(jnp.where(slots == ids, 1.0, 0.0).astype(BF), table_ref[...], 1, 1).astype(BF)
    refs[-1][...] = rows if len(refs) == 1 else refs[0][...] + rows


def lookup(first, slots, table, others, block):
    width, held = table.shape
    rows = pl.BlockSpec((block, width), lambda i: (i, 0))
    given = () if others is None else (others,)
    return pl.pallas_call(
        lookup_kernel,
        grid=(slots.shape[0] // block,),
        out_shape=jax.ShapeDtypeStruct((slots.shape[0], width), BF),
        in_specs=[
            pl.BlockSpec(memory_space=pltpu.SMEM),
            pl.BlockSpec((block, 1), lambda i: (i, 0)),
            pl.BlockSpec((width, held), lambda i: (0, 0)),
        ]
        + [rows] * len(given),
        out_specs=rows,
    )(first, slots, table, *given)


def adamw(weight, moment_a, moment_b, gradient, rate, decay):
    moment_a = MOMENT_ONE * moment_a + (1.0 - MOMENT_ONE) * gradient
    moment_b = MOMENT_TWO * moment_b + (1.0 - MOMENT_TWO) * gradient * gradient
    update = (
        moment_a
        / (1.0 - MOMENT_ONE**STEP)
        / (jnp.sqrt(moment_b / (1.0 - MOMENT_TWO**STEP)) + EPS_ADAM)
    )
    weight = weight - rate * (update + decay * weight)
    return (weight, moment_a, moment_b, weight.astype(BF))


def on_device(
    tokens,
    targets,
    counted,
    cont_label,
    pair_map,
    ref_logp,
    vocab_slot,
    embed_table,
    embed_first,
    embed_second,
    layer_weights,
    layer_first,
    layer_second,
    norm_params,
    norm_first,
    norm_second,
):
    seq_count = lax.axis_size("seq")
    group_count = lax.axis_size("dp")
    all_count = seq_count * group_count
    seq_rank = lax.axis_index("seq")
    group_rank = lax.axis_index("dp")
    device_rank = group_rank * seq_count + seq_rank
    rows_dev = tokens.shape[3]
    half = rows_dev * seq_count
    vocab_dev, width = embed_table.shape
    run_count = half // CLEN
    run_devs = CLEN // rows_dev
    own_rows = MB * 2 * rows_dev

    table_t = embed_table.T
    norm_dev = norm_params.shape[0]
    norm_parts = [norm_params]
    for step in range(1, group_count):
        norm_parts.append(
            lax.ppermute(
                norm_params, "dp", [(i, (i - step) % group_count) for i in range(group_count)]
            )
        )
    sent, *norm_parts = lax.optimization_barrier((table_t.astype(BF), *norm_parts))
    norm_all = jnp.zeros((group_count, norm_dev), F32)
    for step in range(group_count):
        norm_all = lax.dynamic_update_index_in_dim(
            norm_all, norm_parts[step], lax.rem(group_rank + step, group_count), 0
        )
    slab_t = [sent]
    for step in range(1, group_count):
        slab_t.append(
            lax.ppermute(
                slab_t[0], "dp", [(i, (i - step) % group_count) for i in range(group_count)]
            )
        )
    weights = lax.all_gather(
        layer_weights.T.astype(BF)[None], ("dp", "seq"), axis=0, tiled=True
    ).reshape(-1, width)
    w_q = weights[:width]
    w_o = weights[3 * width : 4 * width]
    w_kv = weights[width : 3 * width]
    w_up = weights[4 * width : 4 * width + FF]
    w_dn = weights[4 * width + FF :]

    marks = counted[:, 0]
    spots = jnp.arange(rows_dev, dtype=jnp.int32)
    ranks = (
        jnp.sum(jnp.where(spots[None, :, None] <= spots[None, None, :], marks[:, :, None], 0), axis=1)
        - 1
    )
    pick_ids = jnp.arange(PICK, dtype=jnp.int32)
    pick_hit = (ranks[:, None, :] == pick_ids[None, :, None]) & (marks[:, None, :] == 1)
    pick_targets = jnp.sum(jnp.where(pick_hit, targets[:, 0][:, None, :], 0), axis=2)
    pick_low = pick_hit.astype(BF)
    slots = vocab_slot[jnp.concatenate([tokens[:, 0].reshape(-1), pick_targets.reshape(-1)])]
    small = jnp.concatenate([slots.astype(F32), norm_all.reshape(-1)])
    small = jnp.pad(small, (0, -small.shape[0] % 1024)).reshape(-1, 128)
    small_all = direct_gather(small, False, 1).reshape(seq_count, -1)
    slots_all = small_all[:, : own_rows + MB * PICK].astype(jnp.int32)
    gains = (
        small_all[:, own_rows + MB * PICK :][:, : group_count * norm_dev]
        .reshape(seq_count, group_count, norm_dev)
        .transpose(1, 0, 2)
        .astype(BF)
        .astype(F32)
        .reshape(6, width)
    )
    row_slots = slots_all[:, :own_rows].reshape(-1)
    target_slots = slots_all[:, own_rows:].reshape(-1)
    vocab_ids = jnp.arange(vocab_dev, dtype=jnp.int32)

    def hits(slot_ids, step):
        part = lax.rem(group_rank + step, group_count)
        first = (part * seq_count + seq_rank) * vocab_dev
        return (slot_ids - first)[:, None] == vocab_ids[None, :]

    partial = None
    for step in range(group_count):
        part = lax.rem(group_rank + step, group_count)
        first = (part * seq_count + seq_rank) * vocab_dev
        partial = lookup(first[None], row_slots[:, None], slab_t[step], partial, own_rows)
    line = seq_count // 4
    (stream,) = fold(
        [partial.reshape(seq_count, own_rows, width)],
        [(own_rows, width)],
        row_pieces(line, own_rows, width, 2),
        2,
    )

    normed, unit_one, inverse_one = norm_forward(stream, gains[0], gains[3])
    hidden_one = normed.astype(BF)
    run_dev = seq_rank // run_devs * run_devs
    key_rows = half + CLEN
    (hidden_sel,) = spread(
        [hidden_one.reshape(MB, 2, rows_dev, width)],
        [jax.ShapeDtypeStruct((MB, key_rows, width), BF)],
        visible_gather(line, run_devs, rows_dev, half),
        3,
    )
    hidden_sel = hidden_sel.reshape(MB * key_rows, width)
    pairs = contract(w_kv, hidden_sel, 1, 1).astype(BF).reshape(2, width, MB * key_rows)
    queries = contract(w_q, hidden_one, 1, 1).astype(BF)
    start = seq_rank * rows_dev
    query_pos = jnp.concatenate([start + spots, half + (start - run_dev * rows_dev) + spots])[:, None]
    attended = attend(query_pos, queries, pairs)
    stream_one = stream + contract(attended, w_o, 0, 0)
    normed, unit_two, inverse_two = norm_forward(stream_one, gains[1], gains[4])
    hidden_two = normed.astype(BF)
    up_proj = contract(w_up, hidden_two, 1, 1)
    activated = jax.nn.gelu(up_proj, approximate=False).astype(BF)
    stream_two = stream_one + contract(activated, w_dn, 0, 0)
    normed, unit_final, inverse_final = norm_forward(stream_two, gains[2], gains[5])
    final = normed.astype(BF).reshape(MB, 2, rows_dev, width)[:, 1]
    picked = jnp.einsum("mpr,mrd->mpd", pick_low, final, preferred_element_type=F32).astype(BF)

    (head_rows,) = spread(
        [picked.reshape(MB * PICK, width)],
        [jax.ShapeDtypeStruct((seq_count, MB * PICK, width), BF)],
        row_gather(line, MB * PICK, 1),
        4,
    )
    head_rows = head_rows.reshape(seq_count * MB * PICK, width)
    logits = [contract(head_rows, slab_t[part], 1, 0) for part in range(group_count)]
    target_hits = [hits(target_slots, part) for part in range(group_count)]
    highest = jnp.max(logits[0], axis=1)
    for part in range(1, group_count):
        highest = jnp.maximum(highest, jnp.max(logits[part], axis=1))
    summed = jnp.zeros_like(highest)
    target_logit = jnp.zeros_like(highest)
    for part in range(group_count):
        summed = summed + jnp.sum(jnp.exp(logits[part] - highest[:, None]), axis=1)
        target_logit = target_logit + jnp.sum(jnp.where(target_hits[part], logits[part], 0.0), axis=1)
    stats = direct_gather(
        jnp.stack([highest, summed, target_logit]).reshape(-1, 128), False, 5
    ).reshape(seq_count, 3, -1)
    overall = jnp.max(stats[:, 0], axis=0)
    total = jnp.sum(stats[:, 1] * jnp.exp(stats[:, 0] - overall[None]), axis=0)
    log_total = overall + jnp.log(total)
    token_lp = jnp.sum(stats[:, 2], axis=0) - log_total

    run_ids = jnp.arange(run_count, dtype=jnp.int32)
    run_of_dev = jnp.arange(seq_count, dtype=jnp.int32) * rows_dev // CLEN
    run_match = run_of_dev[:, None] == run_ids[None, :]
    dev_lp = jnp.sum(token_lp.reshape(seq_count, MB, PICK), axis=2)
    run_lp = jnp.sum(jnp.where(run_match[:, None, :], dev_lp[:, :, None], 0.0), axis=0)
    labels = lax.dynamic_index_in_dim(cont_label, group_rank, 1, keepdims=False)
    pairing = lax.dynamic_index_in_dim(pair_map, group_rank, 1, keepdims=False)
    reference_lp = lax.dynamic_index_in_dim(ref_logp, group_rank, 1, keepdims=False)
    label_match = labels[:, :, None] == run_ids[None, None, :]
    label_lp = jnp.sum(jnp.where(label_match, run_lp[:, :, None], 0.0), axis=1)
    margin = label_lp - reference_lp
    chosen = pairing[:, 0::2, None] == run_ids[None, None, :]
    rejected = pairing[:, 1::2, None] == run_ids[None, None, :]
    delta = jnp.sum(jnp.where(chosen, margin[:, None, :], 0.0), axis=2) - jnp.sum(
        jnp.where(rejected, margin[:, None, :], 0.0), axis=2
    )
    loss = jnp.sum(jax.nn.softplus(-DPO_BETA * delta))
    pair_grad = -DPO_BETA * jax.nn.sigmoid(-DPO_BETA * delta)
    label_grad = jnp.sum(
        jnp.where(chosen, pair_grad[:, :, None], 0.0)
        - jnp.where(rejected, pair_grad[:, :, None], 0.0),
        axis=1,
    )
    run_grad = jnp.sum(jnp.where(label_match, label_grad[:, None, :], 0.0), axis=2)
    dev_grad = jnp.sum(jnp.where(run_match[:, None, :], run_grad[None], 0.0), axis=2)
    row_grad = jnp.broadcast_to(dev_grad[:, :, None], (seq_count, MB, PICK)).reshape(-1)

    head_back = 0.0
    logit_grads = []
    for part in range(group_count):
        logit_grad = (
            row_grad[:, None]
            * (target_hits[part].astype(F32) - jnp.exp(logits[part] - log_total[:, None]))
        ).astype(BF)
        logit_grads.append(logit_grad)
        head_back = head_back + contract(logit_grad, slab_t[part], 1, 1)
    head_back = head_back.astype(BF)
    moved = [(i, (i + 1) % group_count) for i in range(group_count)]
    if group_count == 2:
        head_back, head_part = lax.optimization_barrier(
            (head_back, contract(head_rows, logit_grads[1], 0, 0).astype(BF))
        )
        head_other = lax.ppermute(head_part, "dp", moved)
    (row_back,) = fold(
        [head_back.reshape(seq_count, MB * PICK, width)],
        [(MB * PICK, width)],
        row_pieces(line, MB * PICK, width, 1),
        6,
    )
    row_back = row_back.astype(BF).reshape(MB, PICK, width)
    cont_back = jnp.einsum("mpr,mpd->mrd", pick_low, row_back, preferred_element_type=F32)
    upstream = jnp.concatenate(
        [jnp.zeros((MB, 1, rows_dev, width), F32), cont_back[:, None]], axis=1
    ).reshape(own_rows, width)

    grad_two, gain_final, bias_final = norm_backward(upstream, unit_final, inverse_final, gains[2])
    grad_ffn = grad_two.astype(BF)
    columns = weights.shape[0]
    weight_grad = place_product(None, activated, grad_ffn, 4 * width + FF, columns)
    grad_act = contract(w_dn, grad_ffn, 1, 1)
    _, gelu_pull = jax.vjp(lambda pre_act: jax.nn.gelu(pre_act, approximate=False), up_proj)
    grad_up = gelu_pull(grad_act)[0].astype(BF)
    weight_grad = place_product(weight_grad, grad_up, hidden_two, 4 * width, columns)
    grad_hidden = contract(grad_up, w_up, 0, 0)
    grad_mid, gain_two, bias_two = norm_backward(grad_hidden, unit_two, inverse_two, gains[1])
    grad_one = grad_two + grad_mid
    grad_branch = grad_one.astype(BF)
    weight_grad = place_product(weight_grad, attended, grad_branch, 3 * width, columns)
    grad_attended = contract(w_o, grad_branch, 1, 1).astype(BF)
    grad_query, grad_pairs = attend_back(query_pos, queries, pairs, grad_attended)
    if group_count == 2:
        grad_query, head_other = lax.optimization_barrier((grad_query, head_other))
    grad_pairs = grad_pairs.reshape(2 * width, MB * key_rows)
    weight_grad = place_product(weight_grad, grad_query, hidden_one, 0, columns)
    weight_grad = place_product(weight_grad, grad_pairs, hidden_sel, width, columns)
    low_sel = turned_product(grad_pairs, w_kv, 2 * 2 * rows_dev).reshape(MB, key_rows, width)
    weight_sum = lax.psum_scatter(
        weight_grad.reshape(all_count, -1, width), ("dp", "seq"), scatter_dimension=0, tiled=True
    )[0].astype(F32)
    (low_own,) = fold(
        [low_sel],
        [(MB, 2, rows_dev, width)],
        visible_sum(line, run_devs, rows_dev, half, width),
        7,
    )
    grad_low = low_own.reshape(own_rows, width) + contract(grad_query, w_q, 0, 0)
    grad_first, gain_one, bias_one = norm_backward(grad_low, unit_one, inverse_one, gains[0])
    norm_rows = jnp.stack([gain_one, gain_two, gain_final, bias_one, bias_two, bias_final])
    if group_count == 2:
        head_own = contract(head_rows, logit_grads[0], 0, 0)
        pad_rows = 8
        own_grads, other_grads = exchange(
            jnp.concatenate(
                [grad_one + grad_first, norm_rows, jnp.zeros((pad_rows - 6, width), F32)]
            ).astype(BF),
            8,
        )
        other_slots = lax.ppermute(row_slots, "dp", moved)
        embed_sum = lax.optimization_barrier(head_own + head_other.astype(F32))
        norm_all = 0.0
        for grads, part_slots in ((own_grads, row_slots), (other_grads, other_slots)):
            part_slots = jnp.pad(
                part_slots.reshape(seq_count, own_rows), ((0, 0), (0, pad_rows)), constant_values=-1
            ).reshape(-1)
            embed_sum = embed_sum + contract(
                grads.reshape(-1, width), hits(part_slots, 0).astype(BF), 0, 0
            )
            norm_all = norm_all + jnp.sum(
                grads[:, own_rows : own_rows + 6].astype(F32), axis=0
            )
    else:
        row_grads, norm_grads = spread(
            [
                (grad_one + grad_first).astype(BF),
                jnp.concatenate([norm_rows, jnp.zeros((10, width), F32)]).astype(BF),
            ],
            [
                jax.ShapeDtypeStruct((seq_count, own_rows, width), BF),
                jax.ShapeDtypeStruct((seq_count, 16, width), BF),
            ],
            row_gather(line, own_rows, 2)
            + ((line, lambda x: x[1], lambda o, q: o[1].at[q]),),
            8,
        )
        row_grads = row_grads.reshape(-1, width)
        norm_sum = jnp.sum(norm_grads[:, :6].astype(F32), axis=0)
        norm_all = norm_sum
        for step in range(1, group_count):
            norm_all = norm_all + lax.ppermute(
                norm_sum, "dp", [(i, (i + step) % group_count) for i in range(group_count)]
            )

        def table_grad(step):
            return contract(head_rows, logit_grads[step], 0, 0) + contract(
                row_grads, hits(row_slots, step).astype(BF), 0, 0
            )

        arrived = [
            lax.ppermute(
                table_grad(step).astype(BF),
                "dp",
                [(i, (i + step) % group_count) for i in range(group_count)],
            )
            for step in range(1, group_count)
        ]
        embed_sum = table_grad(0)
        for block in arrived:
            embed_sum = embed_sum + block.astype(F32)
    norm_own = lax.dynamic_slice_in_dim(norm_all.reshape(-1), device_rank * norm_dev, norm_dev, 0)
    squares = (
        jnp.sum(embed_sum * embed_sum)
        + jnp.sum(weight_sum * weight_sum)
        + jnp.sum(norm_own * norm_own)
    )
    lanes = lax.broadcasted_iota(jnp.int32, (8, 128), 1)
    scalars = direct_gather(
        jnp.where(lanes == 0, squares, jnp.where(lanes == 1, loss, 0.0)), True, 9
    )
    square_total = jnp.sum(scalars[:, 0, 0])
    loss_total = jnp.sum(scalars[::seq_count, 0, 1])
    grad_norm = jnp.sqrt(square_total)
    factor = jnp.minimum(1.0, CLIP_NORM / grad_norm)
    embed_out = adamw(
        table_t, embed_first.T, embed_second.T, embed_sum * factor, LEARN_RATE, WEIGHT_DECAY
    )
    layer_out = adamw(
        layer_weights.T,
        layer_first.T,
        layer_second.T,
        weight_sum * factor,
        LEARN_RATE,
        WEIGHT_DECAY,
    )
    norm_out = adamw(norm_params, norm_first, norm_second, norm_own * factor, NORM_RATE, 0.0)
    return (
        embed_out[0].T,
        embed_out[1].T,
        embed_out[2].T,
        embed_out[3].T,
        layer_out[0].T,
        layer_out[1].T,
        layer_out[2].T,
        layer_out[3].T,
        norm_out[0],
        norm_out[1],
        norm_out[2],
        norm_out[3],
        grad_norm,
        loss_total,
    )


def solution(mesh):
    return jax.shard_map(
        on_device,
        mesh=mesh,
        in_specs=(
            P(None, "dp", None, "seq"),
            P(None, "dp", "seq"),
            P(None, "dp", "seq"),
            P(),
            P(),
            P(),
            P(),
            P(("dp", "seq"), None),
            P(("dp", "seq"), None),
            P(("dp", "seq"), None),
            P(None, ("dp", "seq")),
            P(None, ("dp", "seq")),
            P(None, ("dp", "seq")),
            P(("dp", "seq")),
            P(("dp", "seq")),
            P(("dp", "seq")),
        ),
        out_specs=(
            P(("dp", "seq"), None),
            P(("dp", "seq"), None),
            P(("dp", "seq"), None),
            P(("dp", "seq"), None),
            P(None, ("dp", "seq")),
            P(None, ("dp", "seq")),
            P(None, ("dp", "seq")),
            P(None, ("dp", "seq")),
            P(("dp", "seq")),
            P(("dp", "seq")),
            P(("dp", "seq")),
            P(("dp", "seq")),
            P(),
            P(),
        ),
        check_vma=False,
    )
```

```python
import functools

import jax
import jax.numpy as jnp
from jax import lax
from jax.experimental import pallas as pl
from jax.experimental.pallas import tpu as pltpu
from jax.sharding import PartitionSpec as P


HEADS = 17
HD = 64
FF = 4352
PICK = 32
CLEN = 512
MB = 2
STEP = 10


EPS_NORM = 1e-05
DPO_BETA = 0.05
CLIP_NORM = 1.0
LEARN_RATE = 0.03
NORM_RATE = 0.4
WEIGHT_DECAY = 0.1
MOMENT_ONE = 0.9
MOMENT_TWO = 0.999
EPS_ADAM = 1e-08
MASKED = -1e30
BF = jnp.bfloat16
F32 = jnp.float32
MESH = pl.DeviceIdType.MESH
VMEM = pltpu.VMEM


def meet(peers):
    barrier = pltpu.get_barrier_semaphore()
    for there, peer in peers:

        @pl.when(there)
        def _():
            pl.semaphore_signal(barrier, inc=1, device_id=peer, device_id_type=MESH)

    pl.semaphore_wait(barrier, sum(jnp.where(there, 1, 0) for there, _ in peers))


def direct_kernel(whole, x_ref, o_ref, send_sem, recv_sem):
    seq_count = lax.axis_size("seq")
    group_rank = lax.axis_index("dp")
    me = lax.axis_index("seq")
    count = o_ref.shape[0]
    if whole:
        me = group_rank * seq_count + me

    def peer(step):
        other = lax.rem(me + step, count)
        if whole:
            return (other // seq_count, lax.rem(other, seq_count))
        return (group_rank, other)

    barrier = pltpu.get_barrier_semaphore()

    def greet(step, carry):
        pl.semaphore_signal(barrier, inc=1, device_id=peer(step), device_id_type=MESH)
        return carry

    lax.fori_loop(1, count, greet, 0)
    o_ref[me] = x_ref[...]
    pl.semaphore_wait(barrier, count - 1)

    def copy(step):
        return pltpu.make_async_remote_copy(
            src_ref=x_ref,
            dst_ref=o_ref.at[me],
            send_sem=send_sem.at[step],
            recv_sem=recv_sem.at[step],
            device_id=peer(step),
            device_id_type=MESH,
        )

    def begin(step, carry):
        copy(step).start()
        return carry

    def finish(step, carry):
        copy(step).wait()
        return carry

    lax.fori_loop(1, count, begin, 0)
    lax.fori_loop(1, count, finish, 0)


def direct_gather(x, whole, collective_id):
    count = lax.axis_size("seq") * (lax.axis_size("dp") if whole else 1)
    return pl.pallas_call(
        functools.partial(direct_kernel, whole),
        out_shape=jax.ShapeDtypeStruct((count,) + x.shape, x.dtype),
        in_specs=[pl.BlockSpec(memory_space=VMEM)],
        out_specs=pl.BlockSpec(memory_space=VMEM),
        scratch_shapes=[pltpu.SemaphoreType.DMA((count,)), pltpu.SemaphoreType.DMA((count,))],
        compiler_params=pltpu.CompilerParams(collective_id=collective_id, has_side_effects=True),
    )(x)


def place(rank):
    return (rank // 4, lax.rem(rank, 4) // 2, lax.rem(rank, 2))


def line_peers(at, side, core, group, line):
    return [
        (at > 0, (group, 4 * (at - 1) + 2 * side + core)),
        (at < line - 1, (group, 4 * (at + 1) + 2 * side + core)),
        (at >= 0, (group, 4 * at + 2 * (1 - side) + core)),
        (at >= 0, (group, 4 * at + 2 * side + 1 - core)),
    ]


def spread_kernel(parts, count, *refs):
    given, wanted, pieces = parts
    total = len(pieces)
    x_refs, o_refs = refs[:given], refs[given : given + wanted]
    local_sem, z_send, z_recv, b_send, b_recv, c_send, c_recv = refs[given + wanted :]
    spans = [piece[0] for piece in pieces]
    ins = [piece[1](x_refs) for piece in pieces]
    line = count // 4
    group = lax.axis_index("dp")
    at, side, core = place(lax.axis_index("seq"))
    peers = line_peers(at, side, core, group, line)
    below, above, beside, sibling = (peer for _, peer in peers)
    meet(peers)

    def seq_of(where, which_side, which_core):
        return 4 * where + 2 * which_side + which_core

    def remote(src, dst, send, recv, peer):
        return pltpu.make_async_remote_copy(
            src_ref=src, dst_ref=dst, send_sem=send, recv_sem=recv, device_id=peer, device_id_type=MESH
        )

    def low_high(span):
        low = at // span * span
        return low, low + span

    def view(part, where, which_side, which_core):
        return pieces[part][2](o_refs, seq_of(where, which_side, which_core))

    def where_of(item):
        far = (item + 1) // 2
        return at - far if item % 2 else at + far

    def valid(part, item):
        low, high = low_high(spans[part])
        where = where_of(item)
        return (where >= low) & (where < high)

    def z_copy(part, item, up):
        where = where_of(item)
        far = (item + 1) // 2 + 1
        mark = 2 * far - 1 if up else 2 * far
        src = ins[part] if item == 0 else view(part, where, side, core)
        return remote(
            src,
            view(part, where, side, core),
            z_send.at[part, mark],
            z_recv.at[part, mark],
            above if up else below,
        )

    def b_copy(part, item):
        where = where_of(item)
        src = ins[part] if item == 0 else view(part, where, side, core)
        return remote(
            src, view(part, where, side, core), b_send.at[part, item], b_recv.at[part, item], beside
        )

    def b_arrived(part, item):
        where = where_of(item)
        spot = view(part, where, 1 - side, core)
        return remote(spot, spot, b_send.at[part, item], b_recv.at[part, item], beside)

    def z_arrived(part, item):
        spot = view(part, where_of(item), side, core)
        return remote(spot, spot, z_send.at[part, item], z_recv.at[part, item], beside)

    def c_copy(part, item, from_side):
        where = where_of(item)
        mine = item == 0 and not from_side
        which = 1 - side if from_side else side
        src = ins[part] if mine else view(part, where, which, core)
        index = 2 * item + from_side
        return remote(
            src, view(part, where, which, core), c_send.at[part, index], c_recv.at[part, index], sibling
        )

    def c_arrived(part, item, from_side):
        which = 1 - side if from_side else side
        spot = view(part, where_of(item), which, 1 - core)
        index = 2 * item + from_side
        return remote(spot, spot, c_send.at[part, index], c_recv.at[part, index], sibling)

    items = 2 * line - 1

    def goes_up(part):
        _, high = low_high(spans[part])
        return at + 1 < high

    def goes_down(part):
        low, _ = low_high(spans[part])
        return at - 1 >= low

    def active(part, item):
        return (item + 1) // 2 < spans[part]

    for part in range(total):
        pltpu.make_async_copy(
            ins[part], view(part, at, side, core), local_sem.at[part]
        ).start()

    def launch(part, item):
        @pl.when(valid(part, item))
        def _():
            if item == 0 or item % 2 == 1:
                if (item + 1) // 2 + 1 < spans[part]:
                    @pl.when(goes_up(part))
                    def _():
                        z_copy(part, item, True).start()
            if item == 0 or item % 2 == 0:
                if (item + 1) // 2 + 1 < spans[part]:
                    @pl.when(goes_down(part))
                    def _():
                        z_copy(part, item, False).start()
            b_copy(part, item).start()
            c_copy(part, item, 0).start()

    def relay(part, item):
        @pl.when(valid(part, item))
        def _():
            b_arrived(part, item).wait_recv()
            c_copy(part, item, 1).start()

    for part in range(total):
        launch(part, 0)
    for far in range(1, line + 1):
        for item in (2 * far - 1, 2 * far):
            for part in range(total):
                if far < line and active(part, item):
                    @pl.when(valid(part, item))
                    def _():
                        z_arrived(part, item).wait_recv()

                    launch(part, item)
        last = [0] if far == 1 else [2 * far - 3, 2 * far - 2]
        for item in last:
            for part in range(total):
                if active(part, item):
                    relay(part, item)
    for part in range(total):
        pltpu.make_async_copy(ins[part], view(part, at, side, core), local_sem.at[part]).wait()
        for item in range(items):
            if not active(part, item):
                continue

            @pl.when(valid(part, item))
            def _():
                if (item == 0 or item % 2 == 1) and (item + 1) // 2 + 1 < spans[part]:
                    @pl.when(goes_up(part))
                    def _():
                        z_copy(part, item, True).wait_send()
                if (item == 0 or item % 2 == 0) and (item + 1) // 2 + 1 < spans[part]:
                    @pl.when(goes_down(part))
                    def _():
                        z_copy(part, item, False).wait_send()
                b_copy(part, item).wait_send()
                c_copy(part, item, 0).wait_send()
                c_copy(part, item, 1).wait_send()
                c_arrived(part, item, 0).wait_recv()
                c_arrived(part, item, 1).wait_recv()


def spread(blocks, out_shapes, pieces, collective_id):
    count = lax.axis_size("seq")
    total = len(pieces)
    items = 2 * (count // 4) + 1
    sem = pltpu.SemaphoreType.DMA
    return pl.pallas_call(
        functools.partial(spread_kernel, (len(blocks), len(out_shapes), pieces), count),
        out_shape=out_shapes,
        in_specs=[pl.BlockSpec(memory_space=VMEM)] * len(blocks),
        out_specs=[pl.BlockSpec(memory_space=pl.ANY)] * len(out_shapes),
        scratch_shapes=[sem((total,))] + [sem((total, items))] * 4 + [sem((total, 2 * items))] * 2,
        compiler_params=pltpu.CompilerParams(collective_id=collective_id, has_side_effects=True),
    )(*blocks)


def fold_kernel(parts, count, *refs):
    given, wanted, pieces = parts
    total = len(pieces)
    spans = [piece[0] for piece in pieces]
    x_refs, o_refs = refs[:given], refs[given : given + wanted]
    scratch = refs[given + wanted :]
    outs = [piece[3](o_refs) for piece in pieces]
    c_bufs, s_bufs, b_bufs, u_bufs, d_bufs, t_bufs = (
        scratch[i * total : (i + 1) * total] for i in range(6)
    )
    c_send, c_recv, b_send, b_recv, u_send, u_recv, d_send, d_recv = scratch[6 * total :]
    line = count // 4
    group = lax.axis_index("dp")
    at, side, core = place(lax.axis_index("seq"))
    peers = line_peers(at, side, core, group, line)
    below, above, beside, sibling = (peer for _, peer in peers)
    meet(peers)

    def remote(src, dst, send, recv, peer):
        return pltpu.make_async_remote_copy(
            src_ref=src, dst_ref=dst, send_sem=send, recv_sem=recv, device_id=peer, device_id_type=MESH
        )

    def view(part, where, which_side, which_core):
        return pieces[part][2](x_refs, 4 * where + 2 * which_side + which_core)

    def valid(part, where):
        low = at // spans[part] * spans[part]
        return (where >= low) & (where < low + spans[part])

    def slot(part, where):
        return lax.rem(where, spans[part])

    order = []
    for far in range(line - 1, 0, -1):
        order += [(far, 1), (far, -1)]
    order.append((0, 1))

    def c_copy(part, where, other):
        which = 1 - side if other else side
        index = 2 * slot(part, where) + other
        return remote(
            view(part, where, which, 1 - core),
            c_bufs[part].at[index],
            c_send.at[part, index],
            c_recv.at[part, index],
            sibling,
        )

    def b_copy(part, where):
        index = slot(part, where)
        return remote(
            s_bufs[part].at[index], b_bufs[part].at[index], b_send.at[part, index], b_recv.at[part, index], beside
        )

    def u_copy(part, where):
        index = slot(part, where)
        return remote(
            t_bufs[part].at[index], u_bufs[part].at[index], u_send.at[part, index], u_recv.at[part, index], above
        )

    def d_copy(part, where):
        index = slot(part, where)
        return remote(
            t_bufs[part].at[index], d_bufs[part].at[index], d_send.at[part, index], d_recv.at[part, index], below
        )

    def each(action):
        for far, sign in order:
            for part in range(total):
                if far >= spans[part]:
                    continue
                where = at + sign * far

                @pl.when(valid(part, where))
                def _():
                    action(part, where, far, sign)

    each(lambda part, where, far, sign: c_copy(part, where, 1).start())
    each(lambda part, where, far, sign: c_copy(part, where, 0).start())

    def aside(part, where, far, sign):
        c_copy(part, where, 1).wait_recv()
        index = slot(part, where)
        mine = view(part, where, 1 - side, core)[...]
        s_bufs[part][index] = (
            mine.astype(F32) + c_bufs[part][2 * index + 1].astype(F32)
        ).astype(BF)
        b_copy(part, where).start()

    each(aside)

    def along(part, where, far, sign):
        c_copy(part, where, 0).wait_recv()
        b_copy(part, where).wait_recv()
        index = slot(part, where)
        here = slot(part, at)
        value = (
            view(part, where, side, core)[...].astype(F32)
            + c_bufs[part][2 * index].astype(F32)
            + b_bufs[part][index].astype(F32)
        )
        if far == 0:
            outs[part][...] = value

            @pl.when(here > 0)
            def _():
                u_copy(part, where).wait_recv()
                outs[part][...] += u_bufs[part][index].astype(F32)

            @pl.when(here < spans[part] - 1)
            def _():
                d_copy(part, where).wait_recv()
                outs[part][...] += d_bufs[part][index].astype(F32)
        elif sign > 0:
            t_bufs[part][index] = value.astype(BF)

            @pl.when(here > 0)
            def _():
                u_copy(part, where).wait_recv()
                t_bufs[part][index] = (value + u_bufs[part][index].astype(F32)).astype(BF)

            u_copy(part, where).start()
        else:
            t_bufs[part][index] = value.astype(BF)

            @pl.when(here < spans[part] - 1)
            def _():
                d_copy(part, where).wait_recv()
                t_bufs[part][index] = (value + d_bufs[part][index].astype(F32)).astype(BF)

            d_copy(part, where).start()

    each(along)

    def finish(part, where, far, sign):
        c_copy(part, where, 0).wait_send()
        c_copy(part, where, 1).wait_send()
        b_copy(part, where).wait_send()
        if far > 0:
            (u_copy if sign > 0 else d_copy)(part, where).wait_send()

    each(finish)


def fold(arrays, out_shapes, pieces, collective_id):
    count = lax.axis_size("seq")
    total = len(pieces)
    sem = pltpu.SemaphoreType.DMA
    line = count // 4
    bufs = []
    for times in (2, 1, 1, 1, 1, 1):
        bufs += [VMEM((times * piece[0],) + piece[1], BF) for piece in pieces]
    return pl.pallas_call(
        functools.partial(fold_kernel, (len(arrays), len(out_shapes), pieces), count),
        out_shape=[jax.ShapeDtypeStruct(shape, F32) for shape in out_shapes],
        in_specs=[pl.BlockSpec(memory_space=VMEM)] * len(arrays),
        out_specs=[pl.BlockSpec(memory_space=VMEM)] * len(out_shapes),
        scratch_shapes=bufs + [sem((total, 2 * line))] * 2 + [sem((total, line))] * 6,
        compiler_params=pltpu.CompilerParams(
            collective_id=collective_id, has_side_effects=True, vmem_limit_bytes=60 * 2**20
        ),
    )(*arrays)


def settle_kernel(parts, count, *refs):
    given, wanted, pieces = parts
    total = len(pieces)
    spans = [piece[0] for piece in pieces]
    x_refs, o_refs = refs[:given], refs[given : given + wanted]
    scratch = refs[given + wanted :]
    outs = [piece[3](o_refs) for piece in pieces]
    c_bufs, u_bufs, d_bufs, t_bufs, s_bufs, b_bufs = (
        scratch[i * total : (i + 1) * total] for i in range(6)
    )
    c_send, c_recv, u_send, u_recv, d_send, d_recv, b_send, b_recv = scratch[6 * total :]
    line = count // 4
    group = lax.axis_index("dp")
    at, side, core = place(lax.axis_index("seq"))
    peers = line_peers(at, side, core, group, line)
    below, above, beside, sibling = (peer for _, peer in peers)
    meet(peers)

    def remote(src, dst, send, recv, peer):
        return pltpu.make_async_remote_copy(
            src_ref=src, dst_ref=dst, send_sem=send, recv_sem=recv, device_id=peer, device_id_type=MESH
        )

    def view(part, where, other, which_core):
        which = 1 - side if other else side
        return pieces[part][2](x_refs, 4 * where + 2 * which + which_core)

    def slot(part, where):
        return lax.rem(where, spans[part])

    def index_of(part, where, other):
        return 2 * slot(part, where) + other

    order = []
    for far in range(line - 1, 0, -1):
        order += [(far, 1), (far, -1)]
    order.append((0, 1))

    def c_copy(part, where, other):
        index = index_of(part, where, other)
        return remote(
            view(part, where, other, 1 - core),
            c_bufs[part].at[index],
            c_send.at[part, index],
            c_recv.at[part, index],
            sibling,
        )

    def u_copy(part, where, other):
        index = index_of(part, where, other)
        return remote(
            t_bufs[part].at[index], u_bufs[part].at[index], u_send.at[part, index], u_recv.at[part, index], above
        )

    def d_copy(part, where, other):
        index = index_of(part, where, other)
        return remote(
            t_bufs[part].at[index], d_bufs[part].at[index], d_send.at[part, index], d_recv.at[part, index], below
        )

    def b_copy(part):
        return remote(s_bufs[part], b_bufs[part], b_send.at[part], b_recv.at[part], beside)

    def each(action):
        for far, sign in order:
            for part in range(total):
                if far >= spans[part]:
                    continue
                where = at + sign * far
                low = at // spans[part] * spans[part]

                @pl.when((where >= low) & (where < low + spans[part]))
                def _():
                    for other in (1, 0):
                        action(part, where, far, sign, other)

    each(lambda part, where, far, sign, other: c_copy(part, where, other).start())

    def along(part, where, far, sign, other):
        c_copy(part, where, other).wait_recv()
        index = index_of(part, where, other)
        here = slot(part, at)
        value = view(part, where, other, core)[...].astype(F32) + c_bufs[part][index].astype(F32)
        goal = outs[part] if far == 0 and not other else t_bufs[part].at[index]
        kind = F32 if far == 0 and not other else BF
        goal[...] = value.astype(kind)
        if far == 0 or sign > 0:

            @pl.when(here > 0)
            def _():
                u_copy(part, where, other).wait_recv()
                goal[...] = (goal[...].astype(F32) + u_bufs[part][index].astype(F32)).astype(kind)

        if far == 0 or sign < 0:

            @pl.when(here < spans[part] - 1)
            def _():
                d_copy(part, where, other).wait_recv()
                goal[...] = (goal[...].astype(F32) + d_bufs[part][index].astype(F32)).astype(kind)

        if far > 0:
            (u_copy if sign > 0 else d_copy)(part, where, other).start()
        elif other:
            s_bufs[part][...] = goal[...]
            b_copy(part).start()

    each(along)
    for part in range(total):
        b_copy(part).wait_recv()
        outs[part][...] += b_bufs[part][...].astype(F32)

    def finish(part, where, far, sign, other):
        c_copy(part, where, other).wait_send()
        if far > 0:
            (u_copy if sign > 0 else d_copy)(part, where, other).wait_send()

    each(finish)
    for part in range(total):
        b_copy(part).wait_send()


def settle(arrays, out_shapes, pieces, collective_id):
    count = lax.axis_size("seq")
    total = len(pieces)
    sem = pltpu.SemaphoreType.DMA
    line = count // 4
    bufs = []
    for _ in range(4):
        bufs += [VMEM((2 * piece[0],) + piece[1], BF) for piece in pieces]
    for _ in range(2):
        bufs += [VMEM(piece[1], BF) for piece in pieces]
    return pl.pallas_call(
        functools.partial(settle_kernel, (len(arrays), len(out_shapes), pieces), count),
        out_shape=[jax.ShapeDtypeStruct(shape, F32) for shape in out_shapes],
        in_specs=[pl.BlockSpec(memory_space=VMEM)] * len(arrays),
        out_specs=[pl.BlockSpec(memory_space=VMEM)] * len(out_shapes),
        scratch_shapes=bufs + [sem((total, 2 * line))] * 6 + [sem((total,))] * 2,
        compiler_params=pltpu.CompilerParams(
            collective_id=collective_id, has_side_effects=True, vmem_limit_bytes=60 * 2**20
        ),
    )(*arrays)


def exchange_kernel(x_ref, own_ref, other_ref, own_sem, z_send, z_recv, x_send, x_recv, y_send, y_recv, c_send, c_recv):
    count = own_ref.shape[0]
    line = count // 4
    group = lax.axis_index("dp")
    me = lax.axis_index("seq")
    at, side, core = place(me)
    peers = line_peers(at, side, core, group, line)
    below, above, beside, sibling = (peer for _, peer in peers)
    across = (1 - group, me)
    meet(peers + [(at >= 0, across)])

    def remote(src, dst, send, recv, index, peer):
        return pltpu.make_async_remote_copy(
            src_ref=src, dst_ref=dst, send_sem=send.at[index], recv_sem=recv.at[index],
            device_id=peer, device_id_type=MESH,
        )

    items = [(0, 0)] + [(far, turn) for far in range(1, line) for turn in range(2)]

    def where_of(item):
        return at + item[0] * (2 * item[1] - 1)

    def number(item):
        return 2 * item[0] + item[1]

    def given(item, action):
        @pl.when((where_of(item) >= 0) & (where_of(item) < line))
        def _():
            action()

    def spot(item, other_group, other_side, other_core):
        ref = other_ref if other_group else own_ref
        s = 1 - side if other_side else side
        c = 1 - core if other_core else core
        return ref.at[4 * where_of(item) + 2 * s + c]

    def here(item, other_group, other_side):
        if item == (0, 0) and not other_group and not other_side:
            return x_ref
        return spot(item, other_group, other_side, False)

    def z_copy(item, turn, peer):
        far = (item[0] + 1, turn)
        return remote(here(item, 0, 0), spot(item, 0, 0, 0), z_send, z_recv, number(far), peer)

    def side_copy(item, other_group, arrived):
        dst = spot(item, other_group, arrived, 0)
        src = dst if arrived else here(item, other_group, 0)
        return remote(src, dst, x_send, x_recv, 2 * number(item) + other_group, beside)

    def cross_copy(item, other_side, arrived):
        dst = spot(item, 1, other_side, 0)
        src = dst if arrived else here(item, 0, other_side)
        return remote(src, dst, y_send, y_recv, 2 * number(item) + other_side, across)

    def core_copy(item, other_group, other_side, arrived):
        dst = spot(item, other_group, other_side, arrived)
        src = dst if arrived else here(item, other_group, other_side)
        index = 4 * number(item) + 2 * other_group + other_side
        return remote(src, dst, c_send, c_recv, index, sibling)

    def z_links(item, act):
        far, turn = item
        if far + 1 < line:
            if far == 0 or turn == 0:

                @pl.when(at + 1 < line)
                def _():
                    act(z_copy(item, 0, above))

            if far == 0 or turn == 1:

                @pl.when(at > 0)
                def _():
                    act(z_copy(item, 1, below))

    def start(copy):
        copy.start()

    def launch(item):
        z_links(item, start)
        side_copy(item, 0, False).start()
        cross_copy(item, 0, False).start()
        core_copy(item, 0, 0, False).start()

    def first(item):
        z = remote(spot(item, 0, 0, 0), spot(item, 0, 0, 0), z_send, z_recv, number(item), beside)
        z.wait_recv()
        launch(item)

    def second(item):
        side_copy(item, 0, True).wait_recv()
        core_copy(item, 0, 1, False).start()
        cross_copy(item, 0, True).wait_recv()
        core_copy(item, 1, 0, False).start()

    def diagonal(item):
        side_copy(item, 1, False).start()

    def third(item):
        side_copy(item, 1, True).wait_recv()
        core_copy(item, 1, 1, False).start()

    def at_far(far):
        return [item for item in items if item[0] == far]

    own = pltpu.make_async_copy(x_ref, spot((0, 0), 0, 0, 0), own_sem.at[0])
    own.start()
    launch((0, 0))
    for step in range(1, line + 1):
        for item in at_far(step):
            given(item, functools.partial(first, item))
        for item in at_far(step - 1):
            given(item, functools.partial(second, item))
        if step >= line - 1:
            for far in range(line - 1) if step == line - 1 else [line - 1]:
                for item in at_far(far):
                    given(item, functools.partial(diagonal, item))
    for item in items:
        given(item, functools.partial(third, item))
    own.wait()

    def finish(item):
        z_links(item, lambda copy: copy.wait_send())
        side_copy(item, 0, False).wait_send()
        cross_copy(item, 0, False).wait_send()

        side_copy(item, 1, False).wait_send()
        for other_group in range(2):
            for other_side in range(2):
                core_copy(item, other_group, other_side, False).wait_send()
                core_copy(item, other_group, other_side, True).wait_recv()

    for item in items:
        given(item, functools.partial(finish, item))


def exchange(x, collective_id):
    count = lax.axis_size("seq")
    marks = 2 * (count // 4) + 2
    sem = pltpu.SemaphoreType.DMA
    return pl.pallas_call(
        exchange_kernel,
        out_shape=[jax.ShapeDtypeStruct((count,) + x.shape, x.dtype)] * 2,
        in_specs=[pl.BlockSpec(memory_space=VMEM)],
        out_specs=[pl.BlockSpec(memory_space=pl.ANY)] * 2,
        scratch_shapes=[sem((1,))] + [sem((marks,))] * 2 + [sem((2 * marks,))] * 4 + [sem((4 * marks,))] * 2,
        compiler_params=pltpu.CompilerParams(collective_id=collective_id, has_side_effects=True),
    )(x)


def row_gather(line, rows, cuts):
    size = rows // cuts
    return tuple(
        (
            line,
            lambda x, h=h: x[0].at[pl.ds(h * size, size)],
            lambda o, q, h=h: o[0].at[q, pl.ds(h * size, size)],
        )
        for h in range(cuts)
    )


def row_pieces(line, rows, width, cuts):
    size = rows // cuts
    return tuple(
        (
            line,
            (size, width),
            lambda x, q, h=h: x[0].at[q, pl.ds(h * size, size)],
            lambda o, h=h: o[0].at[pl.ds(h * size, size)],
        )
        for h in range(cuts)
    )


def turned_kernel(l_ref, k_ref, v_ref, o_ref):
    width = k_ref.shape[0]
    o_ref[...] = (
        contract(l_ref[:width], k_ref[...], 0, 0) + contract(l_ref[width:], v_ref[...], 0, 0)
    ).astype(BF)


def turned_product(left, weights, block):
    depth, rows = left.shape
    width = weights.shape[1]
    return pl.pallas_call(
        turned_kernel,
        grid=(rows // block,),
        out_shape=jax.ShapeDtypeStruct((rows, width), BF),
        in_specs=[
            pl.BlockSpec((depth, block), lambda i: (0, i)),
            pl.BlockSpec((width, width), lambda i: (1, 0)),
            pl.BlockSpec((width, width), lambda i: (2, 0)),
        ],
        out_specs=pl.BlockSpec((block, width), lambda i: (i, 0)),
    )(left, weights, weights)


def visible_rows(kind, run_devs, rows_dev, half, q):
    first = half + rows_dev * lax.rem(q, run_devs) if kind else rows_dev * q
    return pl.multiple_of(first, 32)


def visible_gather(line, run_devs, rows_dev, half):
    size = rows_dev // 2
    return tuple(
        (
            run_devs // 4 if kind else line,
            lambda x, m=m, kind=kind, j=j: x[0].at[m, kind, pl.ds(size * j, size)],
            lambda o, q, m=m, kind=kind, j=j: o[0].at[
                m, pl.ds(visible_rows(kind, run_devs, rows_dev, half, q) + size * j, size)
            ],
        )
        for kind in range(2)
        for m in range(MB)
        for j in range(2)
    )


def visible_sum(line, run_devs, rows_dev, half, width):
    return tuple(
        (
            run_devs // 4 if kind else line,
            (MB, rows_dev, width),
            lambda x, q, kind=kind: x[0].at[
                :, pl.ds(visible_rows(kind, run_devs, rows_dev, half, q), rows_dev)
            ],
            lambda o, kind=kind: o[0].at[:, kind],
        )
        for kind in range(2)
    )


def place_kernel(l_ref, r_ref, *refs):
    refs[-1][...] = jnp.dot(l_ref[...], r_ref[...], preferred_element_type=F32).astype(BF)


def place_product(buffer, left, right, first, rows):
    depth, width = right.shape
    block = width // 2
    given = () if buffer is None else (buffer,)
    return pl.pallas_call(
        place_kernel,
        grid=(left.shape[0] // block,),
        out_shape=jax.ShapeDtypeStruct((rows, width), BF),
        in_specs=[
            pl.BlockSpec((block, depth), lambda i: (i, 0)),
            pl.BlockSpec((depth, width), lambda i: (0, 0)),
        ]
        + [pl.BlockSpec(memory_space=pl.ANY)] * len(given),
        out_specs=pl.BlockSpec((block, width), lambda i: (first // block + i, 0)),
        input_output_aliases={2: 0} if given else {},
    )(left, right, *given)


def contract(left, right, left_dim, right_dim):
    return lax.dot_general(
        left, right, (((left_dim,), (right_dim,)), ((), ())), preferred_element_type=F32
    )


def norm_forward(values, gain, bias):
    centred = values - jnp.mean(values, axis=-1, keepdims=True)
    inverse = lax.rsqrt(jnp.mean(centred * centred, axis=-1, keepdims=True) + EPS_NORM)
    unit = centred * inverse
    return (unit * gain + bias, unit, inverse)


def norm_backward(upstream, unit, inverse, gain):
    scaled = upstream * gain
    inner = (
        scaled
        - jnp.mean(scaled, axis=-1, keepdims=True)
        - unit * jnp.mean(scaled * unit, axis=-1, keepdims=True)
    )
    return (inverse * inner, jnp.sum(upstream * unit, axis=0), jnp.sum(upstream, axis=0))


def head_probs(pos_ref, q, k):
    scores = contract(q, k, 0, 0) * HD ** (-0.5)
    key_pos = lax.broadcasted_iota(jnp.int32, scores.shape, 1)
    scores = jnp.where(key_pos <= pos_ref[...], scores, MASKED)
    shifted = jnp.exp(scores - jnp.max(scores, axis=1, keepdims=True))
    return shifted * (1.0 / jnp.sum(shifted, axis=1, keepdims=True))


def attend_kernel(pos_ref, q_ref, kv_ref, o_ref):
    probs = head_probs(pos_ref, q_ref[...], kv_ref[0]).astype(BF)
    o_ref[...] = contract(kv_ref[1], probs, 1, 1).astype(BF)


def attend_back_kernel(pos_ref, q_ref, kv_ref, g_ref, dq_ref, dkv_ref):
    q, k, v, g = q_ref[...], kv_ref[0], kv_ref[1], g_ref[...]
    probs = head_probs(pos_ref, q, k)
    grad = contract(g, v, 0, 0)
    back = (probs * (grad - jnp.sum(probs * grad, axis=1, keepdims=True))).astype(BF)
    scale = HD ** (-0.5)
    dq_ref[...] = (contract(k, back, 1, 1) * scale).astype(BF)
    dkv_ref[0] = (contract(q, back, 1, 0) * scale).astype(BF)
    dkv_ref[1] = contract(g, probs.astype(BF), 1, 0).astype(BF)


def attend(query_pos, q, kv):
    rows, keys = query_pos.shape[0], kv.shape[2] * query_pos.shape[0] // q.shape[1]
    small = pl.BlockSpec((HD, rows), lambda m, h: (h, m))
    large = pl.BlockSpec((2, HD, keys), lambda m, h: (0, h, m))
    return pl.pallas_call(
        attend_kernel,
        grid=(q.shape[1] // rows, HEADS),
        out_shape=jax.ShapeDtypeStruct(q.shape, BF),
        in_specs=[pl.BlockSpec((rows, 1), lambda m, h: (0, 0)), small, large],
        out_specs=small,
    )(query_pos, q, kv)


def attend_back(query_pos, q, kv, grad_out):
    rows, keys = query_pos.shape[0], kv.shape[2] * query_pos.shape[0] // q.shape[1]
    small = pl.BlockSpec((HD, rows), lambda m, h: (h, m))
    large = pl.BlockSpec((2, HD, keys), lambda m, h: (0, h, m))
    return pl.pallas_call(
        attend_back_kernel,
        grid=(q.shape[1] // rows, HEADS),
        out_shape=[jax.ShapeDtypeStruct(q.shape, BF), jax.ShapeDtypeStruct(kv.shape, BF)],
        in_specs=[pl.BlockSpec((rows, 1), lambda m, h: (0, 0)), small, large, small],
        out_specs=[small, large],
    )(query_pos, q, kv, grad_out)


def lookup_kernel(first_ref, slot_ref, table_ref, *refs):
    slots = slot_ref[...] - first_ref[0]
    ids = lax.broadcasted_iota(jnp.int32, (slots.shape[0], table_ref.shape[1]), 1)
    rows = contract(jnp.where(slots == ids, 1.0, 0.0).astype(BF), table_ref[...], 1, 1).astype(BF)
    refs[-1][...] = rows if len(refs) == 1 else refs[0][...] + rows


def lookup(first, slots, table, others, block):
    width, held = table.shape
    rows = pl.BlockSpec((block, width), lambda i: (i, 0))
    given = () if others is None else (others,)
    return pl.pallas_call(
        lookup_kernel,
        grid=(slots.shape[0] // block,),
        out_shape=jax.ShapeDtypeStruct((slots.shape[0], width), BF),
        in_specs=[
            pl.BlockSpec(memory_space=pltpu.SMEM),
            pl.BlockSpec((block, 1), lambda i: (i, 0)),
            pl.BlockSpec((width, held), lambda i: (0, 0)),
        ]
        + [rows] * len(given),
        out_specs=rows,
    )(first, slots, table, *given)


def adamw(weight, moment_a, moment_b, gradient, rate, decay):
    moment_a = MOMENT_ONE * moment_a + (1.0 - MOMENT_ONE) * gradient
    moment_b = MOMENT_TWO * moment_b + (1.0 - MOMENT_TWO) * gradient * gradient
    update = (
        moment_a
        / (1.0 - MOMENT_ONE**STEP)
        / (jnp.sqrt(moment_b / (1.0 - MOMENT_TWO**STEP)) + EPS_ADAM)
    )
    weight = weight - rate * (update + decay * weight)
    return (weight, moment_a, moment_b, weight.astype(BF))


def on_device(
    tokens,
    targets,
    counted,
    cont_label,
    pair_map,
    ref_logp,
    vocab_slot,
    embed_table,
    embed_first,
    embed_second,
    layer_weights,
    layer_first,
    layer_second,
    norm_params,
    norm_first,
    norm_second,
):
    seq_count = lax.axis_size("seq")
    group_count = lax.axis_size("dp")
    all_count = seq_count * group_count
    seq_rank = lax.axis_index("seq")
    group_rank = lax.axis_index("dp")
    device_rank = group_rank * seq_count + seq_rank
    rows_dev = tokens.shape[3]
    half = rows_dev * seq_count
    vocab_dev, width = embed_table.shape
    run_count = half // CLEN
    run_devs = CLEN // rows_dev
    own_rows = MB * 2 * rows_dev

    table_t = embed_table.T
    norm_dev = norm_params.shape[0]
    norm_parts = [norm_params]
    for step in range(1, group_count):
        norm_parts.append(
            lax.ppermute(
                norm_params, "dp", [(i, (i - step) % group_count) for i in range(group_count)]
            )
        )
    sent, *norm_parts = lax.optimization_barrier((table_t.astype(BF), *norm_parts))
    norm_all = jnp.zeros((group_count, norm_dev), F32)
    for step in range(group_count):
        norm_all = lax.dynamic_update_index_in_dim(
            norm_all, norm_parts[step], lax.rem(group_rank + step, group_count), 0
        )
    slab_t = [sent]
    for step in range(1, group_count):
        slab_t.append(
            lax.ppermute(
                slab_t[0], "dp", [(i, (i - step) % group_count) for i in range(group_count)]
            )
        )
    weights = lax.all_gather(
        layer_weights.T.astype(BF)[None], ("dp", "seq"), axis=0, tiled=True
    ).reshape(-1, width)
    w_q = weights[:width]
    w_o = weights[3 * width : 4 * width]
    w_kv = weights[width : 3 * width]
    w_up = weights[4 * width : 4 * width + FF]
    w_dn = weights[4 * width + FF :]

    marks = counted[:, 0]
    spots = jnp.arange(rows_dev, dtype=jnp.int32)
    ranks = (
        jnp.sum(jnp.where(spots[None, :, None] <= spots[None, None, :], marks[:, :, None], 0), axis=1)
        - 1
    )
    pick_ids = jnp.arange(PICK, dtype=jnp.int32)
    pick_hit = (ranks[:, None, :] == pick_ids[None, :, None]) & (marks[:, None, :] == 1)
    pick_targets = jnp.sum(jnp.where(pick_hit, targets[:, 0][:, None, :], 0), axis=2)
    pick_low = pick_hit.astype(BF)
    slots = vocab_slot[jnp.concatenate([tokens[:, 0].reshape(-1), pick_targets.reshape(-1)])]
    small = jnp.concatenate([slots.astype(F32), norm_all.reshape(-1)])
    small = jnp.pad(small, (0, -small.shape[0] % 1024)).reshape(-1, 128)
    small_all = direct_gather(small, False, 1).reshape(seq_count, -1)
    slots_all = small_all[:, : own_rows + MB * PICK].astype(jnp.int32)
    gains = (
        small_all[:, own_rows + MB * PICK :][:, : group_count * norm_dev]
        .reshape(seq_count, group_count, norm_dev)
        .transpose(1, 0, 2)
        .astype(BF)
        .astype(F32)
        .reshape(6, width)
    )
    row_slots = slots_all[:, :own_rows].reshape(-1)
    target_slots = slots_all[:, own_rows:].reshape(-1)
    vocab_ids = jnp.arange(vocab_dev, dtype=jnp.int32)

    def hits(slot_ids, step):
        part = lax.rem(group_rank + step, group_count)
        first = (part * seq_count + seq_rank) * vocab_dev
        return (slot_ids - first)[:, None] == vocab_ids[None, :]

    partial = None
    for step in range(group_count):
        part = lax.rem(group_rank + step, group_count)
        first = (part * seq_count + seq_rank) * vocab_dev
        partial = lookup(first[None], row_slots[:, None], slab_t[step], partial, own_rows)
    line = seq_count // 4
    (stream,) = fold(
        [partial.reshape(seq_count, own_rows, width)],
        [(own_rows, width)],
        row_pieces(line, own_rows, width, 2),
        2,
    )

    normed, unit_one, inverse_one = norm_forward(stream, gains[0], gains[3])
    hidden_one = normed.astype(BF)
    run_dev = seq_rank // run_devs * run_devs
    key_rows = half + CLEN
    (hidden_sel,) = spread(
        [hidden_one.reshape(MB, 2, rows_dev, width)],
        [jax.ShapeDtypeStruct((MB, key_rows, width), BF)],
        visible_gather(line, run_devs, rows_dev, half),
        3,
    )
    hidden_sel = hidden_sel.reshape(MB * key_rows, width)
    pairs = contract(w_kv, hidden_sel, 1, 1).astype(BF).reshape(2, width, MB * key_rows)
    queries = contract(w_q, hidden_one, 1, 1).astype(BF)
    start = seq_rank * rows_dev
    query_pos = jnp.concatenate([start + spots, half + (start - run_dev * rows_dev) + spots])[:, None]
    attended = attend(query_pos, queries, pairs)
    stream_one = stream + contract(attended, w_o, 0, 0)
    normed, unit_two, inverse_two = norm_forward(stream_one, gains[1], gains[4])
    hidden_two = normed.astype(BF)
    up_proj = contract(w_up, hidden_two, 1, 1)
    activated = jax.nn.gelu(up_proj, approximate=False).astype(BF)
    stream_two = stream_one + contract(activated, w_dn, 0, 0)
    normed, unit_final, inverse_final = norm_forward(stream_two, gains[2], gains[5])
    final = normed.astype(BF).reshape(MB, 2, rows_dev, width)[:, 1]
    picked = jnp.einsum("mpr,mrd->mpd", pick_low, final, preferred_element_type=F32).astype(BF)

    (head_rows,) = spread(
        [picked.reshape(MB * PICK, width)],
        [jax.ShapeDtypeStruct((seq_count, MB * PICK, width), BF)],
        row_gather(line, MB * PICK, 1),
        4,
    )
    head_rows = head_rows.reshape(seq_count * MB * PICK, width)
    logits = [contract(head_rows, slab_t[part], 1, 0) for part in range(group_count)]
    target_hits = [hits(target_slots, part) for part in range(group_count)]
    highest = jnp.max(logits[0], axis=1)
    for part in range(1, group_count):
        highest = jnp.maximum(highest, jnp.max(logits[part], axis=1))
    summed = jnp.zeros_like(highest)
    target_logit = jnp.zeros_like(highest)
    for part in range(group_count):
        summed = summed + jnp.sum(jnp.exp(logits[part] - highest[:, None]), axis=1)
        target_logit = target_logit + jnp.sum(jnp.where(target_hits[part], logits[part], 0.0), axis=1)
    stats = direct_gather(
        jnp.stack([highest, summed, target_logit]).reshape(-1, 128), False, 5
    ).reshape(seq_count, 3, -1)
    overall = jnp.max(stats[:, 0], axis=0)
    total = jnp.sum(stats[:, 1] * jnp.exp(stats[:, 0] - overall[None]), axis=0)
    log_total = overall + jnp.log(total)
    token_lp = jnp.sum(stats[:, 2], axis=0) - log_total

    run_ids = jnp.arange(run_count, dtype=jnp.int32)
    run_of_dev = jnp.arange(seq_count, dtype=jnp.int32) * rows_dev // CLEN
    run_match = run_of_dev[:, None] == run_ids[None, :]
    dev_lp = jnp.sum(token_lp.reshape(seq_count, MB, PICK), axis=2)
    run_lp = jnp.sum(jnp.where(run_match[:, None, :], dev_lp[:, :, None], 0.0), axis=0)
    labels = lax.dynamic_index_in_dim(cont_label, group_rank, 1, keepdims=False)
    pairing = lax.dynamic_index_in_dim(pair_map, group_rank, 1, keepdims=False)
    reference_lp = lax.dynamic_index_in_dim(ref_logp, group_rank, 1, keepdims=False)
    label_match = labels[:, :, None] == run_ids[None, None, :]
    label_lp = jnp.sum(jnp.where(label_match, run_lp[:, :, None], 0.0), axis=1)
    margin = label_lp - reference_lp
    chosen = pairing[:, 0::2, None] == run_ids[None, None, :]
    rejected = pairing[:, 1::2, None] == run_ids[None, None, :]
    delta = jnp.sum(jnp.where(chosen, margin[:, None, :], 0.0), axis=2) - jnp.sum(
        jnp.where(rejected, margin[:, None, :], 0.0), axis=2
    )
    loss = jnp.sum(jax.nn.softplus(-DPO_BETA * delta))
    pair_grad = -DPO_BETA * jax.nn.sigmoid(-DPO_BETA * delta)
    label_grad = jnp.sum(
        jnp.where(chosen, pair_grad[:, :, None], 0.0)
        - jnp.where(rejected, pair_grad[:, :, None], 0.0),
        axis=1,
    )
    run_grad = jnp.sum(jnp.where(label_match, label_grad[:, None, :], 0.0), axis=2)
    dev_grad = jnp.sum(jnp.where(run_match[:, None, :], run_grad[None], 0.0), axis=2)
    row_grad = jnp.broadcast_to(dev_grad[:, :, None], (seq_count, MB, PICK)).reshape(-1)

    head_back = 0.0
    logit_grads = []
    for part in range(group_count):
        logit_grad = (
            row_grad[:, None]
            * (target_hits[part].astype(F32) - jnp.exp(logits[part] - log_total[:, None]))
        ).astype(BF)
        logit_grads.append(logit_grad)
        head_back = head_back + contract(logit_grad, slab_t[part], 1, 1)
    head_back = head_back.astype(BF)
    moved = [(i, (i + 1) % group_count) for i in range(group_count)]
    if group_count == 2:
        head_back, head_part = lax.optimization_barrier(
            (head_back, contract(head_rows, logit_grads[1], 0, 0).astype(BF))
        )
        head_other = lax.ppermute(head_part, "dp", moved)
    (row_back,) = fold(
        [head_back.reshape(seq_count, MB * PICK, width)],
        [(MB * PICK, width)],
        row_pieces(line, MB * PICK, width, 1),
        6,
    )
    row_back = row_back.astype(BF).reshape(MB, PICK, width)
    cont_back = jnp.einsum("mpr,mpd->mrd", pick_low, row_back, preferred_element_type=F32)
    upstream = jnp.concatenate(
        [jnp.zeros((MB, 1, rows_dev, width), F32), cont_back[:, None]], axis=1
    ).reshape(own_rows, width)

    grad_two, gain_final, bias_final = norm_backward(upstream, unit_final, inverse_final, gains[2])
    grad_ffn = grad_two.astype(BF)
    columns = weights.shape[0]
    weight_grad = place_product(None, activated, grad_ffn, 4 * width + FF, columns)
    grad_act = contract(w_dn, grad_ffn, 1, 1)
    _, gelu_pull = jax.vjp(lambda pre_act: jax.nn.gelu(pre_act, approximate=False), up_proj)
    grad_up = gelu_pull(grad_act)[0].astype(BF)
    weight_grad = place_product(weight_grad, grad_up, hidden_two, 4 * width, columns)
    grad_hidden = contract(grad_up, w_up, 0, 0)
    grad_mid, gain_two, bias_two = norm_backward(grad_hidden, unit_two, inverse_two, gains[1])
    grad_one = grad_two + grad_mid
    grad_branch = grad_one.astype(BF)
    weight_grad = place_product(weight_grad, attended, grad_branch, 3 * width, columns)
    grad_attended = contract(w_o, grad_branch, 1, 1).astype(BF)
    grad_query, grad_pairs = attend_back(query_pos, queries, pairs, grad_attended)
    if group_count == 2:
        grad_query, head_other = lax.optimization_barrier((grad_query, head_other))
    grad_pairs = grad_pairs.reshape(2 * width, MB * key_rows)
    weight_grad = place_product(weight_grad, grad_query, hidden_one, 0, columns)
    weight_grad = place_product(weight_grad, grad_pairs, hidden_sel, width, columns)
    low_sel = turned_product(grad_pairs, weights, 2 * 2 * rows_dev).reshape(MB, key_rows, width)
    weight_sum = lax.psum_scatter(
        weight_grad.reshape(all_count, -1, width), ("dp", "seq"), scatter_dimension=0, tiled=True
    )[0].astype(F32)
    (low_own,) = settle(
        [low_sel],
        [(MB, 2, rows_dev, width)],
        visible_sum(line, run_devs, rows_dev, half, width),
        7,
    )
    grad_low = low_own.reshape(own_rows, width) + contract(grad_query, w_q, 0, 0)
    grad_first, gain_one, bias_one = norm_backward(grad_low, unit_one, inverse_one, gains[0])
    norm_rows = jnp.stack([gain_one, gain_two, gain_final, bias_one, bias_two, bias_final])
    if group_count == 2:
        head_own = contract(head_rows, logit_grads[0], 0, 0)
        pad_rows = 8
        own_grads, other_grads = exchange(
            jnp.concatenate(
                [grad_one + grad_first, norm_rows, jnp.zeros((pad_rows - 6, width), F32)]
            ).astype(BF),
            8,
        )
        other_slots = lax.ppermute(row_slots, "dp", moved)
        embed_sum = lax.optimization_barrier(head_own + head_other.astype(F32))
        norm_all = 0.0
        for grads, part_slots in ((own_grads, row_slots), (other_grads, other_slots)):
            part_slots = jnp.pad(
                part_slots.reshape(seq_count, own_rows), ((0, 0), (0, pad_rows)), constant_values=-1
            ).reshape(-1)
            embed_sum = embed_sum + contract(
                grads.reshape(-1, width), hits(part_slots, 0).astype(BF), 0, 0
            )
            norm_all = norm_all + jnp.sum(
                grads[:, own_rows : own_rows + 6].astype(F32), axis=0
            )
    else:
        row_grads, norm_grads = spread(
            [
                (grad_one + grad_first).astype(BF),
                jnp.concatenate([norm_rows, jnp.zeros((10, width), F32)]).astype(BF),
            ],
            [
                jax.ShapeDtypeStruct((seq_count, own_rows, width), BF),
                jax.ShapeDtypeStruct((seq_count, 16, width), BF),
            ],
            row_gather(line, own_rows, 2)
            + ((line, lambda x: x[1], lambda o, q: o[1].at[q]),),
            8,
        )
        row_grads = row_grads.reshape(-1, width)
        norm_sum = jnp.sum(norm_grads[:, :6].astype(F32), axis=0)
        norm_all = norm_sum
        for step in range(1, group_count):
            norm_all = norm_all + lax.ppermute(
                norm_sum, "dp", [(i, (i + step) % group_count) for i in range(group_count)]
            )

        def table_grad(step):
            return contract(head_rows, logit_grads[step], 0, 0) + contract(
                row_grads, hits(row_slots, step).astype(BF), 0, 0
            )

        arrived = [
            lax.ppermute(
                table_grad(step).astype(BF),
                "dp",
                [(i, (i + step) % group_count) for i in range(group_count)],
            )
            for step in range(1, group_count)
        ]
        embed_sum = table_grad(0)
        for block in arrived:
            embed_sum = embed_sum + block.astype(F32)
    norm_own = lax.dynamic_slice_in_dim(norm_all.reshape(-1), device_rank * norm_dev, norm_dev, 0)
    squares = (
        jnp.sum(embed_sum * embed_sum)
        + jnp.sum(weight_sum * weight_sum)
        + jnp.sum(norm_own * norm_own)
    )
    lanes = lax.broadcasted_iota(jnp.int32, (8, 128), 1)
    scalars = direct_gather(
        jnp.where(lanes == 0, squares, jnp.where(lanes == 1, loss, 0.0)), True, 9
    )
    square_total = jnp.sum(scalars[:, 0, 0])
    loss_total = jnp.sum(scalars[::seq_count, 0, 1])
    grad_norm = jnp.sqrt(square_total)
    factor = jnp.minimum(1.0, CLIP_NORM / grad_norm)
    embed_out = adamw(
        table_t, embed_first.T, embed_second.T, embed_sum * factor, LEARN_RATE, WEIGHT_DECAY
    )
    layer_out = adamw(
        layer_weights.T,
        layer_first.T,
        layer_second.T,
        weight_sum * factor,
        LEARN_RATE,
        WEIGHT_DECAY,
    )
    norm_out = adamw(norm_params, norm_first, norm_second, norm_own * factor, NORM_RATE, 0.0)
    return (
        embed_out[0].T,
        embed_out[1].T,
        embed_out[2].T,
        embed_out[3].T,
        layer_out[0].T,
        layer_out[1].T,
        layer_out[2].T,
        layer_out[3].T,
        norm_out[0],
        norm_out[1],
        norm_out[2],
        norm_out[3],
        grad_norm,
        loss_total,
    )


def solution(mesh):
    return jax.shard_map(
        on_device,
        mesh=mesh,
        in_specs=(
            P(None, "dp", None, "seq"),
            P(None, "dp", "seq"),
            P(None, "dp", "seq"),
            P(),
            P(),
            P(),
            P(),
            P(("dp", "seq"), None),
            P(("dp", "seq"), None),
            P(("dp", "seq"), None),
            P(None, ("dp", "seq")),
            P(None, ("dp", "seq")),
            P(None, ("dp", "seq")),
            P(("dp", "seq")),
            P(("dp", "seq")),
            P(("dp", "seq")),
        ),
        out_specs=(
            P(("dp", "seq"), None),
            P(("dp", "seq"), None),
            P(("dp", "seq"), None),
            P(("dp", "seq"), None),
            P(None, ("dp", "seq")),
            P(None, ("dp", "seq")),
            P(None, ("dp", "seq")),
            P(None, ("dp", "seq")),
            P(("dp", "seq")),
            P(("dp", "seq")),
            P(("dp", "seq")),
            P(("dp", "seq")),
            P(),
            P(),
        ),
        check_vma=False,
    )
```

```python
import functools

import jax
import jax.numpy as jnp
from jax import lax
from jax.experimental import pallas as pl
from jax.experimental.pallas import tpu as pltpu
from jax.sharding import PartitionSpec as P


HEADS = 17
HD = 64
FF = 4352
PICK = 32
CLEN = 512
MB = 2
STEP = 10


EPS_NORM = 1e-05
DPO_BETA = 0.05
CLIP_NORM = 1.0
LEARN_RATE = 0.03
NORM_RATE = 0.4
WEIGHT_DECAY = 0.1
MOMENT_ONE = 0.9
MOMENT_TWO = 0.999
EPS_ADAM = 1e-08
MASKED = -1e30
BF = jnp.bfloat16
F32 = jnp.float32
MESH = pl.DeviceIdType.MESH
VMEM = pltpu.VMEM


def meet(peers):
    barrier = pltpu.get_barrier_semaphore()
    for there, peer in peers:

        @pl.when(there)
        def _():
            pl.semaphore_signal(barrier, inc=1, device_id=peer, device_id_type=MESH)

    pl.semaphore_wait(barrier, sum(jnp.where(there, 1, 0) for there, _ in peers))


def direct_kernel(whole, x_ref, o_ref, send_sem, recv_sem):
    seq_count = lax.axis_size("seq")
    group_rank = lax.axis_index("dp")
    me = lax.axis_index("seq")
    count = o_ref.shape[0]
    if whole:
        me = group_rank * seq_count + me

    def peer(step):
        other = lax.rem(me + step, count)
        if whole:
            return (other // seq_count, lax.rem(other, seq_count))
        return (group_rank, other)

    barrier = pltpu.get_barrier_semaphore()

    def greet(step, carry):
        pl.semaphore_signal(barrier, inc=1, device_id=peer(step), device_id_type=MESH)
        return carry

    lax.fori_loop(1, count, greet, 0)
    o_ref[me] = x_ref[...]
    pl.semaphore_wait(barrier, count - 1)

    def copy(step):
        return pltpu.make_async_remote_copy(
            src_ref=x_ref,
            dst_ref=o_ref.at[me],
            send_sem=send_sem.at[step],
            recv_sem=recv_sem.at[step],
            device_id=peer(step),
            device_id_type=MESH,
        )

    def begin(step, carry):
        copy(step).start()
        return carry

    def finish(step, carry):
        copy(step).wait()
        return carry

    lax.fori_loop(1, count, begin, 0)
    lax.fori_loop(1, count, finish, 0)


def direct_gather(x, whole, collective_id):
    count = lax.axis_size("seq") * (lax.axis_size("dp") if whole else 1)
    return pl.pallas_call(
        functools.partial(direct_kernel, whole),
        out_shape=jax.ShapeDtypeStruct((count,) + x.shape, x.dtype),
        in_specs=[pl.BlockSpec(memory_space=VMEM)],
        out_specs=pl.BlockSpec(memory_space=VMEM),
        scratch_shapes=[pltpu.SemaphoreType.DMA((count,)), pltpu.SemaphoreType.DMA((count,))],
        compiler_params=pltpu.CompilerParams(collective_id=collective_id, has_side_effects=True),
    )(x)


def place(rank):
    return (rank // 4, lax.rem(rank, 4) // 2, lax.rem(rank, 2))


def line_peers(at, side, core, group, line):
    return [
        (at > 0, (group, 4 * (at - 1) + 2 * side + core)),
        (at < line - 1, (group, 4 * (at + 1) + 2 * side + core)),
        (at >= 0, (group, 4 * at + 2 * (1 - side) + core)),
        (at >= 0, (group, 4 * at + 2 * side + 1 - core)),
    ]


def spread_kernel(parts, count, *refs):
    given, wanted, pieces = parts
    total = len(pieces)
    x_refs, o_refs = refs[:given], refs[given : given + wanted]
    local_sem, z_send, z_recv, b_send, b_recv, c_send, c_recv = refs[given + wanted :]
    spans = [piece[0] for piece in pieces]
    ins = [piece[1](x_refs) for piece in pieces]
    line = count // 4
    group = lax.axis_index("dp")
    at, side, core = place(lax.axis_index("seq"))
    peers = line_peers(at, side, core, group, line)
    below, above, beside, sibling = (peer for _, peer in peers)
    meet(peers)

    def seq_of(where, which_side, which_core):
        return 4 * where + 2 * which_side + which_core

    def remote(src, dst, send, recv, peer):
        return pltpu.make_async_remote_copy(
            src_ref=src, dst_ref=dst, send_sem=send, recv_sem=recv, device_id=peer, device_id_type=MESH
        )

    def low_high(span):
        low = at // span * span
        return low, low + span

    def view(part, where, which_side, which_core):
        return pieces[part][2](o_refs, seq_of(where, which_side, which_core))

    def where_of(item):
        far = (item + 1) // 2
        return at - far if item % 2 else at + far

    def valid(part, item):
        low, high = low_high(spans[part])
        where = where_of(item)
        return (where >= low) & (where < high)

    def z_copy(part, item, up):
        where = where_of(item)
        far = (item + 1) // 2 + 1
        mark = 2 * far - 1 if up else 2 * far
        src = ins[part] if item == 0 else view(part, where, side, core)
        return remote(
            src,
            view(part, where, side, core),
            z_send.at[part, mark],
            z_recv.at[part, mark],
            above if up else below,
        )

    def b_copy(part, item):
        where = where_of(item)
        src = ins[part] if item == 0 else view(part, where, side, core)
        return remote(
            src, view(part, where, side, core), b_send.at[part, item], b_recv.at[part, item], beside
        )

    def b_arrived(part, item):
        where = where_of(item)
        spot = view(part, where, 1 - side, core)
        return remote(spot, spot, b_send.at[part, item], b_recv.at[part, item], beside)

    def z_arrived(part, item):
        spot = view(part, where_of(item), side, core)
        return remote(spot, spot, z_send.at[part, item], z_recv.at[part, item], beside)

    def c_copy(part, item, from_side):
        where = where_of(item)
        mine = item == 0 and not from_side
        which = 1 - side if from_side else side
        src = ins[part] if mine else view(part, where, which, core)
        index = 2 * item + from_side
        return remote(
            src, view(part, where, which, core), c_send.at[part, index], c_recv.at[part, index], sibling
        )

    def c_arrived(part, item, from_side):
        which = 1 - side if from_side else side
        spot = view(part, where_of(item), which, 1 - core)
        index = 2 * item + from_side
        return remote(spot, spot, c_send.at[part, index], c_recv.at[part, index], sibling)

    items = 2 * line - 1

    def goes_up(part):
        _, high = low_high(spans[part])
        return at + 1 < high

    def goes_down(part):
        low, _ = low_high(spans[part])
        return at - 1 >= low

    def active(part, item):
        return (item + 1) // 2 < spans[part]

    for part in range(total):
        pltpu.make_async_copy(
            ins[part], view(part, at, side, core), local_sem.at[part]
        ).start()

    def launch(part, item):
        @pl.when(valid(part, item))
        def _():
            if item == 0 or item % 2 == 1:
                if (item + 1) // 2 + 1 < spans[part]:
                    @pl.when(goes_up(part))
                    def _():
                        z_copy(part, item, True).start()
            if item == 0 or item % 2 == 0:
                if (item + 1) // 2 + 1 < spans[part]:
                    @pl.when(goes_down(part))
                    def _():
                        z_copy(part, item, False).start()
            b_copy(part, item).start()
            c_copy(part, item, 0).start()

    def relay(part, item):
        @pl.when(valid(part, item))
        def _():
            b_arrived(part, item).wait_recv()
            c_copy(part, item, 1).start()

    for part in range(total):
        launch(part, 0)
    for far in range(1, line + 1):
        for item in (2 * far - 1, 2 * far):
            for part in range(total):
                if far < line and active(part, item):
                    @pl.when(valid(part, item))
                    def _():
                        z_arrived(part, item).wait_recv()

                    launch(part, item)
        last = [0] if far == 1 else [2 * far - 3, 2 * far - 2]
        for item in last:
            for part in range(total):
                if active(part, item):
                    relay(part, item)
    for part in range(total):
        pltpu.make_async_copy(ins[part], view(part, at, side, core), local_sem.at[part]).wait()
        for item in range(items):
            if not active(part, item):
                continue

            @pl.when(valid(part, item))
            def _():
                if (item == 0 or item % 2 == 1) and (item + 1) // 2 + 1 < spans[part]:
                    @pl.when(goes_up(part))
                    def _():
                        z_copy(part, item, True).wait_send()
                if (item == 0 or item % 2 == 0) and (item + 1) // 2 + 1 < spans[part]:
                    @pl.when(goes_down(part))
                    def _():
                        z_copy(part, item, False).wait_send()
                b_copy(part, item).wait_send()
                c_copy(part, item, 0).wait_send()
                c_copy(part, item, 1).wait_send()
                c_arrived(part, item, 0).wait_recv()
                c_arrived(part, item, 1).wait_recv()


def spread(blocks, out_shapes, pieces, collective_id):
    count = lax.axis_size("seq")
    total = len(pieces)
    items = 2 * (count // 4) + 1
    sem = pltpu.SemaphoreType.DMA
    return pl.pallas_call(
        functools.partial(spread_kernel, (len(blocks), len(out_shapes), pieces), count),
        out_shape=out_shapes,
        in_specs=[pl.BlockSpec(memory_space=VMEM)] * len(blocks),
        out_specs=[pl.BlockSpec(memory_space=pl.ANY)] * len(out_shapes),
        scratch_shapes=[sem((total,))] + [sem((total, items))] * 4 + [sem((total, 2 * items))] * 2,
        compiler_params=pltpu.CompilerParams(collective_id=collective_id, has_side_effects=True),
    )(*blocks)


def fold_kernel(parts, count, *refs):
    given, wanted, pieces = parts
    total = len(pieces)
    spans = [piece[0] for piece in pieces]
    x_refs, o_refs = refs[:given], refs[given : given + wanted]
    scratch = refs[given + wanted :]
    outs = [piece[3](o_refs) for piece in pieces]
    c_bufs, s_bufs, b_bufs, u_bufs, d_bufs, t_bufs = (
        scratch[i * total : (i + 1) * total] for i in range(6)
    )
    c_send, c_recv, b_send, b_recv, u_send, u_recv, d_send, d_recv = scratch[6 * total :]
    line = count // 4
    group = lax.axis_index("dp")
    at, side, core = place(lax.axis_index("seq"))
    peers = line_peers(at, side, core, group, line)
    below, above, beside, sibling = (peer for _, peer in peers)
    meet(peers)

    def remote(src, dst, send, recv, peer):
        return pltpu.make_async_remote_copy(
            src_ref=src, dst_ref=dst, send_sem=send, recv_sem=recv, device_id=peer, device_id_type=MESH
        )

    def view(part, where, which_side, which_core):
        return pieces[part][2](x_refs, 4 * where + 2 * which_side + which_core)

    def valid(part, where):
        low = at // spans[part] * spans[part]
        return (where >= low) & (where < low + spans[part])

    def slot(part, where):
        return lax.rem(where, spans[part])

    order = []
    for far in range(line - 1, 0, -1):
        order += [(far, 1), (far, -1)]
    order.append((0, 1))

    def c_copy(part, where, other):
        which = 1 - side if other else side
        index = 2 * slot(part, where) + other
        return remote(
            view(part, where, which, 1 - core),
            c_bufs[part].at[index],
            c_send.at[part, index],
            c_recv.at[part, index],
            sibling,
        )

    def b_copy(part, where):
        index = slot(part, where)
        return remote(
            s_bufs[part].at[index], b_bufs[part].at[index], b_send.at[part, index], b_recv.at[part, index], beside
        )

    def u_copy(part, where):
        index = slot(part, where)
        return remote(
            t_bufs[part].at[index], u_bufs[part].at[index], u_send.at[part, index], u_recv.at[part, index], above
        )

    def d_copy(part, where):
        index = slot(part, where)
        return remote(
            t_bufs[part].at[index], d_bufs[part].at[index], d_send.at[part, index], d_recv.at[part, index], below
        )

    def each(action):
        for far, sign in order:
            for part in range(total):
                if far >= spans[part]:
                    continue
                where = at + sign * far

                @pl.when(valid(part, where))
                def _():
                    action(part, where, far, sign)

    each(lambda part, where, far, sign: c_copy(part, where, 1).start())
    each(lambda part, where, far, sign: c_copy(part, where, 0).start())

    def aside(part, where, far, sign):
        c_copy(part, where, 1).wait_recv()
        index = slot(part, where)
        mine = view(part, where, 1 - side, core)[...]
        s_bufs[part][index] = (
            mine.astype(F32) + c_bufs[part][2 * index + 1].astype(F32)
        ).astype(BF)
        b_copy(part, where).start()

    each(aside)

    def along(part, where, far, sign):
        c_copy(part, where, 0).wait_recv()
        b_copy(part, where).wait_recv()
        index = slot(part, where)
        here = slot(part, at)
        value = (
            view(part, where, side, core)[...].astype(F32)
            + c_bufs[part][2 * index].astype(F32)
            + b_bufs[part][index].astype(F32)
        )
        if far == 0:
            outs[part][...] = value

            @pl.when(here > 0)
            def _():
                u_copy(part, where).wait_recv()
                outs[part][...] += u_bufs[part][index].astype(F32)

            @pl.when(here < spans[part] - 1)
            def _():
                d_copy(part, where).wait_recv()
                outs[part][...] += d_bufs[part][index].astype(F32)
        elif sign > 0:
            t_bufs[part][index] = value.astype(BF)

            @pl.when(here > 0)
            def _():
                u_copy(part, where).wait_recv()
                t_bufs[part][index] = (value + u_bufs[part][index].astype(F32)).astype(BF)

            u_copy(part, where).start()
        else:
            t_bufs[part][index] = value.astype(BF)

            @pl.when(here < spans[part] - 1)
            def _():
                d_copy(part, where).wait_recv()
                t_bufs[part][index] = (value + d_bufs[part][index].astype(F32)).astype(BF)

            d_copy(part, where).start()

    each(along)

    def finish(part, where, far, sign):
        c_copy(part, where, 0).wait_send()
        c_copy(part, where, 1).wait_send()
        b_copy(part, where).wait_send()
        if far > 0:
            (u_copy if sign > 0 else d_copy)(part, where).wait_send()

    each(finish)


def fold(arrays, out_shapes, pieces, collective_id):
    count = lax.axis_size("seq")
    total = len(pieces)
    sem = pltpu.SemaphoreType.DMA
    line = count // 4
    bufs = []
    for times in (2, 1, 1, 1, 1, 1):
        bufs += [VMEM((times * piece[0],) + piece[1], BF) for piece in pieces]
    return pl.pallas_call(
        functools.partial(fold_kernel, (len(arrays), len(out_shapes), pieces), count),
        out_shape=[jax.ShapeDtypeStruct(shape, F32) for shape in out_shapes],
        in_specs=[pl.BlockSpec(memory_space=VMEM)] * len(arrays),
        out_specs=[pl.BlockSpec(memory_space=VMEM)] * len(out_shapes),
        scratch_shapes=bufs + [sem((total, 2 * line))] * 2 + [sem((total, line))] * 6,
        compiler_params=pltpu.CompilerParams(
            collective_id=collective_id, has_side_effects=True, vmem_limit_bytes=60 * 2**20
        ),
    )(*arrays)


def exchange_kernel(x_ref, own_ref, other_ref, own_sem, z_send, z_recv, x_send, x_recv, y_send, y_recv, c_send, c_recv):
    count = own_ref.shape[0]
    line = count // 4
    group = lax.axis_index("dp")
    me = lax.axis_index("seq")
    at, side, core = place(me)
    peers = line_peers(at, side, core, group, line)
    below, above, beside, sibling = (peer for _, peer in peers)
    across = (1 - group, me)
    meet(peers + [(at >= 0, across)])

    def remote(src, dst, send, recv, index, peer):
        return pltpu.make_async_remote_copy(
            src_ref=src, dst_ref=dst, send_sem=send.at[index], recv_sem=recv.at[index],
            device_id=peer, device_id_type=MESH,
        )

    items = [(0, 0)] + [(far, turn) for far in range(1, line) for turn in range(2)]

    def where_of(item):
        return at + item[0] * (2 * item[1] - 1)

    def number(item):
        return 2 * item[0] + item[1]

    def given(item, action):
        @pl.when((where_of(item) >= 0) & (where_of(item) < line))
        def _():
            action()

    def spot(item, other_group, other_side, other_core):
        ref = other_ref if other_group else own_ref
        s = 1 - side if other_side else side
        c = 1 - core if other_core else core
        return ref.at[4 * where_of(item) + 2 * s + c]

    def here(item, other_group, other_side):
        if item == (0, 0) and not other_group and not other_side:
            return x_ref
        return spot(item, other_group, other_side, False)

    def z_copy(item, turn, peer):
        far = (item[0] + 1, turn)
        return remote(here(item, 0, 0), spot(item, 0, 0, 0), z_send, z_recv, number(far), peer)

    def side_copy(item, other_group, arrived):
        dst = spot(item, other_group, arrived, 0)
        src = dst if arrived else here(item, other_group, 0)
        return remote(src, dst, x_send, x_recv, 2 * number(item) + other_group, beside)

    def cross_copy(item, other_side, arrived):
        dst = spot(item, 1, other_side, 0)
        src = dst if arrived else here(item, 0, other_side)
        return remote(src, dst, y_send, y_recv, 2 * number(item) + other_side, across)

    def core_copy(item, other_group, other_side, arrived):
        dst = spot(item, other_group, other_side, arrived)
        src = dst if arrived else here(item, other_group, other_side)
        index = 4 * number(item) + 2 * other_group + other_side
        return remote(src, dst, c_send, c_recv, index, sibling)

    def by_side(item):
        return lax.rem(where_of(item), 2) == 0

    def z_links(item, act):
        far, turn = item
        if far + 1 < line:
            if far == 0 or turn == 0:

                @pl.when(at + 1 < line)
                def _():
                    act(z_copy(item, 0, above))

            if far == 0 or turn == 1:

                @pl.when(at > 0)
                def _():
                    act(z_copy(item, 1, below))

    def start(copy):
        copy.start()

    def launch(item):
        z_links(item, start)
        side_copy(item, 0, False).start()
        cross_copy(item, 0, False).start()
        core_copy(item, 0, 0, False).start()

    def first(item):
        z = remote(spot(item, 0, 0, 0), spot(item, 0, 0, 0), z_send, z_recv, number(item), beside)
        z.wait_recv()
        launch(item)

    def second(item):
        side_copy(item, 0, True).wait_recv()
        core_copy(item, 0, 1, False).start()
        cross_copy(item, 0, True).wait_recv()
        core_copy(item, 1, 0, False).start()

    def diagonal(item):
        @pl.when(by_side(item))
        def _():
            side_copy(item, 1, False).start()

        @pl.when(jnp.logical_not(by_side(item)))
        def _():
            cross_copy(item, 1, False).start()

    def third(item):
        @pl.when(by_side(item))
        def _():
            side_copy(item, 1, True).wait_recv()

        @pl.when(jnp.logical_not(by_side(item)))
        def _():
            cross_copy(item, 1, True).wait_recv()

        core_copy(item, 1, 1, False).start()

    def at_far(far):
        return [item for item in items if item[0] == far]

    own = pltpu.make_async_copy(x_ref, spot((0, 0), 0, 0, 0), own_sem.at[0])
    own.start()
    launch((0, 0))
    for step in range(1, line + 1):
        for item in at_far(step):
            given(item, functools.partial(first, item))
        for item in at_far(step - 1):
            given(item, functools.partial(second, item))
        if step >= line - 1:
            for far in range(line - 1) if step == line - 1 else [line - 1]:
                for item in at_far(far):
                    given(item, functools.partial(diagonal, item))
    for item in items:
        given(item, functools.partial(third, item))
    own.wait()

    def finish(item):
        z_links(item, lambda copy: copy.wait_send())
        side_copy(item, 0, False).wait_send()
        cross_copy(item, 0, False).wait_send()

        @pl.when(by_side(item))
        def _():
            side_copy(item, 1, False).wait_send()

        @pl.when(jnp.logical_not(by_side(item)))
        def _():
            cross_copy(item, 1, False).wait_send()

        for other_group in range(2):
            for other_side in range(2):
                core_copy(item, other_group, other_side, False).wait_send()
                core_copy(item, other_group, other_side, True).wait_recv()

    for item in items:
        given(item, functools.partial(finish, item))


def exchange(x, collective_id):
    count = lax.axis_size("seq")
    marks = 2 * (count // 4) + 2
    sem = pltpu.SemaphoreType.DMA
    return pl.pallas_call(
        exchange_kernel,
        out_shape=[jax.ShapeDtypeStruct((count,) + x.shape, x.dtype)] * 2,
        in_specs=[pl.BlockSpec(memory_space=VMEM)],
        out_specs=[pl.BlockSpec(memory_space=pl.ANY)] * 2,
        scratch_shapes=[sem((1,))] + [sem((marks,))] * 2 + [sem((2 * marks,))] * 4 + [sem((4 * marks,))] * 2,
        compiler_params=pltpu.CompilerParams(collective_id=collective_id, has_side_effects=True),
    )(x)


def row_gather(line, rows, cuts):
    size = rows // cuts
    return tuple(
        (
            line,
            lambda x, h=h: x[0].at[pl.ds(h * size, size)],
            lambda o, q, h=h: o[0].at[q, pl.ds(h * size, size)],
        )
        for h in range(cuts)
    )


def row_pieces(line, rows, width, cuts):
    size = rows // cuts
    return tuple(
        (
            line,
            (size, width),
            lambda x, q, h=h: x[0].at[q, pl.ds(h * size, size)],
            lambda o, h=h: o[0].at[pl.ds(h * size, size)],
        )
        for h in range(cuts)
    )


def turned_kernel(l_ref, k_ref, v_ref, o_ref):
    width = k_ref.shape[0]
    o_ref[...] = (
        contract(l_ref[:width], k_ref[...], 0, 0) + contract(l_ref[width:], v_ref[...], 0, 0)
    ).astype(BF)


def turned_product(left, weights, block):
    depth, rows = left.shape
    width = weights.shape[1]
    return pl.pallas_call(
        turned_kernel,
        grid=(rows // block,),
        out_shape=jax.ShapeDtypeStruct((rows, width), BF),
        in_specs=[
            pl.BlockSpec((depth, block), lambda i: (0, i)),
            pl.BlockSpec((width, width), lambda i: (1, 0)),
            pl.BlockSpec((width, width), lambda i: (2, 0)),
        ],
        out_specs=pl.BlockSpec((block, width), lambda i: (i, 0)),
    )(left, weights, weights)


def visible_rows(kind, run_devs, rows_dev, half, q):
    first = half + rows_dev * lax.rem(q, run_devs) if kind else rows_dev * q
    return pl.multiple_of(first, 32)


def visible_gather(line, run_devs, rows_dev, half):
    size = rows_dev // 2
    return tuple(
        (
            run_devs // 4 if kind else line,
            lambda x, m=m, kind=kind, j=j: x[0].at[m, kind, pl.ds(size * j, size)],
            lambda o, q, m=m, kind=kind, j=j: o[0].at[
                m, pl.ds(visible_rows(kind, run_devs, rows_dev, half, q) + size * j, size)
            ],
        )
        for kind in range(2)
        for m in range(MB)
        for j in range(2)
    )


def visible_sum(line, run_devs, rows_dev, half, width):
    return tuple(
        (
            run_devs // 4 if kind else line,
            (MB, rows_dev, width),
            lambda x, q, kind=kind: x[0].at[
                :, pl.ds(visible_rows(kind, run_devs, rows_dev, half, q), rows_dev)
            ],
            lambda o, kind=kind: o[0].at[:, kind],
        )
        for kind in range(2)
    )


def place_kernel(l_ref, r_ref, *refs):
    refs[-1][...] = jnp.dot(l_ref[...], r_ref[...], preferred_element_type=F32).astype(BF)


def place_product(buffer, left, right, first, rows):
    depth, width = right.shape
    block = width // 2
    given = () if buffer is None else (buffer,)
    return pl.pallas_call(
        place_kernel,
        grid=(left.shape[0] // block,),
        out_shape=jax.ShapeDtypeStruct((rows, width), BF),
        in_specs=[
            pl.BlockSpec((block, depth), lambda i: (i, 0)),
            pl.BlockSpec((depth, width), lambda i: (0, 0)),
        ]
        + [pl.BlockSpec(memory_space=pl.ANY)] * len(given),
        out_specs=pl.BlockSpec((block, width), lambda i: (first // block + i, 0)),
        input_output_aliases={2: 0} if given else {},
    )(left, right, *given)


def contract(left, right, left_dim, right_dim):
    return lax.dot_general(
        left, right, (((left_dim,), (right_dim,)), ((), ())), preferred_element_type=F32
    )


def norm_forward(values, gain, bias):
    centred = values - jnp.mean(values, axis=-1, keepdims=True)
    inverse = lax.rsqrt(jnp.mean(centred * centred, axis=-1, keepdims=True) + EPS_NORM)
    unit = centred * inverse
    return (unit * gain + bias, unit, inverse)


def norm_backward(upstream, unit, inverse, gain):
    scaled = upstream * gain
    inner = (
        scaled
        - jnp.mean(scaled, axis=-1, keepdims=True)
        - unit * jnp.mean(scaled * unit, axis=-1, keepdims=True)
    )
    return (inverse * inner, jnp.sum(upstream * unit, axis=0), jnp.sum(upstream, axis=0))


def head_probs(pos_ref, q, k):
    scores = contract(q, k, 0, 0) * HD ** (-0.5)
    key_pos = lax.broadcasted_iota(jnp.int32, scores.shape, 1)
    scores = jnp.where(key_pos <= pos_ref[...], scores, MASKED)
    shifted = jnp.exp(scores - jnp.max(scores, axis=1, keepdims=True))
    return shifted * (1.0 / jnp.sum(shifted, axis=1, keepdims=True))


def attend_kernel(pos_ref, q_ref, kv_ref, o_ref):
    probs = head_probs(pos_ref, q_ref[...], kv_ref[0]).astype(BF)
    o_ref[...] = contract(kv_ref[1], probs, 1, 1).astype(BF)


def attend_back_kernel(pos_ref, q_ref, kv_ref, g_ref, dq_ref, dkv_ref):
    q, k, v, g = q_ref[...], kv_ref[0], kv_ref[1], g_ref[...]
    probs = head_probs(pos_ref, q, k)
    grad = contract(g, v, 0, 0)
    back = (probs * (grad - jnp.sum(probs * grad, axis=1, keepdims=True))).astype(BF)
    scale = HD ** (-0.5)
    dq_ref[...] = (contract(k, back, 1, 1) * scale).astype(BF)
    dkv_ref[0] = (contract(q, back, 1, 0) * scale).astype(BF)
    dkv_ref[1] = contract(g, probs.astype(BF), 1, 0).astype(BF)


def attend(query_pos, q, kv):
    rows, keys = query_pos.shape[0], kv.shape[2] * query_pos.shape[0] // q.shape[1]
    small = pl.BlockSpec((HD, rows), lambda m, h: (h, m))
    large = pl.BlockSpec((2, HD, keys), lambda m, h: (0, h, m))
    return pl.pallas_call(
        attend_kernel,
        grid=(q.shape[1] // rows, HEADS),
        out_shape=jax.ShapeDtypeStruct(q.shape, BF),
        in_specs=[pl.BlockSpec((rows, 1), lambda m, h: (0, 0)), small, large],
        out_specs=small,
    )(query_pos, q, kv)


def attend_back(query_pos, q, kv, grad_out):
    rows, keys = query_pos.shape[0], kv.shape[2] * query_pos.shape[0] // q.shape[1]
    small = pl.BlockSpec((HD, rows), lambda m, h: (h, m))
    large = pl.BlockSpec((2, HD, keys), lambda m, h: (0, h, m))
    return pl.pallas_call(
        attend_back_kernel,
        grid=(q.shape[1] // rows, HEADS),
        out_shape=[jax.ShapeDtypeStruct(q.shape, BF), jax.ShapeDtypeStruct(kv.shape, BF)],
        in_specs=[pl.BlockSpec((rows, 1), lambda m, h: (0, 0)), small, large, small],
        out_specs=[small, large],
    )(query_pos, q, kv, grad_out)


def lookup_kernel(first_ref, slot_ref, table_ref, *refs):
    slots = slot_ref[...] - first_ref[0]
    ids = lax.broadcasted_iota(jnp.int32, (slots.shape[0], table_ref.shape[1]), 1)
    rows = contract(jnp.where(slots == ids, 1.0, 0.0).astype(BF), table_ref[...], 1, 1).astype(BF)
    refs[-1][...] = rows if len(refs) == 1 else refs[0][...] + rows


def lookup(first, slots, table, others, block):
    width, held = table.shape
    rows = pl.BlockSpec((block, width), lambda i: (i, 0))
    given = () if others is None else (others,)
    return pl.pallas_call(
        lookup_kernel,
        grid=(slots.shape[0] // block,),
        out_shape=jax.ShapeDtypeStruct((slots.shape[0], width), BF),
        in_specs=[
            pl.BlockSpec(memory_space=pltpu.SMEM),
            pl.BlockSpec((block, 1), lambda i: (i, 0)),
            pl.BlockSpec((width, held), lambda i: (0, 0)),
        ]
        + [rows] * len(given),
        out_specs=rows,
    )(first, slots, table, *given)


def adamw(weight, moment_a, moment_b, gradient, rate, decay):
    moment_a = MOMENT_ONE * moment_a + (1.0 - MOMENT_ONE) * gradient
    moment_b = MOMENT_TWO * moment_b + (1.0 - MOMENT_TWO) * gradient * gradient
    update = (
        moment_a
        / (1.0 - MOMENT_ONE**STEP)
        / (jnp.sqrt(moment_b / (1.0 - MOMENT_TWO**STEP)) + EPS_ADAM)
    )
    weight = weight - rate * (update + decay * weight)
    return (weight, moment_a, moment_b, weight.astype(BF))


def on_device(
    tokens,
    targets,
    counted,
    cont_label,
    pair_map,
    ref_logp,
    vocab_slot,
    embed_table,
    embed_first,
    embed_second,
    layer_weights,
    layer_first,
    layer_second,
    norm_params,
    norm_first,
    norm_second,
):
    seq_count = lax.axis_size("seq")
    group_count = lax.axis_size("dp")
    all_count = seq_count * group_count
    seq_rank = lax.axis_index("seq")
    group_rank = lax.axis_index("dp")
    device_rank = group_rank * seq_count + seq_rank
    rows_dev = tokens.shape[3]
    half = rows_dev * seq_count
    vocab_dev, width = embed_table.shape
    run_count = half // CLEN
    run_devs = CLEN // rows_dev
    own_rows = MB * 2 * rows_dev

    table_t = embed_table.T
    norm_dev = norm_params.shape[0]
    norm_parts = [norm_params]
    for step in range(1, group_count):
        norm_parts.append(
            lax.ppermute(
                norm_params, "dp", [(i, (i - step) % group_count) for i in range(group_count)]
            )
        )
    sent, *norm_parts = lax.optimization_barrier((table_t.astype(BF), *norm_parts))
    norm_all = jnp.zeros((group_count, norm_dev), F32)
    for step in range(group_count):
        norm_all = lax.dynamic_update_index_in_dim(
            norm_all, norm_parts[step], lax.rem(group_rank + step, group_count), 0
        )
    slab_t = [sent]
    for step in range(1, group_count):
        slab_t.append(
            lax.ppermute(
                slab_t[0], "dp", [(i, (i - step) % group_count) for i in range(group_count)]
            )
        )
    weights = lax.all_gather(
        layer_weights.T.astype(BF)[None], ("dp", "seq"), axis=0, tiled=True
    ).reshape(-1, width)
    w_q = weights[:width]
    w_o = weights[3 * width : 4 * width]
    w_kv = weights[width : 3 * width]
    w_up = weights[4 * width : 4 * width + FF]
    w_dn = weights[4 * width + FF :]

    marks = counted[:, 0]
    spots = jnp.arange(rows_dev, dtype=jnp.int32)
    ranks = (
        jnp.sum(jnp.where(spots[None, :, None] <= spots[None, None, :], marks[:, :, None], 0), axis=1)
        - 1
    )
    pick_ids = jnp.arange(PICK, dtype=jnp.int32)
    pick_hit = (ranks[:, None, :] == pick_ids[None, :, None]) & (marks[:, None, :] == 1)
    pick_targets = jnp.sum(jnp.where(pick_hit, targets[:, 0][:, None, :], 0), axis=2)
    pick_low = pick_hit.astype(BF)
    slots = vocab_slot[jnp.concatenate([tokens[:, 0].reshape(-1), pick_targets.reshape(-1)])]
    small = jnp.concatenate([slots.astype(F32), norm_all.reshape(-1)])
    small = jnp.pad(small, (0, -small.shape[0] % 1024)).reshape(-1, 128)
    small_all = direct_gather(small, False, 1).reshape(seq_count, -1)
    slots_all = small_all[:, : own_rows + MB * PICK].astype(jnp.int32)
    gains = (
        small_all[:, own_rows + MB * PICK :][:, : group_count * norm_dev]
        .reshape(seq_count, group_count, norm_dev)
        .transpose(1, 0, 2)
        .astype(BF)
        .astype(F32)
        .reshape(6, width)
    )
    row_slots = slots_all[:, :own_rows].reshape(-1)
    target_slots = slots_all[:, own_rows:].reshape(-1)
    vocab_ids = jnp.arange(vocab_dev, dtype=jnp.int32)

    def hits(slot_ids, step):
        part = lax.rem(group_rank + step, group_count)
        first = (part * seq_count + seq_rank) * vocab_dev
        return (slot_ids - first)[:, None] == vocab_ids[None, :]

    partial = None
    for step in range(group_count):
        part = lax.rem(group_rank + step, group_count)
        first = (part * seq_count + seq_rank) * vocab_dev
        partial = lookup(first[None], row_slots[:, None], slab_t[step], partial, own_rows)
    line = seq_count // 4
    (stream,) = fold(
        [partial.reshape(seq_count, own_rows, width)],
        [(own_rows, width)],
        row_pieces(line, own_rows, width, 2),
        2,
    )

    normed, unit_one, inverse_one = norm_forward(stream, gains[0], gains[3])
    hidden_one = normed.astype(BF)
    run_dev = seq_rank // run_devs * run_devs
    key_rows = half + CLEN
    (hidden_sel,) = spread(
        [hidden_one.reshape(MB, 2, rows_dev, width)],
        [jax.ShapeDtypeStruct((MB, key_rows, width), BF)],
        visible_gather(line, run_devs, rows_dev, half),
        3,
    )
    hidden_sel = hidden_sel.reshape(MB * key_rows, width)
    pairs = contract(w_kv, hidden_sel, 1, 1).astype(BF).reshape(2, width, MB * key_rows)
    queries = contract(w_q, hidden_one, 1, 1).astype(BF)
    start = seq_rank * rows_dev
    query_pos = jnp.concatenate([start + spots, half + (start - run_dev * rows_dev) + spots])[:, None]
    attended = attend(query_pos, queries, pairs)
    stream_one = stream + contract(attended, w_o, 0, 0)
    normed, unit_two, inverse_two = norm_forward(stream_one, gains[1], gains[4])
    hidden_two = normed.astype(BF)
    up_proj = contract(w_up, hidden_two, 1, 1)
    activated = jax.nn.gelu(up_proj, approximate=False).astype(BF)
    stream_two = stream_one + contract(activated, w_dn, 0, 0)
    normed, unit_final, inverse_final = norm_forward(stream_two, gains[2], gains[5])
    final = normed.astype(BF).reshape(MB, 2, rows_dev, width)[:, 1]
    picked = jnp.einsum("mpr,mrd->mpd", pick_low, final, preferred_element_type=F32).astype(BF)

    (head_rows,) = spread(
        [picked.reshape(MB * PICK, width)],
        [jax.ShapeDtypeStruct((seq_count, MB * PICK, width), BF)],
        row_gather(line, MB * PICK, 1),
        4,
    )
    head_rows = head_rows.reshape(seq_count * MB * PICK, width)
    logits = [contract(head_rows, slab_t[part], 1, 0) for part in range(group_count)]
    target_hits = [hits(target_slots, part) for part in range(group_count)]
    highest = jnp.max(logits[0], axis=1)
    for part in range(1, group_count):
        highest = jnp.maximum(highest, jnp.max(logits[part], axis=1))
    summed = jnp.zeros_like(highest)
    target_logit = jnp.zeros_like(highest)
    for part in range(group_count):
        summed = summed + jnp.sum(jnp.exp(logits[part] - highest[:, None]), axis=1)
        target_logit = target_logit + jnp.sum(jnp.where(target_hits[part], logits[part], 0.0), axis=1)
    stats = direct_gather(
        jnp.stack([highest, summed, target_logit]).reshape(-1, 128), False, 5
    ).reshape(seq_count, 3, -1)
    overall = jnp.max(stats[:, 0], axis=0)
    total = jnp.sum(stats[:, 1] * jnp.exp(stats[:, 0] - overall[None]), axis=0)
    log_total = overall + jnp.log(total)
    token_lp = jnp.sum(stats[:, 2], axis=0) - log_total

    run_ids = jnp.arange(run_count, dtype=jnp.int32)
    run_of_dev = jnp.arange(seq_count, dtype=jnp.int32) * rows_dev // CLEN
    run_match = run_of_dev[:, None] == run_ids[None, :]
    dev_lp = jnp.sum(token_lp.reshape(seq_count, MB, PICK), axis=2)
    run_lp = jnp.sum(jnp.where(run_match[:, None, :], dev_lp[:, :, None], 0.0), axis=0)
    labels = lax.dynamic_index_in_dim(cont_label, group_rank, 1, keepdims=False)
    pairing = lax.dynamic_index_in_dim(pair_map, group_rank, 1, keepdims=False)
    reference_lp = lax.dynamic_index_in_dim(ref_logp, group_rank, 1, keepdims=False)
    label_match = labels[:, :, None] == run_ids[None, None, :]
    label_lp = jnp.sum(jnp.where(label_match, run_lp[:, :, None], 0.0), axis=1)
    margin = label_lp - reference_lp
    chosen = pairing[:, 0::2, None] == run_ids[None, None, :]
    rejected = pairing[:, 1::2, None] == run_ids[None, None, :]
    delta = jnp.sum(jnp.where(chosen, margin[:, None, :], 0.0), axis=2) - jnp.sum(
        jnp.where(rejected, margin[:, None, :], 0.0), axis=2
    )
    loss = jnp.sum(jax.nn.softplus(-DPO_BETA * delta))
    pair_grad = -DPO_BETA * jax.nn.sigmoid(-DPO_BETA * delta)
    label_grad = jnp.sum(
        jnp.where(chosen, pair_grad[:, :, None], 0.0)
        - jnp.where(rejected, pair_grad[:, :, None], 0.0),
        axis=1,
    )
    run_grad = jnp.sum(jnp.where(label_match, label_grad[:, None, :], 0.0), axis=2)
    dev_grad = jnp.sum(jnp.where(run_match[:, None, :], run_grad[None], 0.0), axis=2)
    row_grad = jnp.broadcast_to(dev_grad[:, :, None], (seq_count, MB, PICK)).reshape(-1)

    head_back = 0.0
    logit_grads = []
    for part in range(group_count):
        logit_grad = (
            row_grad[:, None]
            * (target_hits[part].astype(F32) - jnp.exp(logits[part] - log_total[:, None]))
        ).astype(BF)
        logit_grads.append(logit_grad)
        head_back = head_back + contract(logit_grad, slab_t[part], 1, 1)
    head_back = head_back.astype(BF)
    moved = [(i, (i + 1) % group_count) for i in range(group_count)]
    if group_count == 2:
        head_back, head_part = lax.optimization_barrier(
            (head_back, contract(head_rows, logit_grads[1], 0, 0).astype(BF))
        )
        head_other = lax.ppermute(head_part, "dp", moved)
    (row_back,) = fold(
        [head_back.reshape(seq_count, MB * PICK, width)],
        [(MB * PICK, width)],
        row_pieces(line, MB * PICK, width, 1),
        6,
    )
    row_back = row_back.astype(BF).reshape(MB, PICK, width)
    cont_back = jnp.einsum("mpr,mpd->mrd", pick_low, row_back, preferred_element_type=F32)
    upstream = jnp.concatenate(
        [jnp.zeros((MB, 1, rows_dev, width), F32), cont_back[:, None]], axis=1
    ).reshape(own_rows, width)

    grad_two, gain_final, bias_final = norm_backward(upstream, unit_final, inverse_final, gains[2])
    grad_ffn = grad_two.astype(BF)
    columns = weights.shape[0]
    weight_grad = place_product(None, activated, grad_ffn, 4 * width + FF, columns)
    grad_act = contract(w_dn, grad_ffn, 1, 1)
    _, gelu_pull = jax.vjp(lambda pre_act: jax.nn.gelu(pre_act, approximate=False), up_proj)
    grad_up = gelu_pull(grad_act)[0].astype(BF)
    weight_grad = place_product(weight_grad, grad_up, hidden_two, 4 * width, columns)
    grad_hidden = contract(grad_up, w_up, 0, 0)
    grad_mid, gain_two, bias_two = norm_backward(grad_hidden, unit_two, inverse_two, gains[1])
    grad_one = grad_two + grad_mid
    grad_branch = grad_one.astype(BF)
    weight_grad = place_product(weight_grad, attended, grad_branch, 3 * width, columns)
    grad_attended = contract(w_o, grad_branch, 1, 1).astype(BF)
    grad_query, grad_pairs = attend_back(query_pos, queries, pairs, grad_attended)
    if group_count == 2:
        grad_query, head_other = lax.optimization_barrier((grad_query, head_other))
    grad_pairs = grad_pairs.reshape(2 * width, MB * key_rows)
    weight_grad = place_product(weight_grad, grad_query, hidden_one, 0, columns)
    weight_grad = place_product(weight_grad, grad_pairs, hidden_sel, width, columns)
    low_sel = turned_product(grad_pairs, weights, 2 * 2 * rows_dev).reshape(MB, key_rows, width)
    weight_sum = lax.psum_scatter(
        weight_grad.reshape(all_count, -1, width), ("dp", "seq"), scatter_dimension=0, tiled=True
    )[0].astype(F32)
    (low_own,) = fold(
        [low_sel],
        [(MB, 2, rows_dev, width)],
        visible_sum(line, run_devs, rows_dev, half, width),
        7,
    )
    grad_low = low_own.reshape(own_rows, width) + contract(grad_query, w_q, 0, 0)
    grad_first, gain_one, bias_one = norm_backward(grad_low, unit_one, inverse_one, gains[0])
    norm_rows = jnp.stack([gain_one, gain_two, gain_final, bias_one, bias_two, bias_final])
    if group_count == 2:
        head_own = contract(head_rows, logit_grads[0], 0, 0)
        pad_rows = 8
        own_grads, other_grads = exchange(
            jnp.concatenate(
                [grad_one + grad_first, norm_rows, jnp.zeros((pad_rows - 6, width), F32)]
            ).astype(BF),
            8,
        )
        other_slots = lax.ppermute(row_slots, "dp", moved)
        embed_sum = lax.optimization_barrier(head_own + head_other.astype(F32))
        norm_all = 0.0
        for grads, part_slots in ((own_grads, row_slots), (other_grads, other_slots)):
            part_slots = jnp.pad(
                part_slots.reshape(seq_count, own_rows), ((0, 0), (0, pad_rows)), constant_values=-1
            ).reshape(-1)
            embed_sum = embed_sum + contract(
                grads.reshape(-1, width), hits(part_slots, 0).astype(BF), 0, 0
            )
            norm_all = norm_all + jnp.sum(
                grads[:, own_rows : own_rows + 6].astype(F32), axis=0
            )
    else:
        row_grads, norm_grads = spread(
            [
                (grad_one + grad_first).astype(BF),
                jnp.concatenate([norm_rows, jnp.zeros((10, width), F32)]).astype(BF),
            ],
            [
                jax.ShapeDtypeStruct((seq_count, own_rows, width), BF),
                jax.ShapeDtypeStruct((seq_count, 16, width), BF),
            ],
            row_gather(line, own_rows, 2)
            + ((line, lambda x: x[1], lambda o, q: o[1].at[q]),),
            8,
        )
        row_grads = row_grads.reshape(-1, width)
        norm_sum = jnp.sum(norm_grads[:, :6].astype(F32), axis=0)
        norm_all = norm_sum
        for step in range(1, group_count):
            norm_all = norm_all + lax.ppermute(
                norm_sum, "dp", [(i, (i + step) % group_count) for i in range(group_count)]
            )

        def table_grad(step):
            return contract(head_rows, logit_grads[step], 0, 0) + contract(
                row_grads, hits(row_slots, step).astype(BF), 0, 0
            )

        arrived = [
            lax.ppermute(
                table_grad(step).astype(BF),
                "dp",
                [(i, (i + step) % group_count) for i in range(group_count)],
            )
            for step in range(1, group_count)
        ]
        embed_sum = table_grad(0)
        for block in arrived:
            embed_sum = embed_sum + block.astype(F32)
    norm_own = lax.dynamic_slice_in_dim(norm_all.reshape(-1), device_rank * norm_dev, norm_dev, 0)
    squares = (
        jnp.sum(embed_sum * embed_sum)
        + jnp.sum(weight_sum * weight_sum)
        + jnp.sum(norm_own * norm_own)
    )
    lanes = lax.broadcasted_iota(jnp.int32, (8, 128), 1)
    scalars = direct_gather(
        jnp.where(lanes == 0, squares, jnp.where(lanes == 1, loss, 0.0)), True, 9
    )
    square_total = jnp.sum(scalars[:, 0, 0])
    loss_total = jnp.sum(scalars[::seq_count, 0, 1])
    grad_norm = jnp.sqrt(square_total)
    factor = jnp.minimum(1.0, CLIP_NORM / grad_norm)
    embed_out = adamw(
        table_t, embed_first.T, embed_second.T, embed_sum * factor, LEARN_RATE, WEIGHT_DECAY
    )
    layer_out = adamw(
        layer_weights.T,
        layer_first.T,
        layer_second.T,
        weight_sum * factor,
        LEARN_RATE,
        WEIGHT_DECAY,
    )
    norm_out = adamw(norm_params, norm_first, norm_second, norm_own * factor, NORM_RATE, 0.0)
    return (
        embed_out[0].T,
        embed_out[1].T,
        embed_out[2].T,
        embed_out[3].T,
        layer_out[0].T,
        layer_out[1].T,
        layer_out[2].T,
        layer_out[3].T,
        norm_out[0],
        norm_out[1],
        norm_out[2],
        norm_out[3],
        grad_norm,
        loss_total,
    )


def solution(mesh):
    return jax.shard_map(
        on_device,
        mesh=mesh,
        in_specs=(
            P(None, "dp", None, "seq"),
            P(None, "dp", "seq"),
            P(None, "dp", "seq"),
            P(),
            P(),
            P(),
            P(),
            P(("dp", "seq"), None),
            P(("dp", "seq"), None),
            P(("dp", "seq"), None),
            P(None, ("dp", "seq")),
            P(None, ("dp", "seq")),
            P(None, ("dp", "seq")),
            P(("dp", "seq")),
            P(("dp", "seq")),
            P(("dp", "seq")),
        ),
        out_specs=(
            P(("dp", "seq"), None),
            P(("dp", "seq"), None),
            P(("dp", "seq"), None),
            P(("dp", "seq"), None),
            P(None, ("dp", "seq")),
            P(None, ("dp", "seq")),
            P(None, ("dp", "seq")),
            P(None, ("dp", "seq")),
            P(("dp", "seq")),
            P(("dp", "seq")),
            P(("dp", "seq")),
            P(("dp", "seq")),
            P(),
            P(),
        ),
        check_vma=False,
    )
```

```python
import functools

import jax
import jax.numpy as jnp
from jax import lax
from jax.experimental import pallas as pl
from jax.experimental.pallas import tpu as pltpu
from jax.sharding import PartitionSpec as P


HEADS = 17
HD = 64
FF = 4352
PICK = 32
CLEN = 512
MB = 2
STEP = 10


EPS_NORM = 1e-05
DPO_BETA = 0.05
CLIP_NORM = 1.0
LEARN_RATE = 0.03
NORM_RATE = 0.4
WEIGHT_DECAY = 0.1
MOMENT_ONE = 0.9
MOMENT_TWO = 0.999
EPS_ADAM = 1e-08
MASKED = -1e30
BF = jnp.bfloat16
F32 = jnp.float32
MESH = pl.DeviceIdType.MESH
VMEM = pltpu.VMEM


def meet(peers):
    barrier = pltpu.get_barrier_semaphore()
    for there, peer in peers:

        @pl.when(there)
        def _():
            pl.semaphore_signal(barrier, inc=1, device_id=peer, device_id_type=MESH)

    pl.semaphore_wait(barrier, sum(jnp.where(there, 1, 0) for there, _ in peers))


def direct_kernel(whole, x_ref, o_ref, send_sem, recv_sem):
    seq_count = lax.axis_size("seq")
    group_rank = lax.axis_index("dp")
    me = lax.axis_index("seq")
    count = o_ref.shape[0]
    if whole:
        me = group_rank * seq_count + me

    def peer(step):
        other = lax.rem(me + step, count)
        if whole:
            return (other // seq_count, lax.rem(other, seq_count))
        return (group_rank, other)

    barrier = pltpu.get_barrier_semaphore()

    def greet(step, carry):
        pl.semaphore_signal(barrier, inc=1, device_id=peer(step), device_id_type=MESH)
        return carry

    lax.fori_loop(1, count, greet, 0)
    o_ref[me] = x_ref[...]
    pl.semaphore_wait(barrier, count - 1)

    def copy(step):
        return pltpu.make_async_remote_copy(
            src_ref=x_ref,
            dst_ref=o_ref.at[me],
            send_sem=send_sem.at[step],
            recv_sem=recv_sem.at[step],
            device_id=peer(step),
            device_id_type=MESH,
        )

    def begin(step, carry):
        copy(step).start()
        return carry

    def finish(step, carry):
        copy(step).wait()
        return carry

    lax.fori_loop(1, count, begin, 0)
    lax.fori_loop(1, count, finish, 0)


def direct_gather(x, whole, collective_id):
    count = lax.axis_size("seq") * (lax.axis_size("dp") if whole else 1)
    return pl.pallas_call(
        functools.partial(direct_kernel, whole),
        out_shape=jax.ShapeDtypeStruct((count,) + x.shape, x.dtype),
        in_specs=[pl.BlockSpec(memory_space=VMEM)],
        out_specs=pl.BlockSpec(memory_space=VMEM),
        scratch_shapes=[pltpu.SemaphoreType.DMA((count,)), pltpu.SemaphoreType.DMA((count,))],
        compiler_params=pltpu.CompilerParams(collective_id=collective_id, has_side_effects=True),
    )(x)


def place(rank):
    return (rank // 4, lax.rem(rank, 4) // 2, lax.rem(rank, 2))


def line_peers(at, side, core, group, line):
    return [
        (at > 0, (group, 4 * (at - 1) + 2 * side + core)),
        (at < line - 1, (group, 4 * (at + 1) + 2 * side + core)),
        (at >= 0, (group, 4 * at + 2 * (1 - side) + core)),
        (at >= 0, (group, 4 * at + 2 * side + 1 - core)),
    ]


def spread_kernel(parts, count, *refs):
    given, wanted, pieces = parts
    total = len(pieces)
    x_refs, o_refs = refs[:given], refs[given : given + wanted]
    local_sem, z_send, z_recv, b_send, b_recv, c_send, c_recv = refs[given + wanted :]
    spans = [piece[0] for piece in pieces]
    ins = [piece[1](x_refs) for piece in pieces]
    line = count // 4
    group = lax.axis_index("dp")
    at, side, core = place(lax.axis_index("seq"))
    peers = line_peers(at, side, core, group, line)
    below, above, beside, sibling = (peer for _, peer in peers)
    meet(peers)

    def seq_of(where, which_side, which_core):
        return 4 * where + 2 * which_side + which_core

    def remote(src, dst, send, recv, peer):
        return pltpu.make_async_remote_copy(
            src_ref=src, dst_ref=dst, send_sem=send, recv_sem=recv, device_id=peer, device_id_type=MESH
        )

    def low_high(span):
        low = at // span * span
        return low, low + span

    def view(part, where, which_side, which_core):
        return pieces[part][2](o_refs, seq_of(where, which_side, which_core))

    def where_of(item):
        far = (item + 1) // 2
        return at - far if item % 2 else at + far

    def valid(part, item):
        low, high = low_high(spans[part])
        where = where_of(item)
        return (where >= low) & (where < high)

    def z_copy(part, item, up):
        where = where_of(item)
        far = (item + 1) // 2 + 1
        mark = 2 * far - 1 if up else 2 * far
        src = ins[part] if item == 0 else view(part, where, side, core)
        return remote(
            src,
            view(part, where, side, core),
            z_send.at[part, mark],
            z_recv.at[part, mark],
            above if up else below,
        )

    def b_copy(part, item):
        where = where_of(item)
        src = ins[part] if item == 0 else view(part, where, side, core)
        return remote(
            src, view(part, where, side, core), b_send.at[part, item], b_recv.at[part, item], beside
        )

    def b_arrived(part, item):
        where = where_of(item)
        spot = view(part, where, 1 - side, core)
        return remote(spot, spot, b_send.at[part, item], b_recv.at[part, item], beside)

    def z_arrived(part, item):
        spot = view(part, where_of(item), side, core)
        return remote(spot, spot, z_send.at[part, item], z_recv.at[part, item], beside)

    def c_copy(part, item, from_side):
        where = where_of(item)
        mine = item == 0 and not from_side
        which = 1 - side if from_side else side
        src = ins[part] if mine else view(part, where, which, core)
        index = 2 * item + from_side
        return remote(
            src, view(part, where, which, core), c_send.at[part, index], c_recv.at[part, index], sibling
        )

    def c_arrived(part, item, from_side):
        which = 1 - side if from_side else side
        spot = view(part, where_of(item), which, 1 - core)
        index = 2 * item + from_side
        return remote(spot, spot, c_send.at[part, index], c_recv.at[part, index], sibling)

    items = 2 * line - 1

    def goes_up(part):
        _, high = low_high(spans[part])
        return at + 1 < high

    def goes_down(part):
        low, _ = low_high(spans[part])
        return at - 1 >= low

    def active(part, item):
        return (item + 1) // 2 < spans[part]

    for part in range(total):
        pltpu.make_async_copy(
            ins[part], view(part, at, side, core), local_sem.at[part]
        ).start()

    def launch(part, item):
        @pl.when(valid(part, item))
        def _():
            if item == 0 or item % 2 == 1:
                if (item + 1) // 2 + 1 < spans[part]:
                    @pl.when(goes_up(part))
                    def _():
                        z_copy(part, item, True).start()
            if item == 0 or item % 2 == 0:
                if (item + 1) // 2 + 1 < spans[part]:
                    @pl.when(goes_down(part))
                    def _():
                        z_copy(part, item, False).start()
            b_copy(part, item).start()
            c_copy(part, item, 0).start()

    def relay(part, item):
        @pl.when(valid(part, item))
        def _():
            b_arrived(part, item).wait_recv()
            c_copy(part, item, 1).start()

    for part in range(total):
        launch(part, 0)
    for far in range(1, line + 1):
        for item in (2 * far - 1, 2 * far):
            for part in range(total):
                if far < line and active(part, item):
                    @pl.when(valid(part, item))
                    def _():
                        z_arrived(part, item).wait_recv()

                    launch(part, item)
        last = [0] if far == 1 else [2 * far - 3, 2 * far - 2]
        for item in last:
            for part in range(total):
                if active(part, item):
                    relay(part, item)
    for part in range(total):
        pltpu.make_async_copy(ins[part], view(part, at, side, core), local_sem.at[part]).wait()
        for item in range(items):
            if not active(part, item):
                continue

            @pl.when(valid(part, item))
            def _():
                if (item == 0 or item % 2 == 1) and (item + 1) // 2 + 1 < spans[part]:
                    @pl.when(goes_up(part))
                    def _():
                        z_copy(part, item, True).wait_send()
                if (item == 0 or item % 2 == 0) and (item + 1) // 2 + 1 < spans[part]:
                    @pl.when(goes_down(part))
                    def _():
                        z_copy(part, item, False).wait_send()
                b_copy(part, item).wait_send()
                c_copy(part, item, 0).wait_send()
                c_copy(part, item, 1).wait_send()
                c_arrived(part, item, 0).wait_recv()
                c_arrived(part, item, 1).wait_recv()


def spread(blocks, out_shapes, pieces, collective_id):
    count = lax.axis_size("seq")
    total = len(pieces)
    items = 2 * (count // 4) + 1
    sem = pltpu.SemaphoreType.DMA
    return pl.pallas_call(
        functools.partial(spread_kernel, (len(blocks), len(out_shapes), pieces), count),
        out_shape=out_shapes,
        in_specs=[pl.BlockSpec(memory_space=VMEM)] * len(blocks),
        out_specs=[pl.BlockSpec(memory_space=pl.ANY)] * len(out_shapes),
        scratch_shapes=[sem((total,))] + [sem((total, items))] * 4 + [sem((total, 2 * items))] * 2,
        compiler_params=pltpu.CompilerParams(collective_id=collective_id, has_side_effects=True),
    )(*blocks)


def fold_kernel(parts, count, *refs):
    given, wanted, pieces = parts
    total = len(pieces)
    spans = [piece[0] for piece in pieces]
    x_refs, o_refs = refs[:given], refs[given : given + wanted]
    scratch = refs[given + wanted :]
    outs = [piece[3](o_refs) for piece in pieces]
    c_bufs, s_bufs, b_bufs, u_bufs, d_bufs, t_bufs = (
        scratch[i * total : (i + 1) * total] for i in range(6)
    )
    c_send, c_recv, b_send, b_recv, u_send, u_recv, d_send, d_recv = scratch[6 * total :]
    line = count // 4
    group = lax.axis_index("dp")
    at, side, core = place(lax.axis_index("seq"))
    peers = line_peers(at, side, core, group, line)
    below, above, beside, sibling = (peer for _, peer in peers)
    meet(peers)

    def remote(src, dst, send, recv, peer):
        return pltpu.make_async_remote_copy(
            src_ref=src, dst_ref=dst, send_sem=send, recv_sem=recv, device_id=peer, device_id_type=MESH
        )

    def view(part, where, which_side, which_core):
        return pieces[part][2](x_refs, 4 * where + 2 * which_side + which_core)

    def valid(part, where):
        low = at // spans[part] * spans[part]
        return (where >= low) & (where < low + spans[part])

    def slot(part, where):
        return lax.rem(where, spans[part])

    order = []
    for far in range(line - 1, 0, -1):
        order += [(far, 1), (far, -1)]
    order.append((0, 1))

    def c_copy(part, where, other):
        which = 1 - side if other else side
        index = 2 * slot(part, where) + other
        return remote(
            view(part, where, which, 1 - core),
            c_bufs[part].at[index],
            c_send.at[part, index],
            c_recv.at[part, index],
            sibling,
        )

    def b_copy(part, where):
        index = slot(part, where)
        return remote(
            s_bufs[part].at[index], b_bufs[part].at[index], b_send.at[part, index], b_recv.at[part, index], beside
        )

    def u_copy(part, where):
        index = slot(part, where)
        return remote(
            t_bufs[part].at[index], u_bufs[part].at[index], u_send.at[part, index], u_recv.at[part, index], above
        )

    def d_copy(part, where):
        index = slot(part, where)
        return remote(
            t_bufs[part].at[index], d_bufs[part].at[index], d_send.at[part, index], d_recv.at[part, index], below
        )

    def each(action):
        for far, sign in order:
            for part in range(total):
                if far >= spans[part]:
                    continue
                where = at + sign * far

                @pl.when(valid(part, where))
                def _():
                    action(part, where, far, sign)

    each(lambda part, where, far, sign: c_copy(part, where, 1).start())
    each(lambda part, where, far, sign: c_copy(part, where, 0).start())

    def aside(part, where, far, sign):
        c_copy(part, where, 1).wait_recv()
        index = slot(part, where)
        mine = view(part, where, 1 - side, core)[...]
        s_bufs[part][index] = (
            mine.astype(F32) + c_bufs[part][2 * index + 1].astype(F32)
        ).astype(BF)
        b_copy(part, where).start()

    each(aside)

    def along(part, where, far, sign):
        c_copy(part, where, 0).wait_recv()
        b_copy(part, where).wait_recv()
        index = slot(part, where)
        here = slot(part, at)
        value = (
            view(part, where, side, core)[...].astype(F32)
            + c_bufs[part][2 * index].astype(F32)
            + b_bufs[part][index].astype(F32)
        )
        if far == 0:
            outs[part][...] = value

            @pl.when(here > 0)
            def _():
                u_copy(part, where).wait_recv()
                outs[part][...] += u_bufs[part][index].astype(F32)

            @pl.when(here < spans[part] - 1)
            def _():
                d_copy(part, where).wait_recv()
                outs[part][...] += d_bufs[part][index].astype(F32)
        elif sign > 0:
            t_bufs[part][index] = value.astype(BF)

            @pl.when(here > 0)
            def _():
                u_copy(part, where).wait_recv()
                t_bufs[part][index] = (value + u_bufs[part][index].astype(F32)).astype(BF)

            u_copy(part, where).start()
        else:
            t_bufs[part][index] = value.astype(BF)

            @pl.when(here < spans[part] - 1)
            def _():
                d_copy(part, where).wait_recv()
                t_bufs[part][index] = (value + d_bufs[part][index].astype(F32)).astype(BF)

            d_copy(part, where).start()

    each(along)

    def finish(part, where, far, sign):
        c_copy(part, where, 0).wait_send()
        c_copy(part, where, 1).wait_send()
        b_copy(part, where).wait_send()
        if far > 0:
            (u_copy if sign > 0 else d_copy)(part, where).wait_send()

    each(finish)


def fold(arrays, out_shapes, pieces, collective_id):
    count = lax.axis_size("seq")
    total = len(pieces)
    sem = pltpu.SemaphoreType.DMA
    line = count // 4
    bufs = []
    for times in (2, 1, 1, 1, 1, 1):
        bufs += [VMEM((times * piece[0],) + piece[1], BF) for piece in pieces]
    return pl.pallas_call(
        functools.partial(fold_kernel, (len(arrays), len(out_shapes), pieces), count),
        out_shape=[jax.ShapeDtypeStruct(shape, F32) for shape in out_shapes],
        in_specs=[pl.BlockSpec(memory_space=VMEM)] * len(arrays),
        out_specs=[pl.BlockSpec(memory_space=VMEM)] * len(out_shapes),
        scratch_shapes=bufs + [sem((total, 2 * line))] * 2 + [sem((total, line))] * 6,
        compiler_params=pltpu.CompilerParams(
            collective_id=collective_id, has_side_effects=True, vmem_limit_bytes=60 * 2**20
        ),
    )(*arrays)


def exchange_kernel(x_ref, own_ref, other_ref, own_sem, z_send, z_recv, x_send, x_recv, y_send, y_recv, c_send, c_recv):
    count = own_ref.shape[0]
    line = count // 4
    group = lax.axis_index("dp")
    me = lax.axis_index("seq")
    at, side, core = place(me)
    peers = line_peers(at, side, core, group, line)
    below, above, beside, sibling = (peer for _, peer in peers)
    across = (1 - group, me)
    meet(peers + [(at >= 0, across)])

    def remote(src, dst, send, recv, index, peer):
        return pltpu.make_async_remote_copy(
            src_ref=src, dst_ref=dst, send_sem=send.at[index], recv_sem=recv.at[index],
            device_id=peer, device_id_type=MESH,
        )

    items = [(0, 0)] + [(far, turn) for far in range(1, line) for turn in range(2)]

    def where_of(item):
        return at + item[0] * (2 * item[1] - 1)

    def number(item):
        return 2 * item[0] + item[1]

    def given(item, action):
        @pl.when((where_of(item) >= 0) & (where_of(item) < line))
        def _():
            action()

    def spot(item, other_group, other_side, other_core):
        ref = other_ref if other_group else own_ref
        s = 1 - side if other_side else side
        c = 1 - core if other_core else core
        return ref.at[4 * where_of(item) + 2 * s + c]

    def here(item, other_group, other_side):
        if item == (0, 0) and not other_group and not other_side:
            return x_ref
        return spot(item, other_group, other_side, False)

    def z_copy(item, turn, peer):
        far = (item[0] + 1, turn)
        return remote(here(item, 0, 0), spot(item, 0, 0, 0), z_send, z_recv, number(far), peer)

    def side_copy(item, other_group, arrived):
        dst = spot(item, other_group, arrived, 0)
        src = dst if arrived else here(item, other_group, 0)
        return remote(src, dst, x_send, x_recv, 2 * number(item) + other_group, beside)

    def cross_copy(item, other_side, arrived):
        dst = spot(item, 1, other_side, 0)
        src = dst if arrived else here(item, 0, other_side)
        return remote(src, dst, y_send, y_recv, 2 * number(item) + other_side, across)

    def core_copy(item, other_group, other_side, arrived):
        dst = spot(item, other_group, other_side, arrived)
        src = dst if arrived else here(item, other_group, other_side)
        index = 4 * number(item) + 2 * other_group + other_side
        return remote(src, dst, c_send, c_recv, index, sibling)

    def z_links(item, act):
        far, turn = item
        if far + 1 < line:
            if far == 0 or turn == 0:

                @pl.when(at + 1 < line)
                def _():
                    act(z_copy(item, 0, above))

            if far == 0 or turn == 1:

                @pl.when(at > 0)
                def _():
                    act(z_copy(item, 1, below))

    def start(copy):
        copy.start()

    def launch(item):
        z_links(item, start)
        side_copy(item, 0, False).start()
        cross_copy(item, 0, False).start()
        core_copy(item, 0, 0, False).start()

    def first(item):
        z = remote(spot(item, 0, 0, 0), spot(item, 0, 0, 0), z_send, z_recv, number(item), beside)
        z.wait_recv()
        launch(item)

    def second(item):
        side_copy(item, 0, True).wait_recv()
        core_copy(item, 0, 1, False).start()
        cross_copy(item, 0, True).wait_recv()
        core_copy(item, 1, 0, False).start()

    def diagonal(item):
        cross_copy(item, 1, False).start()

    def third(item):
        cross_copy(item, 1, True).wait_recv()
        core_copy(item, 1, 1, False).start()

    def at_far(far):
        return [item for item in items if item[0] == far]

    own = pltpu.make_async_copy(x_ref, spot((0, 0), 0, 0, 0), own_sem.at[0])
    own.start()
    launch((0, 0))
    for step in range(1, line + 1):
        for item in at_far(step):
            given(item, functools.partial(first, item))
        for item in at_far(step - 1):
            given(item, functools.partial(second, item))
        if step >= line - 1:
            for far in range(line - 1) if step == line - 1 else [line - 1]:
                for item in at_far(far):
                    given(item, functools.partial(diagonal, item))
    for item in items:
        given(item, functools.partial(third, item))
    own.wait()

    def finish(item):
        z_links(item, lambda copy: copy.wait_send())
        side_copy(item, 0, False).wait_send()
        cross_copy(item, 0, False).wait_send()

        cross_copy(item, 1, False).wait_send()
        for other_group in range(2):
            for other_side in range(2):
                core_copy(item, other_group, other_side, False).wait_send()
                core_copy(item, other_group, other_side, True).wait_recv()

    for item in items:
        given(item, functools.partial(finish, item))


def exchange(x, collective_id):
    count = lax.axis_size("seq")
    marks = 2 * (count // 4) + 2
    sem = pltpu.SemaphoreType.DMA
    return pl.pallas_call(
        exchange_kernel,
        out_shape=[jax.ShapeDtypeStruct((count,) + x.shape, x.dtype)] * 2,
        in_specs=[pl.BlockSpec(memory_space=VMEM)],
        out_specs=[pl.BlockSpec(memory_space=pl.ANY)] * 2,
        scratch_shapes=[sem((1,))] + [sem((marks,))] * 2 + [sem((2 * marks,))] * 4 + [sem((4 * marks,))] * 2,
        compiler_params=pltpu.CompilerParams(collective_id=collective_id, has_side_effects=True),
    )(x)


def row_gather(line, rows, cuts):
    size = rows // cuts
    return tuple(
        (
            line,
            lambda x, h=h: x[0].at[pl.ds(h * size, size)],
            lambda o, q, h=h: o[0].at[q, pl.ds(h * size, size)],
        )
        for h in range(cuts)
    )


def row_pieces(line, rows, width, cuts):
    size = rows // cuts
    return tuple(
        (
            line,
            (size, width),
            lambda x, q, h=h: x[0].at[q, pl.ds(h * size, size)],
            lambda o, h=h: o[0].at[pl.ds(h * size, size)],
        )
        for h in range(cuts)
    )


def turned_kernel(l_ref, k_ref, v_ref, o_ref):
    width = k_ref.shape[0]
    o_ref[...] = (
        contract(l_ref[:width], k_ref[...], 0, 0) + contract(l_ref[width:], v_ref[...], 0, 0)
    ).astype(BF)


def turned_product(left, weights, block):
    depth, rows = left.shape
    width = weights.shape[1]
    return pl.pallas_call(
        turned_kernel,
        grid=(rows // block,),
        out_shape=jax.ShapeDtypeStruct((rows, width), BF),
        in_specs=[
            pl.BlockSpec((depth, block), lambda i: (0, i)),
            pl.BlockSpec((width, width), lambda i: (1, 0)),
            pl.BlockSpec((width, width), lambda i: (2, 0)),
        ],
        out_specs=pl.BlockSpec((block, width), lambda i: (i, 0)),
    )(left, weights, weights)


def visible_rows(kind, run_devs, rows_dev, half, q):
    first = half + rows_dev * lax.rem(q, run_devs) if kind else rows_dev * q
    return pl.multiple_of(first, 32)


def visible_gather(line, run_devs, rows_dev, half):
    size = rows_dev // 2
    return tuple(
        (
            run_devs // 4 if kind else line,
            lambda x, m=m, kind=kind, j=j: x[0].at[m, kind, pl.ds(size * j, size)],
            lambda o, q, m=m, kind=kind, j=j: o[0].at[
                m, pl.ds(visible_rows(kind, run_devs, rows_dev, half, q) + size * j, size)
            ],
        )
        for kind in range(2)
        for m in range(MB)
        for j in range(2)
    )


def visible_sum(line, run_devs, rows_dev, half, width):
    return tuple(
        (
            run_devs // 4 if kind else line,
            (MB, rows_dev, width),
            lambda x, q, kind=kind: x[0].at[
                :, pl.ds(visible_rows(kind, run_devs, rows_dev, half, q), rows_dev)
            ],
            lambda o, kind=kind: o[0].at[:, kind],
        )
        for kind in range(2)
    )


def place_kernel(l_ref, r_ref, *refs):
    refs[-1][...] = jnp.dot(l_ref[...], r_ref[...], preferred_element_type=F32).astype(BF)


def place_product(buffer, left, right, first, rows):
    depth, width = right.shape
    block = width // 2
    given = () if buffer is None else (buffer,)
    return pl.pallas_call(
        place_kernel,
        grid=(left.shape[0] // block,),
        out_shape=jax.ShapeDtypeStruct((rows, width), BF),
        in_specs=[
            pl.BlockSpec((block, depth), lambda i: (i, 0)),
            pl.BlockSpec((depth, width), lambda i: (0, 0)),
        ]
        + [pl.BlockSpec(memory_space=pl.ANY)] * len(given),
        out_specs=pl.BlockSpec((block, width), lambda i: (first // block + i, 0)),
        input_output_aliases={2: 0} if given else {},
    )(left, right, *given)


def contract(left, right, left_dim, right_dim):
    return lax.dot_general(
        left, right, (((left_dim,), (right_dim,)), ((), ())), preferred_element_type=F32
    )


def norm_forward(values, gain, bias):
    centred = values - jnp.mean(values, axis=-1, keepdims=True)
    inverse = lax.rsqrt(jnp.mean(centred * centred, axis=-1, keepdims=True) + EPS_NORM)
    unit = centred * inverse
    return (unit * gain + bias, unit, inverse)


def norm_backward(upstream, unit, inverse, gain):
    scaled = upstream * gain
    inner = (
        scaled
        - jnp.mean(scaled, axis=-1, keepdims=True)
        - unit * jnp.mean(scaled * unit, axis=-1, keepdims=True)
    )
    return (inverse * inner, jnp.sum(upstream * unit, axis=0), jnp.sum(upstream, axis=0))


def head_probs(pos_ref, q, k):
    scores = contract(q, k, 0, 0) * HD ** (-0.5)
    key_pos = lax.broadcasted_iota(jnp.int32, scores.shape, 1)
    scores = jnp.where(key_pos <= pos_ref[...], scores, MASKED)
    shifted = jnp.exp(scores - jnp.max(scores, axis=1, keepdims=True))
    return shifted * (1.0 / jnp.sum(shifted, axis=1, keepdims=True))


def attend_kernel(pos_ref, q_ref, kv_ref, o_ref):
    probs = head_probs(pos_ref, q_ref[...], kv_ref[0]).astype(BF)
    o_ref[...] = contract(kv_ref[1], probs, 1, 1).astype(BF)


def attend_back_kernel(pos_ref, q_ref, kv_ref, g_ref, dq_ref, dkv_ref):
    q, k, v, g = q_ref[...], kv_ref[0], kv_ref[1], g_ref[...]
    probs = head_probs(pos_ref, q, k)
    grad = contract(g, v, 0, 0)
    back = (probs * (grad - jnp.sum(probs * grad, axis=1, keepdims=True))).astype(BF)
    scale = HD ** (-0.5)
    dq_ref[...] = (contract(k, back, 1, 1) * scale).astype(BF)
    dkv_ref[0] = (contract(q, back, 1, 0) * scale).astype(BF)
    dkv_ref[1] = contract(g, probs.astype(BF), 1, 0).astype(BF)


def attend(query_pos, q, kv):
    rows, keys = query_pos.shape[0], kv.shape[2] * query_pos.shape[0] // q.shape[1]
    small = pl.BlockSpec((HD, rows), lambda m, h: (h, m))
    large = pl.BlockSpec((2, HD, keys), lambda m, h: (0, h, m))
    return pl.pallas_call(
        attend_kernel,
        grid=(q.shape[1] // rows, HEADS),
        out_shape=jax.ShapeDtypeStruct(q.shape, BF),
        in_specs=[pl.BlockSpec((rows, 1), lambda m, h: (0, 0)), small, large],
        out_specs=small,
    )(query_pos, q, kv)


def attend_back(query_pos, q, kv, grad_out):
    rows, keys = query_pos.shape[0], kv.shape[2] * query_pos.shape[0] // q.shape[1]
    small = pl.BlockSpec((HD, rows), lambda m, h: (h, m))
    large = pl.BlockSpec((2, HD, keys), lambda m, h: (0, h, m))
    return pl.pallas_call(
        attend_back_kernel,
        grid=(q.shape[1] // rows, HEADS),
        out_shape=[jax.ShapeDtypeStruct(q.shape, BF), jax.ShapeDtypeStruct(kv.shape, BF)],
        in_specs=[pl.BlockSpec((rows, 1), lambda m, h: (0, 0)), small, large, small],
        out_specs=[small, large],
    )(query_pos, q, kv, grad_out)


def lookup_kernel(first_ref, slot_ref, table_ref, *refs):
    slots = slot_ref[...] - first_ref[0]
    ids = lax.broadcasted_iota(jnp.int32, (slots.shape[0], table_ref.shape[1]), 1)
    rows = contract(jnp.where(slots == ids, 1.0, 0.0).astype(BF), table_ref[...], 1, 1).astype(BF)
    refs[-1][...] = rows if len(refs) == 1 else refs[0][...] + rows


def lookup(first, slots, table, others, block):
    width, held = table.shape
    rows = pl.BlockSpec((block, width), lambda i: (i, 0))
    given = () if others is None else (others,)
    return pl.pallas_call(
        lookup_kernel,
        grid=(slots.shape[0] // block,),
        out_shape=jax.ShapeDtypeStruct((slots.shape[0], width), BF),
        in_specs=[
            pl.BlockSpec(memory_space=pltpu.SMEM),
            pl.BlockSpec((block, 1), lambda i: (i, 0)),
            pl.BlockSpec((width, held), lambda i: (0, 0)),
        ]
        + [rows] * len(given),
        out_specs=rows,
    )(first, slots, table, *given)


def adamw(weight, moment_a, moment_b, gradient, rate, decay):
    moment_a = MOMENT_ONE * moment_a + (1.0 - MOMENT_ONE) * gradient
    moment_b = MOMENT_TWO * moment_b + (1.0 - MOMENT_TWO) * gradient * gradient
    update = (
        moment_a
        / (1.0 - MOMENT_ONE**STEP)
        / (jnp.sqrt(moment_b / (1.0 - MOMENT_TWO**STEP)) + EPS_ADAM)
    )
    weight = weight - rate * (update + decay * weight)
    return (weight, moment_a, moment_b, weight.astype(BF))


def on_device(
    tokens,
    targets,
    counted,
    cont_label,
    pair_map,
    ref_logp,
    vocab_slot,
    embed_table,
    embed_first,
    embed_second,
    layer_weights,
    layer_first,
    layer_second,
    norm_params,
    norm_first,
    norm_second,
):
    seq_count = lax.axis_size("seq")
    group_count = lax.axis_size("dp")
    all_count = seq_count * group_count
    seq_rank = lax.axis_index("seq")
    group_rank = lax.axis_index("dp")
    device_rank = group_rank * seq_count + seq_rank
    rows_dev = tokens.shape[3]
    half = rows_dev * seq_count
    vocab_dev, width = embed_table.shape
    run_count = half // CLEN
    run_devs = CLEN // rows_dev
    own_rows = MB * 2 * rows_dev

    table_t = embed_table.T
    norm_dev = norm_params.shape[0]
    norm_parts = [norm_params]
    for step in range(1, group_count):
        norm_parts.append(
            lax.ppermute(
                norm_params, "dp", [(i, (i - step) % group_count) for i in range(group_count)]
            )
        )
    sent, *norm_parts = lax.optimization_barrier((table_t.astype(BF), *norm_parts))
    norm_all = jnp.zeros((group_count, norm_dev), F32)
    for step in range(group_count):
        norm_all = lax.dynamic_update_index_in_dim(
            norm_all, norm_parts[step], lax.rem(group_rank + step, group_count), 0
        )
    slab_t = [sent]
    for step in range(1, group_count):
        slab_t.append(
            lax.ppermute(
                slab_t[0], "dp", [(i, (i - step) % group_count) for i in range(group_count)]
            )
        )
    weights = lax.all_gather(
        layer_weights.T.astype(BF)[None], ("dp", "seq"), axis=0, tiled=True
    ).reshape(-1, width)
    w_q = weights[:width]
    w_o = weights[3 * width : 4 * width]
    w_kv = weights[width : 3 * width]
    w_up = weights[4 * width : 4 * width + FF]
    w_dn = weights[4 * width + FF :]

    marks = counted[:, 0]
    spots = jnp.arange(rows_dev, dtype=jnp.int32)
    ranks = (
        jnp.sum(jnp.where(spots[None, :, None] <= spots[None, None, :], marks[:, :, None], 0), axis=1)
        - 1
    )
    pick_ids = jnp.arange(PICK, dtype=jnp.int32)
    pick_hit = (ranks[:, None, :] == pick_ids[None, :, None]) & (marks[:, None, :] == 1)
    pick_targets = jnp.sum(jnp.where(pick_hit, targets[:, 0][:, None, :], 0), axis=2)
    pick_low = pick_hit.astype(BF)
    slots = vocab_slot[jnp.concatenate([tokens[:, 0].reshape(-1), pick_targets.reshape(-1)])]
    small = jnp.concatenate([slots.astype(F32), norm_all.reshape(-1)])
    small = jnp.pad(small, (0, -small.shape[0] % 1024)).reshape(-1, 128)
    small_all = direct_gather(small, False, 1).reshape(seq_count, -1)
    slots_all = small_all[:, : own_rows + MB * PICK].astype(jnp.int32)
    gains = (
        small_all[:, own_rows + MB * PICK :][:, : group_count * norm_dev]
        .reshape(seq_count, group_count, norm_dev)
        .transpose(1, 0, 2)
        .astype(BF)
        .astype(F32)
        .reshape(6, width)
    )
    row_slots = slots_all[:, :own_rows].reshape(-1)
    target_slots = slots_all[:, own_rows:].reshape(-1)
    vocab_ids = jnp.arange(vocab_dev, dtype=jnp.int32)

    def hits(slot_ids, step):
        part = lax.rem(group_rank + step, group_count)
        first = (part * seq_count + seq_rank) * vocab_dev
        return (slot_ids - first)[:, None] == vocab_ids[None, :]

    partial = None
    for step in range(group_count):
        part = lax.rem(group_rank + step, group_count)
        first = (part * seq_count + seq_rank) * vocab_dev
        partial = lookup(first[None], row_slots[:, None], slab_t[step], partial, own_rows)
    line = seq_count // 4
    (stream,) = fold(
        [partial.reshape(seq_count, own_rows, width)],
        [(own_rows, width)],
        row_pieces(line, own_rows, width, 2),
        2,
    )

    normed, unit_one, inverse_one = norm_forward(stream, gains[0], gains[3])
    hidden_one = normed.astype(BF)
    run_dev = seq_rank // run_devs * run_devs
    key_rows = half + CLEN
    (hidden_sel,) = spread(
        [hidden_one.reshape(MB, 2, rows_dev, width)],
        [jax.ShapeDtypeStruct((MB, key_rows, width), BF)],
        visible_gather(line, run_devs, rows_dev, half),
        3,
    )
    hidden_sel = hidden_sel.reshape(MB * key_rows, width)
    pairs = contract(w_kv, hidden_sel, 1, 1).astype(BF).reshape(2, width, MB * key_rows)
    queries = contract(w_q, hidden_one, 1, 1).astype(BF)
    start = seq_rank * rows_dev
    query_pos = jnp.concatenate([start + spots, half + (start - run_dev * rows_dev) + spots])[:, None]
    attended = attend(query_pos, queries, pairs)
    stream_one = stream + contract(attended, w_o, 0, 0)
    normed, unit_two, inverse_two = norm_forward(stream_one, gains[1], gains[4])
    hidden_two = normed.astype(BF)
    up_proj = contract(w_up, hidden_two, 1, 1)
    activated = jax.nn.gelu(up_proj, approximate=False).astype(BF)
    stream_two = stream_one + contract(activated, w_dn, 0, 0)
    normed, unit_final, inverse_final = norm_forward(stream_two, gains[2], gains[5])
    final = normed.astype(BF).reshape(MB, 2, rows_dev, width)[:, 1]
    picked = jnp.einsum("mpr,mrd->mpd", pick_low, final, preferred_element_type=F32).astype(BF)

    (head_rows,) = spread(
        [picked.reshape(MB * PICK, width)],
        [jax.ShapeDtypeStruct((seq_count, MB * PICK, width), BF)],
        row_gather(line, MB * PICK, 1),
        4,
    )
    head_rows = head_rows.reshape(seq_count * MB * PICK, width)
    logits = [contract(head_rows, slab_t[part], 1, 0) for part in range(group_count)]
    target_hits = [hits(target_slots, part) for part in range(group_count)]
    highest = jnp.max(logits[0], axis=1)
    for part in range(1, group_count):
        highest = jnp.maximum(highest, jnp.max(logits[part], axis=1))
    summed = jnp.zeros_like(highest)
    target_logit = jnp.zeros_like(highest)
    for part in range(group_count):
        summed = summed + jnp.sum(jnp.exp(logits[part] - highest[:, None]), axis=1)
        target_logit = target_logit + jnp.sum(jnp.where(target_hits[part], logits[part], 0.0), axis=1)
    stats = direct_gather(
        jnp.stack([highest, summed, target_logit]).reshape(-1, 128), False, 5
    ).reshape(seq_count, 3, -1)
    overall = jnp.max(stats[:, 0], axis=0)
    total = jnp.sum(stats[:, 1] * jnp.exp(stats[:, 0] - overall[None]), axis=0)
    log_total = overall + jnp.log(total)
    token_lp = jnp.sum(stats[:, 2], axis=0) - log_total

    run_ids = jnp.arange(run_count, dtype=jnp.int32)
    run_of_dev = jnp.arange(seq_count, dtype=jnp.int32) * rows_dev // CLEN
    run_match = run_of_dev[:, None] == run_ids[None, :]
    dev_lp = jnp.sum(token_lp.reshape(seq_count, MB, PICK), axis=2)
    run_lp = jnp.sum(jnp.where(run_match[:, None, :], dev_lp[:, :, None], 0.0), axis=0)
    labels = lax.dynamic_index_in_dim(cont_label, group_rank, 1, keepdims=False)
    pairing = lax.dynamic_index_in_dim(pair_map, group_rank, 1, keepdims=False)
    reference_lp = lax.dynamic_index_in_dim(ref_logp, group_rank, 1, keepdims=False)
    label_match = labels[:, :, None] == run_ids[None, None, :]
    label_lp = jnp.sum(jnp.where(label_match, run_lp[:, :, None], 0.0), axis=1)
    margin = label_lp - reference_lp
    chosen = pairing[:, 0::2, None] == run_ids[None, None, :]
    rejected = pairing[:, 1::2, None] == run_ids[None, None, :]
    delta = jnp.sum(jnp.where(chosen, margin[:, None, :], 0.0), axis=2) - jnp.sum(
        jnp.where(rejected, margin[:, None, :], 0.0), axis=2
    )
    loss = jnp.sum(jax.nn.softplus(-DPO_BETA * delta))
    pair_grad = -DPO_BETA * jax.nn.sigmoid(-DPO_BETA * delta)
    label_grad = jnp.sum(
        jnp.where(chosen, pair_grad[:, :, None], 0.0)
        - jnp.where(rejected, pair_grad[:, :, None], 0.0),
        axis=1,
    )
    run_grad = jnp.sum(jnp.where(label_match, label_grad[:, None, :], 0.0), axis=2)
    dev_grad = jnp.sum(jnp.where(run_match[:, None, :], run_grad[None], 0.0), axis=2)
    row_grad = jnp.broadcast_to(dev_grad[:, :, None], (seq_count, MB, PICK)).reshape(-1)

    head_back = 0.0
    logit_grads = []
    for part in range(group_count):
        logit_grad = (
            row_grad[:, None]
            * (target_hits[part].astype(F32) - jnp.exp(logits[part] - log_total[:, None]))
        ).astype(BF)
        logit_grads.append(logit_grad)
        head_back = head_back + contract(logit_grad, slab_t[part], 1, 1)
    head_back = head_back.astype(BF)
    moved = [(i, (i + 1) % group_count) for i in range(group_count)]
    if group_count == 2:
        head_back, head_part = lax.optimization_barrier(
            (head_back, contract(head_rows, logit_grads[1], 0, 0).astype(BF))
        )
        head_other = lax.ppermute(head_part, "dp", moved)
    (row_back,) = fold(
        [head_back.reshape(seq_count, MB * PICK, width)],
        [(MB * PICK, width)],
        row_pieces(line, MB * PICK, width, 1),
        6,
    )
    row_back = row_back.astype(BF).reshape(MB, PICK, width)
    cont_back = jnp.einsum("mpr,mpd->mrd", pick_low, row_back, preferred_element_type=F32)
    upstream = jnp.concatenate(
        [jnp.zeros((MB, 1, rows_dev, width), F32), cont_back[:, None]], axis=1
    ).reshape(own_rows, width)

    grad_two, gain_final, bias_final = norm_backward(upstream, unit_final, inverse_final, gains[2])
    grad_ffn = grad_two.astype(BF)
    columns = weights.shape[0]
    weight_grad = place_product(None, activated, grad_ffn, 4 * width + FF, columns)
    grad_act = contract(w_dn, grad_ffn, 1, 1)
    _, gelu_pull = jax.vjp(lambda pre_act: jax.nn.gelu(pre_act, approximate=False), up_proj)
    grad_up = gelu_pull(grad_act)[0].astype(BF)
    weight_grad = place_product(weight_grad, grad_up, hidden_two, 4 * width, columns)
    grad_hidden = contract(grad_up, w_up, 0, 0)
    grad_mid, gain_two, bias_two = norm_backward(grad_hidden, unit_two, inverse_two, gains[1])
    grad_one = grad_two + grad_mid
    grad_branch = grad_one.astype(BF)
    weight_grad = place_product(weight_grad, attended, grad_branch, 3 * width, columns)
    grad_attended = contract(w_o, grad_branch, 1, 1).astype(BF)
    grad_query, grad_pairs = attend_back(query_pos, queries, pairs, grad_attended)
    if group_count == 2:
        grad_query, head_other = lax.optimization_barrier((grad_query, head_other))
    grad_pairs = grad_pairs.reshape(2 * width, MB * key_rows)
    weight_grad = place_product(weight_grad, grad_query, hidden_one, 0, columns)
    weight_grad = place_product(weight_grad, grad_pairs, hidden_sel, width, columns)
    low_sel = turned_product(grad_pairs, weights, 2 * 2 * rows_dev).reshape(MB, key_rows, width)
    weight_sum = lax.psum_scatter(
        weight_grad.reshape(all_count, -1, width), ("dp", "seq"), scatter_dimension=0, tiled=True
    )[0].astype(F32)
    (low_own,) = fold(
        [low_sel],
        [(MB, 2, rows_dev, width)],
        visible_sum(line, run_devs, rows_dev, half, width),
        7,
    )
    grad_low = low_own.reshape(own_rows, width) + contract(grad_query, w_q, 0, 0)
    grad_first, gain_one, bias_one = norm_backward(grad_low, unit_one, inverse_one, gains[0])
    norm_rows = jnp.stack([gain_one, gain_two, gain_final, bias_one, bias_two, bias_final])
    if group_count == 2:
        head_own = contract(head_rows, logit_grads[0], 0, 0)
        pad_rows = 8
        own_grads, other_grads = exchange(
            jnp.concatenate(
                [grad_one + grad_first, norm_rows, jnp.zeros((pad_rows - 6, width), F32)]
            ).astype(BF),
            8,
        )
        other_slots = lax.ppermute(row_slots, "dp", moved)
        embed_sum = lax.optimization_barrier(head_own + head_other.astype(F32))
        norm_all = 0.0
        for grads, part_slots in ((own_grads, row_slots), (other_grads, other_slots)):
            part_slots = jnp.pad(
                part_slots.reshape(seq_count, own_rows), ((0, 0), (0, pad_rows)), constant_values=-1
            ).reshape(-1)
            embed_sum = embed_sum + contract(
                grads.reshape(-1, width), hits(part_slots, 0).astype(BF), 0, 0
            )
            norm_all = norm_all + jnp.sum(
                grads[:, own_rows : own_rows + 6].astype(F32), axis=0
            )
    else:
        row_grads, norm_grads = spread(
            [
                (grad_one + grad_first).astype(BF),
                jnp.concatenate([norm_rows, jnp.zeros((10, width), F32)]).astype(BF),
            ],
            [
                jax.ShapeDtypeStruct((seq_count, own_rows, width), BF),
                jax.ShapeDtypeStruct((seq_count, 16, width), BF),
            ],
            row_gather(line, own_rows, 2)
            + ((line, lambda x: x[1], lambda o, q: o[1].at[q]),),
            8,
        )
        row_grads = row_grads.reshape(-1, width)
        norm_sum = jnp.sum(norm_grads[:, :6].astype(F32), axis=0)
        norm_all = norm_sum
        for step in range(1, group_count):
            norm_all = norm_all + lax.ppermute(
                norm_sum, "dp", [(i, (i + step) % group_count) for i in range(group_count)]
            )

        def table_grad(step):
            return contract(head_rows, logit_grads[step], 0, 0) + contract(
                row_grads, hits(row_slots, step).astype(BF), 0, 0
            )

        arrived = [
            lax.ppermute(
                table_grad(step).astype(BF),
                "dp",
                [(i, (i + step) % group_count) for i in range(group_count)],
            )
            for step in range(1, group_count)
        ]
        embed_sum = table_grad(0)
        for block in arrived:
            embed_sum = embed_sum + block.astype(F32)
    norm_own = lax.dynamic_slice_in_dim(norm_all.reshape(-1), device_rank * norm_dev, norm_dev, 0)
    squares = (
        jnp.sum(embed_sum * embed_sum)
        + jnp.sum(weight_sum * weight_sum)
        + jnp.sum(norm_own * norm_own)
    )
    lanes = lax.broadcasted_iota(jnp.int32, (8, 128), 1)
    scalars = direct_gather(
        jnp.where(lanes == 0, squares, jnp.where(lanes == 1, loss, 0.0)), True, 9
    )
    square_total = jnp.sum(scalars[:, 0, 0])
    loss_total = jnp.sum(scalars[::seq_count, 0, 1])
    grad_norm = jnp.sqrt(square_total)
    factor = jnp.minimum(1.0, CLIP_NORM / grad_norm)
    embed_out = adamw(
        table_t, embed_first.T, embed_second.T, embed_sum * factor, LEARN_RATE, WEIGHT_DECAY
    )
    layer_out = adamw(
        layer_weights.T,
        layer_first.T,
        layer_second.T,
        weight_sum * factor,
        LEARN_RATE,
        WEIGHT_DECAY,
    )
    norm_out = adamw(norm_params, norm_first, norm_second, norm_own * factor, NORM_RATE, 0.0)
    return (
        embed_out[0].T,
        embed_out[1].T,
        embed_out[2].T,
        embed_out[3].T,
        layer_out[0].T,
        layer_out[1].T,
        layer_out[2].T,
        layer_out[3].T,
        norm_out[0],
        norm_out[1],
        norm_out[2],
        norm_out[3],
        grad_norm,
        loss_total,
    )


def solution(mesh):
    return jax.shard_map(
        on_device,
        mesh=mesh,
        in_specs=(
            P(None, "dp", None, "seq"),
            P(None, "dp", "seq"),
            P(None, "dp", "seq"),
            P(),
            P(),
            P(),
            P(),
            P(("dp", "seq"), None),
            P(("dp", "seq"), None),
            P(("dp", "seq"), None),
            P(None, ("dp", "seq")),
            P(None, ("dp", "seq")),
            P(None, ("dp", "seq")),
            P(("dp", "seq")),
            P(("dp", "seq")),
            P(("dp", "seq")),
        ),
        out_specs=(
            P(("dp", "seq"), None),
            P(("dp", "seq"), None),
            P(("dp", "seq"), None),
            P(("dp", "seq"), None),
            P(None, ("dp", "seq")),
            P(None, ("dp", "seq")),
            P(None, ("dp", "seq")),
            P(None, ("dp", "seq")),
            P(("dp", "seq")),
            P(("dp", "seq")),
            P(("dp", "seq")),
            P(("dp", "seq")),
            P(),
            P(),
        ),
        check_vma=False,
    )
```
